32 devices in a mesh: groups: 1, ctx: 4 (over z), head: 4 (over y, x), rep: 2 (over core).
Axes of the slice: x: 2, y: 2, z: 4, core: 2. Of those that a mesh axis runs over, the one named last changes fastest.
Arguments:
- queries: bfloat16 [2048, 1024], P(('groups', 'ctx', 'head', 'rep')), may hold values from -6 to 6
- key_vectors: bfloat16 [2048, 1024], P(('groups', 'ctx', 'head', 'rep')), may hold values from -10.5 to 10.5
- values: bfloat16 [2048, 2048], P(('groups', 'ctx', 'head', 'rep')), may hold values from -6 to 6
- out_grad: bfloat16 [2048, 2048], P(('groups', 'ctx', 'head', 'rep')), may hold values from -6 to 6
- decay_logit: bfloat16 [2048, 16], P(('groups', 'ctx', 'head', 'rep')), may hold values from -18 to 0.5
- beta_logit: bfloat16 [2048, 16], P(('groups', 'ctx', 'head', 'rep')), may hold values from -3 to -1.5
- doc_lengths: int32 [65], P('groups'), may hold values from 1 to 1024, 2048 in all
Outputs:
- grad_queries: bfloat16 [2048, 1024], P(('groups', 'ctx', 'head', 'rep'))
- grad_keys: bfloat16 [2048, 1024], P(('groups', 'ctx', 'head', 'rep'))
- grad_values: bfloat16 [2048, 2048], P(('groups', 'ctx', 'head', 'rep'))
- grad_decay: float32 [2048, 16], P(('groups', 'ctx', 'head', 'rep'))
- grad_beta: float32 [2048, 16], P(('groups', 'ctx', 'head', 'rep'))
The draws below stay inside these ranges and needn't reach their ends.
Inputs may be any that keep to these rules, and one draw needn't show every extreme that they name: `doc_lengths`: the 65 lengths sum to 2048 and the largest is exactly 1024.
All inputs are finite; a program needn't handle non-finite values.
Results may differ from the reference program's by a relative error of at most 0.001.
Values may be sent and summed in bfloat16 or wider, within the bound.
No kernel may reach another device: no remote copies, remote signals or barrier semaphores. Data moves between devices by JAX's collectives and lax.ppermute only.
A program may use at most 64 MiB of HBM per device.

```python
import math
import jax
import jax.numpy as jnp
import numpy as np
from jax import lax

VALUE_HEADS = 16
HK = 8
DK = 128
DV = 128
BLOCK_LEN = 64
DOCS = 65
PACKED_TOKENS = 2048


def draw_decay_logit(key, part):
    key_matrix = jax.random.split(key, 7)
    fast_share = 0.5
    fast = jax.random.uniform(key_matrix[0], (VALUE_HEADS,), jnp.float32) < fast_share
    fast_rate = jnp.exp(jax.random.uniform(key_matrix[1], (VALUE_HEADS,), jnp.float32, minval=jnp.log(1.0 / 50.0), maxval=jnp.log(1.0 / 30.0)))
    slow_rate = jnp.exp(jax.random.uniform(key_matrix[2], (VALUE_HEADS,), jnp.float32, minval=jnp.log(0.05 / PACKED_TOKENS), maxval=jnp.log(0.5 / PACKED_TOKENS)))
    decay_speed = jnp.where(fast, fast_rate, slow_rate)[None, :]
    blocks = jax.random.uniform(key_matrix[3], (PACKED_TOKENS // 256 + 1, VALUE_HEADS), jnp.float32, minval=jnp.log(0.5), maxval=jnp.log(2.0))
    block_decay_scale = jnp.exp(jnp.repeat(blocks, 256, axis=0)[:PACKED_TOKENS])
    coarse_estimate = jax.random.uniform(key_matrix[4], (PACKED_TOKENS, VALUE_HEADS), jnp.float32, minval=0.5, maxval=1.5)
    sudden_decay_hit = jax.random.uniform(key_matrix[5], (PACKED_TOKENS, VALUE_HEADS), jnp.float32) < 4.0 / PACKED_TOKENS
    sudden_decay_kept = jax.random.uniform(key_matrix[6], (PACKED_TOKENS, VALUE_HEADS), jnp.float32, minval=0.5, maxval=0.8)
    overall_decay_speed = decay_speed * block_decay_scale * coarse_estimate + jnp.where(sudden_decay_hit, -jnp.log(sudden_decay_kept), 0.0)
    return jnp.log(jnp.expm1(overall_decay_speed)).astype(jnp.bfloat16)


def draw_key_vectors(key, part):
    key_matrix = jax.random.split(key, 3)
    common = jnp.clip(jax.random.normal(key_matrix[0], (1, HK, DK), jnp.float32), -3.0, 3.0)
    noise = jnp.clip(jax.random.normal(key_matrix[1], (PACKED_TOKENS, HK, DK), jnp.float32), -3.0, 3.0)
    weight = jax.random.uniform(key_matrix[2], (1, HK, 1), jnp.float32, minval=1.8, maxval=2.5)
    return (weight * common + noise).reshape(PACKED_TOKENS, HK * DK).astype(jnp.bfloat16)


def steps_of(key, extent, pieces, least, high):
    factor_of = 1.0
    for position, blocks in pieces:
        heights = jax.random.uniform(jax.random.fold_in(jax.random.fold_in(key, 6), position), (blocks,), jnp.float32, least / len(pieces), high / len(pieces))
        factor_of = factor_of * jnp.repeat(jnp.exp(heights), extent[position] // blocks).reshape((-1,) + (1,) * (len(extent) - 1 - position))
    return factor_of


def length_profile(amount, total, most, slope):
    loads = [(1 << 20) // math.isqrt(standing ** slope) + 1 for standing in range(2, amount + 1)]
    surplus, holding = total - most - (amount - 1), [1] * (amount - 1)
    while surplus > 0:
        movable = [i for i in range(amount - 1) if holding[i] < most]
        pool, remaining = sum([loads[i] for i in movable]), surplus
        for i in movable:
            addition = min(most - holding[i], max(1, remaining * loads[i] // pool), surplus)
            holding[i] = holding[i] + addition
            surplus = surplus - addition
    return np.array([most] + holding)


def uneven(own_key, amount, total, bound, slope):
    if amount == 2:
        one = jax.random.randint(own_key, (), max(1, total - bound), min(bound, total - 1) + 1)
        return jnp.stack([one, total - one])
    tallies = jnp.asarray(length_profile(amount, total, bound, slope), jnp.int32)
    twos = (amount - 1) // 2
    giver, sink = tallies[1:1 + 2 * twos:2], tallies[2:2 + 2 * twos:2]
    slack = jnp.minimum(giver - 1, bound - sink)
    passed = jax.random.randint(jax.random.fold_in(own_key, 1), (twos,), 0, 1 << 20) % (slack + 1)
    tallies = tallies.at[1:1 + 2 * twos:2].set(giver - passed).at[2:2 + 2 * twos:2].set(sink + passed)
    return tallies[jax.random.permutation(jax.random.fold_in(own_key, 2), amount)]


def scatter_about(rng, dims, scale, reach, shards=(), kind=jnp.bfloat16):
    drawn = scale * jax.random.normal(rng, dims, jnp.float32)
    if shards:
        drawn = drawn * steps_of(rng, dims, shards, -0.22, 0.18)
    return jnp.clip(drawn, -reach, reach).astype(kind)


def setup_inputs(seed: int = 0, part: int = 0) -> dict:
    arg_keys = jax.random.split(jax.random.key(seed), 8)
    part_splits = jax.random.split(jax.random.fold_in(arg_keys[7], part), 8)
    return {
        "queries": scatter_about(part_splits[0], (PACKED_TOKENS, HK * DK), 1.0, 6.0, ((0, 32),)),
        "key_vectors": draw_key_vectors(jax.random.fold_in(jax.random.fold_in(arg_keys[7], part), 71), part),
        "values": scatter_about(part_splits[2], (PACKED_TOKENS, VALUE_HEADS * DV), 1.0, 6.0, ((0, 32),)),
        "out_grad": scatter_about(part_splits[3], (PACKED_TOKENS, VALUE_HEADS * DV), 1.0, 6.0, ((0, 32),)),
        "decay_logit": draw_decay_logit(jax.random.fold_in(jax.random.fold_in(arg_keys[7], part), 71), part),
        "beta_logit": jnp.clip(-3.0 + 1.5 * jax.random.uniform(part_splits[5], (PACKED_TOKENS, VALUE_HEADS), jnp.float32) ** steps_of(part_splits[5], (PACKED_TOKENS, VALUE_HEADS), ((0, 32),), -0.2, 0.2), -3.0, -1.5).astype(jnp.bfloat16),
        "doc_lengths": uneven(part_splits[6], DOCS, PACKED_TOKENS, PACKED_TOKENS // 2, 0).astype(jnp.int32),
    }


HIGHEST_MODE = lax.Precision.HIGHEST

def matmul(left, right):
    return jnp.dot(left.astype(jnp.float32), right.astype(jnp.float32), precision=HIGHEST_MODE, preferred_element_type=jnp.float32)

def block_step(state, inputs):
    query_rows, key_rows, value_rows, gate_rows, beta_rows, start_rows = inputs
    length = query_rows.shape[0]
    row_index = lax.broadcasted_iota(jnp.int32, (length, length), 0)
    column_index = lax.broadcasted_iota(jnp.int32, (length, length), 1)
    gate_sum = jnp.cumsum(gate_rows)
    start_sum = jnp.cumsum(start_rows)
    keep = (column_index <= row_index) & (start_sum[:, None] == start_sum[None, :])
    spread = jnp.where(keep, gate_sum[:, None] - gate_sum[None, :], 0.0)
    decay = jnp.where(keep, jnp.exp(spread), 0.0)
    front = jnp.where(start_sum == 0.0, jnp.exp(gate_sum), 0.0)
    key_gram = matmul(key_rows, key_rows.T)
    lower = jnp.where(column_index < row_index, beta_rows[:, None] * decay * key_gram, 0.0)
    target = beta_rows[:, None] * (value_rows - front[:, None] * matmul(key_rows, state.T))
    fresh = lax.linalg.triangular_solve(lower, target, left_side=True, lower=True, unit_diagonal=True)
    scores = decay * matmul(query_rows, key_rows.T)
    output = front[:, None] * matmul(query_rows, state.T) + matmul(scores, fresh)
    new_state = front[-1] * state + matmul(fresh.T, decay[-1][:, None] * key_rows)
    return (new_state, output)

def span_forward(query_raw, key_raw, value_rows, decay_raw, beta_raw, start_rows, state):
    query_rows = query_raw * lax.rsqrt(lax.optimization_barrier(jnp.sum(query_raw * query_raw, -1, keepdims=True)) + 1e-06) * query_raw.shape[-1] ** (-0.5)
    key_rows = key_raw * lax.rsqrt(lax.optimization_barrier(jnp.sum(key_raw * key_raw, -1, keepdims=True)) + 1e-06)
    gate_rows = -jax.nn.softplus(decay_raw)
    beta_rows = jax.nn.sigmoid(beta_raw)
    count = query_rows.shape[0] // BLOCK_LEN

    def shape_blocks(array):
        return array.reshape((count, BLOCK_LEN) + array.shape[1:])
    inputs = tuple((shape_blocks(item) for item in (query_rows, key_rows, value_rows, gate_rows, beta_rows, start_rows)))
    last, outputs = lax.scan(jax.checkpoint(block_step), state, inputs)
    return (outputs.reshape(query_rows.shape[0], -1), last)

def head_run(query_in, key_in, value_in, decay_in, beta_in, start_rows, state_in):
    mapped = jax.vmap(span_forward, in_axes=(1, 1, 1, 1, 1, None, 0), out_axes=(1, 0))
    return mapped(query_in, key_in, value_in, decay_in, beta_in, start_rows, state_in)

def reference(queries, key_vectors, values, out_grad, decay_logit, beta_logit, doc_lengths):
    total = queries.shape[0]
    query_heads = jnp.repeat(queries.reshape(total, HK, DK).astype(jnp.float32), VALUE_HEADS // HK, axis=1)
    key_heads = jnp.repeat(key_vectors.reshape(total, HK, DK).astype(jnp.float32), VALUE_HEADS // HK, axis=1)
    value_heads = values.reshape(total, VALUE_HEADS, DV).astype(jnp.float32)
    grad_heads = out_grad.reshape(total, VALUE_HEADS, DV).astype(jnp.float32)
    decay_float = decay_logit.astype(jnp.float32)
    beta_float = beta_logit.astype(jnp.float32)
    offsets = (jnp.cumsum(doc_lengths) - doc_lengths).astype(jnp.int32)
    positions = lax.iota(jnp.int32, total)
    start_rows = jnp.any(positions[None, :] == offsets[:, None], axis=0).astype(jnp.float32)
    zero_states = jnp.zeros((VALUE_HEADS, DV, DK), jnp.float32)

    def forward(query_in, key_in, value_in, decay_in, beta_in):
        return head_run(query_in, key_in, value_in, decay_in, beta_in, start_rows, zero_states)[0]
    outputs, pullback = jax.vjp(forward, query_heads, key_heads, value_heads, decay_float, beta_float)
    grad_query, grad_key, grad_value, grad_gate, grad_strength = pullback(grad_heads)
    grad_queries = grad_query.reshape(total, HK, VALUE_HEADS // HK, DK).sum(2).reshape(total, HK * DK).astype(jnp.bfloat16)
    grad_keys = grad_key.reshape(total, HK, VALUE_HEADS // HK, DK).sum(2).reshape(total, HK * DK).astype(jnp.bfloat16)
    grad_values = grad_value.reshape(total, VALUE_HEADS * DV).astype(jnp.bfloat16)
    return (grad_queries, grad_keys, grad_values, grad_gate, grad_strength)
```

```python
import functools

import jax
import jax.numpy as jnp
from jax import lax
from jax.experimental import pallas as pl
from jax.experimental.pallas import tpu as pltpu
from jax.sharding import PartitionSpec as P

VALUE_HEADS = 16
HK = 8
DK = 128
DV = 128
GROUP = VALUE_HEADS // HK
L = 128
EPS = 1e-06
F32 = jnp.float32
BF16 = jnp.bfloat16

NN = ((1,), (0,))
NT = ((1,), (1,))
TN = ((0,), (0,))


def split(x):
    if isinstance(x, tuple):
        return x
    if x.dtype == BF16:
        return (x,)
    high = x.astype(BF16)
    return (high, (x - high.astype(F32)).astype(BF16))


def mm(a, b, dims=NN):
    a, b = split(a), split(b)
    total = None
    for i, left in enumerate(a):
        for j, right in enumerate(b):
            if i + j < 2:
                term = lax.dot_general(left, right, (dims, ((), ())), preferred_element_type=F32)
                total = term if total is None else total + term
    return total


def iotas():
    rows = lax.broadcasted_iota(jnp.int32, (L, L), 0)
    columns = lax.broadcasted_iota(jnp.int32, (L, L), 1)
    return rows, columns


def unit_lower_inverse(lowers):
    rows, columns = iotas()
    eye = (rows == columns).astype(F32)
    powers = [jnp.where(rows // 16 == columns // 16, -a, 0.0) for a in lowers]
    sums = [eye + x for x in powers]
    for _ in range(3):
        halves = [split(x) for x in powers]
        powers = [mm(x, x) for x in halves]
        sums = [s + mm(s, x) for s, x in zip(sums, powers)]
    size = 16
    while size < L:
        mask = (rows // (2 * size) == columns // (2 * size)) & (rows // size != columns // size)
        edges = [jnp.where(mask, a, 0.0) for a in lowers]
        halves = [split(s) for s in sums]
        inner = [mm(e, t) for e, t in zip(edges, halves)]
        sums = [s - mm(t, i) for s, t, i in zip(sums, halves, inner)]
        size *= 2
    return sums


def doc_offsets(doc_ref):
    lengths = doc_ref[...]
    count = lengths.shape[1]
    rows = lax.broadcasted_iota(jnp.int32, (count, count), 0)
    columns = lax.broadcasted_iota(jnp.int32, (count, count), 1)
    column = jnp.sum(
        jnp.where(columns < rows, lengths.astype(F32), 0.0), axis=1, keepdims=True
    )
    row = jnp.sum(jnp.where(columns == rows, column, 0.0), axis=0, keepdims=True)
    return column, row


def block_terms(x_ref, offsets, base, n, heads):
    rows, columns = iotas()
    here = slice(n * L, (n + 1) * L)
    q = x_ref[here, 0:DK]
    k = x_ref[here, DK : 2 * DK]
    logits = x_ref[here, (2 + 2 * heads) * DK : (3 + 2 * heads) * DK].astype(F32)
    lanes = columns
    soft = jnp.maximum(logits, 0.0) + jnp.log1p(jnp.exp(-jnp.abs(logits)))
    sig = 1.0 / (1.0 + jnp.exp(-logits))
    vals = jnp.where(lanes < heads, -soft, sig)
    vals_rows = vals.T
    off_col, off_row = offsets
    first = (base + n * L).astype(F32)
    pos_row = first + lax.broadcasted_iota(jnp.int32, (1, L), 1).astype(F32)
    pos_col = first + lax.broadcasted_iota(jnp.int32, (L, 1), 0).astype(F32)
    doc_row = jnp.sum((off_col <= pos_row).astype(F32), axis=0, keepdims=True)
    doc_col = jnp.sum((off_row <= pos_col).astype(F32), axis=1, keepdims=True)
    before = jnp.sum((off_row <= first - 1.0).astype(F32), axis=1, keepdims=True)
    keep = (columns <= rows) & (doc_col == doc_row)
    gram = mm(k, k, NT)
    cross = mm(q, k, NT)
    square = jnp.where(rows == columns, gram, 0.0)
    rk_row = lax.rsqrt(jnp.sum(square, axis=0, keepdims=True) + EPS)
    rk_col = lax.rsqrt(jnp.sum(square, axis=1, keepdims=True) + EPS)
    qf = q.astype(F32)
    r_col = lax.rsqrt(jnp.sum(qf * qf, axis=1, keepdims=True) + EPS)
    rq_col = r_col * (DK**-0.5)
    kk = jnp.where(columns < rows, gram * rk_col * rk_row, 0.0)
    qk = cross * rq_col * rk_row
    per_head = []
    for h in range(heads):
        gate_row = vals_rows[h : h + 1, :]
        gate_col = vals[:, h : h + 1]
        beta_col = vals[:, heads + h : heads + h + 1]
        sum_col = jnp.sum(jnp.where(columns <= rows, gate_row, 0.0), axis=1, keepdims=True)
        sum_row = jnp.sum(jnp.where(rows <= columns, gate_col, 0.0), axis=0, keepdims=True)
        decay = jnp.where(keep, jnp.exp(jnp.where(keep, sum_col - sum_row, 0.0)), 0.0)
        front = jnp.where(doc_col == before, jnp.exp(sum_col), 0.0)
        last = jnp.where(
            doc_col == doc_col[L - 1 : L, :], jnp.exp(sum_col[L - 1 : L, :] - sum_col), 0.0
        )
        per_head.append(
            dict(
                beta=beta_col,
                decay=decay,
                front=front,
                last=last,
                keep_all=front[L - 1 : L, :],
                sig=sig[:, h : h + 1],
            )
        )
    return dict(
        q=q, k=k, qf=qf, rk_row=rk_row, rk=rk_col, rq=rq_col, r=r_col, kk=kk, qk=qk, heads=per_head
    )


def value_of(x_ref, n, h, heads):
    here = slice(n * L, (n + 1) * L)
    v = x_ref[here, (2 + h) * DK : (3 + h) * DK]
    g = x_ref[here, (2 + heads + h) * DK : (3 + heads + h) * DK]
    return v, g


def first_kernel(
    heads,
    blocks,
    doc_ref,
    x_ref,
    t_ref,
    w_ref,
    u_ref,
    y_ref,
    m_ref,
    c_ref,
    b_ref,
    end_ref,
    begin_ref,
    total_ref,
):
    rows, columns = iotas()
    eye = (rows == columns).astype(F32)
    base = lax.axis_index("ctx") * (blocks * L)
    offsets = doc_offsets(doc_ref)
    terms = [block_terms(x_ref, offsets, base, n, heads) for n in range(blocks)]
    units = [(n, h) for n in range(blocks) for h in range(heads)]
    lowers = [terms[n]["heads"][h]["beta"] * terms[n]["heads"][h]["decay"] * terms[n]["kk"] for n, h in units]
    inverses = unit_lower_inverse(lowers)
    moves, adds, backs = {}, {}, {}
    for (n, h), inverse in zip(units, inverses):
        at = n * heads + h
        block, head = terms[n], terms[n]["heads"][h]
        v, g = value_of(x_ref, n, h, heads)
        k, q, rk, rq = block["k"], block["q"], block["rk"], block["rq"]
        right = jnp.concatenate(
            [(head["beta"] * head["front"] * rk) * k.astype(F32), head["beta"] * v.astype(F32)], axis=1
        )
        both = mm(inverse, right)
        w, u = both[:, :DK], both[:, DK:]
        spread = mm(k, (head["last"] * rk) * both, TN)
        move = head["keep_all"] * eye - spread[:, :DK]
        add = spread[:, DK:]
        y = mm(head["decay"] * block["qk"], g, TN)
        back = mm(q, (head["front"] * rq) * g.astype(F32), TN) - mm(w, y, TN)
        t_ref[at] = inverse
        w_ref[at] = w
        u_ref[at] = u
        y_ref[at] = y
        m_ref[at] = move
        c_ref[at] = add
        b_ref[at] = back
        moves[n, h], adds[n, h], backs[n, h] = move, add, back
    for h in range(heads):
        state, total = adds[0, h], moves[0, h]
        for n in range(1, blocks):
            both = mm(moves[n, h], jnp.concatenate([state, total], axis=1))
            state, total = both[:, :DV] + adds[n, h], both[:, DV:]
        end_ref[h] = state
        total_ref[h] = total
        back = backs[blocks - 1, h]
        for n in range(blocks - 2, -1, -1):
            back = mm(moves[n, h], back, TN) + backs[n, h]
        begin_ref[h] = back


def turn_kernel(heads, total_ref, end_ref, begin_ref, state_ref, back_ref, state_out, back_out):
    for h in range(heads):
        total = split(total_ref[h])
        state_out[h] = mm(total, state_ref[h]) + end_ref[h]
        back_out[h] = mm(total, back_ref[h], TN) + begin_ref[h]


def second_kernel(
    heads,
    blocks,
    doc_ref,
    x_ref,
    t_ref,
    w_ref,
    u_ref,
    y_ref,
    m_ref,
    c_ref,
    b_ref,
    state_ref,
    back_ref,
    out_ref,
    *wide_refs,
):
    rows, columns = iotas()
    base = lax.axis_index("ctx") * (blocks * L)
    offsets = doc_offsets(doc_ref)
    states, backs = {}, {}
    for h in range(heads):
        state = state_ref[h]
        for n in range(blocks):
            states[n, h] = state
            if n < blocks - 1:
                at = n * heads + h
                state = mm(m_ref[at], state) + c_ref[at]
        back = back_ref[h]
        for n in range(blocks - 1, -1, -1):
            backs[n, h] = back
            if n > 0:
                at = n * heads + h
                back = mm(m_ref[at], back, TN) + b_ref[at]
    lanes = columns
    for n in range(blocks):
        here = slice(n * L, (n + 1) * L)
        block = block_terms(x_ref, offsets, base, n, heads)
        k, q, rk, rq = block["k"], block["q"], block["rk"], block["rq"]
        kf, qf = k.astype(F32), block["qf"]
        dq = dk = bq_sum = b_sum = 0.0
        small = jnp.zeros((L, L), F32)
        for h in range(heads):
            at = n * heads + h
            head = block["heads"][h]
            beta, front, last, decay = head["beta"], head["front"], head["last"], head["decay"]
            v, g = value_of(x_ref, n, h, heads)
            gf = g.astype(F32)
            state, back = states[n, h], backs[n, h]
            state2, back2 = split(state), split(back)
            kh = rk * mm(k, state2)
            qh = rq * mm(q, state2)
            fresh = u_ref[at] - mm(w_ref[at], state2)
            dfresh = y_ref[at] + (last * rk) * mm(k, back2)
            dr = mm(t_ref[at], dfresh, TN)
            dvt = beta * dr
            out_ref[here, (2 + h) * DV : (3 + h) * DV] = dvt.astype(BF16)
            fresh2 = split(fresh)
            da = mm(dr, fresh2, NT)
            dp = mm(g, fresh2, NT)
            scaled = da * decay * block["kk"]
            z = dp * decay * block["qk"] - beta * scaled
            dbeta = jnp.sum(dr * (v.astype(F32) - front * kh), axis=1, keepdims=True) - jnp.sum(
                scaled, axis=1, keepdims=True
            )
            b_sum = b_sum - jnp.where(columns < rows, beta * da * decay, 0.0)
            bq_sum = bq_sum + dp * decay
            outer = mm(fresh, back2, NT)
            e = (last * rk) * jnp.sum(kf * outer, axis=1, keepdims=True)
            dsum = (
                front * jnp.sum(gf * qh - dvt * kh, axis=1, keepdims=True)
                - e
                + jnp.sum(z, axis=1, keepdims=True)
            )
            dsum_row = jnp.sum(jnp.where(rows == columns, dsum, 0.0) - z, axis=0, keepdims=True)
            tail = jnp.sum(e, axis=0, keepdims=True) + head["keep_all"] * jnp.sum(
                jnp.sum(state * back, axis=1, keepdims=True), axis=0, keepdims=True
            )
            dgate = (
                jnp.sum(jnp.where(columns >= rows, dsum_row, 0.0), axis=1, keepdims=True) + tail
            )
            ddecay = -dgate * head["sig"]
            dstrength = dbeta * beta * (1.0 - beta)
            for spot, value in ((h, ddecay), (heads + h, dstrength)):
                high = value.astype(BF16).astype(F32)
                small = jnp.where(lanes == spot, high, small)
                small = jnp.where(lanes == 2 * heads + spot, value - high, small)
            dq = dq + front * mm(g, state2, NT)
            dk = dk + last * outer - front * mm(dvt, state2, NT)
        rk_row = block["rk_row"]
        dq = dq + mm(bq_sum * rk_row, k)
        dk = dk + mm((b_sum + b_sum.T) * rk_row, k) + mm(bq_sum * rq, q, TN)
        dq = rq * (dq - qf * (block["r"] * block["r"] * jnp.sum(qf * dq, axis=1, keepdims=True)))
        dk = rk * (dk - kf * (rk * rk * jnp.sum(kf * dk, axis=1, keepdims=True)))
        if wide_refs:
            wide_refs[0][here, 0:DK] = dq
            wide_refs[0][here, DK : 2 * DK] = dk
        else:
            out_ref[here, 0:DK] = dq.astype(BF16)
            out_ref[here, DK : 2 * DK] = dk.astype(BF16)
        out_ref[here, (2 + heads) * DV : (3 + heads) * DV] = small.astype(BF16)


def passed_along(value, by):
    size = lax.axis_size("ctx")
    pairs = [(i, i + by) for i in range(size) if 0 <= i + by < size]
    return lax.ppermute(value, "ctx", pairs)


def body(queries, key_vectors, values, out_grad, decay_logit, beta_logit, doc_lengths):
    tok = queries.shape[0]
    peers = lax.axis_size("head") * lax.axis_size("rep")
    axes = ("head", "rep")
    heads = VALUE_HEADS // peers
    shared = heads % GROUP != 0
    span = tok * peers
    blocks = span // L
    units = blocks * heads
    assert not shared or heads == 1
    assert shared or heads == GROUP

    def by_peer(array, width):
        return array.reshape(tok, peers, width).transpose(1, 0, 2)

    def keys_by_peer(array):
        split_keys = by_peer(array, DK) if not shared else None
        if shared:
            by_key = array.reshape(tok, HK, DK).transpose(1, 0, 2)
            split_keys = jnp.repeat(by_key, GROUP, axis=0)
        return split_keys

    logits = jnp.concatenate([by_peer(decay_logit, heads), by_peer(beta_logit, heads)], axis=2)
    logits = jnp.pad(logits, ((0, 0), (0, 0), (0, DK - 2 * heads)))
    packed = jnp.concatenate(
        [
            keys_by_peer(queries),
            keys_by_peer(key_vectors),
            by_peer(values, heads * DV),
            by_peer(out_grad, heads * DV),
            logits,
        ],
        axis=2,
    )
    moved = lax.all_to_all(packed, axes, split_axis=0, concat_axis=0, tiled=True)
    x = moved.reshape(span, moved.shape[2])
    docs = doc_lengths.reshape(1, -1)

    square = jax.ShapeDtypeStruct((units, DK, DV), F32)
    edge = jax.ShapeDtypeStruct((heads, DK, DV), F32)
    params = pltpu.CompilerParams(vmem_limit_bytes=56 << 20)
    *kept, end, begin, total = pl.pallas_call(
        functools.partial(first_kernel, heads, blocks),
        out_shape=[square] * 7 + [edge] * 3,
        compiler_params=params,
        name="local_blocks",
    )(docs, x)

    shards = lax.axis_size("ctx")
    turns = min(shards - 1, (shards + 1) // 2)
    state, back = end, begin
    turn = pl.pallas_call(
        functools.partial(turn_kernel, heads),
        out_shape=[edge] * 2,
        name="turn",
    )
    for step in range(turns):
        if step:
            state, back = turn(total, end, begin, state, back)
        state, back = passed_along(state, 1), passed_along(back, -1)
    if not turns:
        state, back = jnp.zeros_like(end), jnp.zeros_like(begin)

    out_width = (3 + heads) * DV
    out_shapes = [jax.ShapeDtypeStruct((span, out_width), BF16)]
    if shared:
        out_shapes.append(jax.ShapeDtypeStruct((span, 2 * DK), F32))
    grads = pl.pallas_call(
        functools.partial(second_kernel, heads, blocks),
        out_shape=out_shapes,
        compiler_params=params,
        name="gradients",
    )(docs, x, *kept, state, back)

    sent = lax.all_to_all(
        grads[0].reshape(peers, tok, out_width), axes, split_axis=0, concat_axis=0, tiled=True
    )
    if shared:
        wide = lax.all_to_all(
            grads[1].reshape(peers, tok, 2 * DK), axes, split_axis=0, concat_axis=0, tiled=True
        )
        wide = wide.reshape(HK, GROUP, tok, 2 * DK).sum(1).astype(BF16)
    else:
        wide = sent[:, :, : 2 * DK]
    grad_queries = wide[:, :, :DK].transpose(1, 0, 2).reshape(tok, HK * DK)
    grad_keys = wide[:, :, DK:].transpose(1, 0, 2).reshape(tok, HK * DK)
    at = 2 * DK
    grad_values = sent[:, :, at : at + heads * DV].transpose(1, 0, 2).reshape(tok, VALUE_HEADS * DV)
    at += heads * DV
    small = sent[:, :, at : at + 4 * heads].astype(F32)
    small = small[:, :, : 2 * heads] + small[:, :, 2 * heads :]
    grad_decay = small[:, :, :heads].transpose(1, 0, 2).reshape(tok, VALUE_HEADS)
    grad_beta = small[:, :, heads:].transpose(1, 0, 2).reshape(tok, VALUE_HEADS)
    return (grad_queries, grad_keys, grad_values, grad_decay, grad_beta)


def solution(mesh):
    spec = P(("groups", "ctx", "head", "rep"), None)
    return jax.shard_map(
        body,
        mesh=mesh,
        in_specs=(spec,) * 6 + (P("groups"),),
        out_specs=(spec,) * 5,
        check_vma=False,
    )
```

```python
import functools

import jax
import jax.numpy as jnp
from jax import lax
from jax.experimental import pallas as pl
from jax.experimental.pallas import tpu as pltpu
from jax.sharding import PartitionSpec as P

VALUE_HEADS = 16
HK = 8
DK = 128
DV = 128
GROUP = VALUE_HEADS // HK
L = 128
ROWS = 16
TOK = 64
PER = L // TOK
EPS = 1e-06
F32 = jnp.float32
BF16 = jnp.bfloat16

NN = ((1,), (0,))
NT = ((1,), (1,))
TN = ((0,), (0,))


def split(x):
    if isinstance(x, tuple):
        return x
    if x.dtype == BF16:
        return (x,)
    high = x.astype(BF16)
    return (high, (x - high.astype(F32)).astype(BF16))


def mm(a, b, dims=NN):
    a, b = split(a), split(b)
    total = None
    for i, left in enumerate(a):
        for j, right in enumerate(b):
            if i + j < 2:
                term = lax.dot_general(left, right, (dims, ((), ())), preferred_element_type=F32)
                total = term if total is None else total + term
    return total


def iotas():
    rows = lax.broadcasted_iota(jnp.int32, (L, L), 0)
    columns = lax.broadcasted_iota(jnp.int32, (L, L), 1)
    return rows, columns


def unit_lower_inverse(lowers):
    rows, columns = iotas()
    eye = (rows == columns).astype(F32)
    powers = [jnp.where(rows // 16 == columns // 16, -a, 0.0) for a in lowers]
    sums = [eye + x for x in powers]
    for _ in range(3):
        halves = [split(x) for x in powers]
        powers = [mm(x, x) for x in halves]
        sums = [s + mm(s, x) for s, x in zip(sums, powers)]
    size = 16
    while size < L:
        mask = (rows // (2 * size) == columns // (2 * size)) & (rows // size != columns // size)
        edges = [jnp.where(mask, a, 0.0) for a in lowers]
        halves = [split(s) for s in sums]
        inner = [mm(e, t) for e, t in zip(edges, halves)]
        sums = [s - mm(t, i) for s, t, i in zip(sums, halves, inner)]
        size *= 2
    return sums


def doc_offsets(doc_ref):
    lengths = doc_ref[...]
    count = lengths.shape[1]
    rows = lax.broadcasted_iota(jnp.int32, (count, count), 0)
    columns = lax.broadcasted_iota(jnp.int32, (count, count), 1)
    column = jnp.sum(
        jnp.where(columns < rows, lengths.astype(F32), 0.0), axis=1, keepdims=True
    )
    row = jnp.sum(jnp.where(columns == rows, column, 0.0), axis=0, keepdims=True)
    return column, row


def taken(ref, n, piece):
    here = slice(piece * TOK, (piece + 1) * TOK)
    return jnp.concatenate([ref[n * PER + i, here, :] for i in range(PER)], axis=0)


def column(cols, spot):
    return cols[:, spot : spot + 1]


def q_scales(q):
    qf = q.astype(F32)
    r = lax.rsqrt(jnp.sum(qf * qf, axis=1, keepdims=True) + EPS)
    return qf, r, r * (DK**-0.5)


def pack_kernel(peers, heads, *refs):
    sources, out_ref, buffers, done = refs[:6], refs[6], refs[7:13], refs[13]
    copies = [
        pltpu.make_async_copy(source, buffer, done.at[i])
        for i, (source, buffer) in enumerate(zip(sources, buffers))
    ]
    for copy in copies:
        copy.start()
    q_ref, k_ref, v_ref, g_ref, decay_ref, beta_ref = buffers
    for i, (ref, piece) in enumerate(((q_ref, 0), (k_ref, 1))):
        copies[i].wait()
        for j in range(peers):
            key_head = j * heads // GROUP
            out_ref[j, piece * TOK : (piece + 1) * TOK, :] = ref[
                :, key_head * DK : (key_head + 1) * DK
            ]
    for i, (ref, piece) in enumerate(((v_ref, 2), (g_ref, 2 + heads))):
        copies[2 + i].wait()
        for j in range(peers):
            for h in range(heads):
                here = slice((piece + h) * TOK, (piece + h + 1) * TOK)
                lanes = slice((j * heads + h) * DV, (j * heads + h + 1) * DV)
                out_ref[j, here, :] = ref[:, lanes]
    copies[4].wait()
    copies[5].wait()
    logits = jnp.concatenate(
        [decay_ref[...].astype(F32), beta_ref[...].astype(F32)], axis=1
    ).astype(BF16)
    for j in range(peers):
        out_ref[j, (2 + 2 * heads) * TOK :, :] = logits


def to_neighbours(parity, even_ref, odd_ref, h, state, back):
    even = parity == 0
    even_ref[h] = jnp.where(even, state, back)
    odd_ref[h] = jnp.where(even, back, state)


def from_neighbours(parity, even_ref, odd_ref, h):
    even = parity == 0
    return jnp.where(even, odd_ref[h], even_ref[h]), jnp.where(even, even_ref[h], odd_ref[h])


def blocks_kernel(
    heads,
    blocks,
    doc_ref,
    x_ref,
    t_ref,
    w_ref,
    u_ref,
    y_ref,
    m_ref,
    decay_ref,
    kk_ref,
    qk_ref,
    cols_ref,
    state_ref,
    back_ref,
    end_ref,
    begin_ref,
    total_ref,
    even_ref,
    odd_ref,
    docs,
    arrived,
):
    rows, columns = iotas()
    eye = (rows == columns).astype(F32)
    shard = lax.axis_index("ctx")
    base = shard * (blocks * L)
    me = lax.axis_index("head") * lax.axis_size("rep") + lax.axis_index("rep")
    fetch = pltpu.make_async_copy(doc_ref, docs, arrived)
    fetch.start()
    small_row = lax.broadcasted_iota(jnp.int32, (ROWS, L), 0)
    lane = lax.broadcasted_iota(jnp.int32, (1, L), 1)
    units = [(n, h) for n in range(blocks) for h in range(heads)]
    half = ROWS // 2
    raw = jnp.zeros((ROWS, L), F32)
    for n in range(blocks):
        pieces = [x_ref[n * PER + i, (2 + 2 * heads) * TOK :, :].astype(F32) for i in range(PER)]
        for h in range(heads):
            mine = small_row == me * heads + h
            first, second = (
                jnp.sum(jnp.where(mine, piece, 0.0), axis=0, keepdims=True) for piece in pieces
            )
            decay_row = jnp.where(lane < TOK, first, pltpu.roll(second, TOK, 1))
            beta_row = jnp.where(lane < TOK, pltpu.roll(first, TOK, 1), second)
            raw = jnp.where(small_row == n * heads + h, decay_row, raw)
            raw = jnp.where(small_row == half + n * heads + h, beta_row, raw)
    soft = jnp.maximum(raw, 0.0) + jnp.log1p(jnp.exp(-jnp.abs(raw)))
    sig_rows = 1.0 / (1.0 + jnp.exp(-raw))
    vals_rows = jnp.where(small_row < half, -soft, sig_rows)
    vals, sigs = vals_rows.T, sig_rows.T
    keys, queries, lowers, infos, qks, decays, scales = [], [], [], {}, [], [], []
    for n in range(blocks):
        q, k = taken(x_ref, n, 0), taken(x_ref, n, 1)
        gram = mm(k, k, NT)
        square = jnp.where(rows == columns, gram, 0.0)
        rk_row = lax.rsqrt(jnp.sum(square, axis=0, keepdims=True) + EPS)
        rk = lax.rsqrt(jnp.sum(square, axis=1, keepdims=True) + EPS)
        _, _, rq = q_scales(q)
        kk_ref[n] = jnp.where(columns < rows, gram * rk * rk_row, 0.0)
        qk_ref[n] = mm(q, k, NT) * rq * rk_row
        keys.append(k)
        queries.append(q)
        scales.append((rk, rq))
    fetch.wait()
    off_col, off_row = doc_offsets(docs)
    for n in range(blocks):
        rk, rq = scales[n]
        kk, qk = kk_ref[n], qk_ref[n]
        first = (base + n * L).astype(F32)
        pos_row = first + lane.astype(F32)
        pos_col = first + lax.broadcasted_iota(jnp.int32, (L, 1), 0).astype(F32)
        doc_row = jnp.sum((off_col <= pos_row).astype(F32), axis=0, keepdims=True)
        doc_col = jnp.sum((off_row <= pos_col).astype(F32), axis=1, keepdims=True)
        before = jnp.sum((off_row <= first - 1.0).astype(F32), axis=1, keepdims=True)
        keep = (columns <= rows) & (doc_col == doc_row)
        qks.append(qk)
        cols = jnp.where(columns == 4 * heads, rk, 0.0)
        for h in range(heads):
            u = n * heads + h
            gate_row, gate_col = vals_rows[u : u + 1, :], column(vals, u)
            beta = column(vals, half + u)
            sum_col = jnp.sum(jnp.where(columns <= rows, gate_row, 0.0), axis=1, keepdims=True)
            sum_row = jnp.sum(jnp.where(rows <= columns, gate_col, 0.0), axis=0, keepdims=True)
            decay = jnp.where(keep, jnp.exp(jnp.where(keep, sum_col - sum_row, 0.0)), 0.0)
            front = jnp.where(doc_col == before, jnp.exp(sum_col), 0.0)
            last = jnp.where(
                doc_col == doc_col[L - 1 : L, :], jnp.exp(sum_col[L - 1 : L, :] - sum_col), 0.0
            )
            decay_ref[u] = decay
            decays.append(decay)
            lowers.append(beta * decay * kk)
            infos[n, h] = (beta, front, last, rk, rq)
            for spot, value in enumerate((beta, front, last, column(sigs, u))):
                cols = jnp.where(columns == spot * heads + h, value, cols)
        cols_ref[n] = cols
    inverses = unit_lower_inverse(lowers)
    moves, adds, backs = {}, {}, {}
    for n, h in units:
        u = n * heads + h
        beta, front, last, rk, rq = infos[n, h]
        k, q = keys[n], queries[n]
        v = taken(x_ref, n, 2 + h).astype(F32)
        g = taken(x_ref, n, 2 + heads + h)
        right = jnp.concatenate([(beta * front * rk) * k.astype(F32), beta * v], axis=1)
        both = mm(inverses[u], right)
        w = both[:, :DK]
        spread = mm(k, (last * rk) * both, TN)
        move = front[L - 1 : L, :] * eye - spread[:, :DK]
        y = mm(decays[u] * qks[n], g, TN)
        back = mm(q, (front * rq) * g.astype(F32), TN) - mm(w, y, TN)
        t_ref[u] = inverses[u]
        w_ref[u] = w
        u_ref[u] = both[:, DK:]
        y_ref[u] = y
        m_ref[u] = move
        moves[n, h], adds[n, h], backs[n, h] = split(move), spread[:, DK:], back
    ends, totals, begins = [], [], []
    zero = jnp.zeros((DK, DV), F32)
    for h in range(heads):
        state_ref[h] = zero
        back_ref[(blocks - 1) * heads + h] = zero
        ends.append(adds[0, h])
        begins.append(backs[blocks - 1, h])
        totals.append(moves[0, h][0].astype(F32) + moves[0, h][1].astype(F32))
    for step in range(1, blocks):
        ahead, behind = step, blocks - 1 - step
        for h in range(heads):
            state_ref[ahead * heads + h] = ends[h]
            both = mm(moves[ahead, h], jnp.concatenate([ends[h], totals[h]], axis=1))
            ends[h], totals[h] = both[:, :DV] + adds[ahead, h], both[:, DV:]
            back_ref[behind * heads + h] = begins[h]
            begins[h] = mm(moves[behind, h], begins[h], TN) + backs[behind, h]
    for h in range(heads):
        end_ref[h] = ends[h]
        begin_ref[h] = begins[h]
        total_ref[h] = totals[h]
        to_neighbours(shard % 2, even_ref, odd_ref, h, ends[h], begins[h])


def maps_kernel(
    heads, blocks, x_ref, t_ref, w_ref, m_ref, cols_ref, pre_ref, post_ref, fmap_ref, rmap_ref
):
    rows, columns = iotas()
    eye = (rows == columns).astype(F32)
    pres, posts = [eye] * heads, [eye] * heads
    for step in range(blocks):
        ahead, behind = step, blocks - 1 - step
        k = taken(x_ref, behind, 1)
        cols = cols_ref[behind]
        rk = column(cols, 4 * heads)
        for h in range(heads):
            u = ahead * heads + h
            pre_ref[u] = pres[h]
            if step == 0:
                fmap_ref[u] = w_ref[u]
                pres[h] = m_ref[u]
            else:
                halves = split(pres[h])
                fmap_ref[u] = mm(w_ref[u], halves)
                if step < blocks - 1:
                    pres[h] = mm(m_ref[u], halves)
            u = behind * heads + h
            post_ref[u] = posts[h]
            last = column(cols, 2 * heads + h)
            if step == 0:
                spread = k.astype(F32)
                posts[h] = m_ref[u].T
            else:
                halves = split(posts[h])
                spread = mm(k, halves)
                if step < blocks - 1:
                    posts[h] = mm(m_ref[u], halves, TN)
            rmap_ref[u] = mm(t_ref[u], (last * rk) * spread, TN)


def local_kernel(
    heads,
    blocks,
    x_ref,
    t_ref,
    w_ref,
    cols_ref,
    u_ref,
    y_ref,
    state_ref,
    back_ref,
    fresh_ref,
    dr_ref,
):
    for n in range(blocks):
        cols = cols_ref[n]
        k = taken(x_ref, n, 1)
        rk = column(cols, 4 * heads)
        for h in range(heads):
            u = n * heads + h
            last = column(cols, 2 * heads + h)
            fresh_ref[u] = u_ref[u] - mm(w_ref[u], state_ref[u]) if n else u_ref[u]
            dfresh = y_ref[u]
            if n < blocks - 1:
                dfresh = dfresh + (last * rk) * mm(k, back_ref[u])
            dr_ref[u] = mm(t_ref[u], dfresh, TN)


def turn_kernel(heads, total_ref, end_ref, begin_ref, even_in, odd_in, even_out, odd_out):
    parity = lax.axis_index("ctx") % 2
    for h in range(heads):
        total = split(total_ref[h])
        state, back = from_neighbours(parity, even_in, odd_in, h)
        state = mm(total, state) + end_ref[h]
        back = mm(total, back, TN) + begin_ref[h]
        to_neighbours(parity, even_out, odd_out, h, state, back)


def gradients_kernel(
    heads,
    x_ref,
    decay_ref,
    kk_ref,
    qk_ref,
    cols_ref,
    fresh_ref,
    dr_ref,
    state_ref,
    back_ref,
    pre_ref,
    post_ref,
    fmap_ref,
    rmap_ref,
    even_ref,
    odd_ref,
    out_ref,
    *wide_refs,
):
    rows, columns = iotas()
    parity = lax.axis_index("ctx") % 2
    cols = cols_ref[0]
    kk, qk = kk_ref[0], qk_ref[0]
    q, k = taken(x_ref, 0, 0), taken(x_ref, 0, 1)
    kf = k.astype(F32)
    qf, r, rq = q_scales(q)
    rk = column(cols, 4 * heads)
    dq = dk = bq_sum = b_sum = 0.0
    small = jnp.zeros((L, L), F32)
    wide = len(wide_refs) > 0
    at = 0 if wide else 2
    for h in range(heads):
        beta, front, last, sig = (column(cols, s * heads + h) for s in range(4))
        decay = decay_ref[h]
        v = taken(x_ref, 0, 2 + h)
        g = taken(x_ref, 0, 2 + heads + h)
        enter, leave = from_neighbours(parity, even_ref, odd_ref, h)
        enter2, leave2 = split(enter), split(leave)
        state = state_ref[h] + mm(pre_ref[h], enter2)
        back = back_ref[h] + mm(post_ref[h], leave2)
        fresh = fresh_ref[h] - mm(fmap_ref[h], enter2)
        dr = dr_ref[h] + mm(rmap_ref[h], leave2)
        state2, back2 = split(state), split(back)
        kh = rk * mm(k, state2)
        dvt = beta * dr
        dv = dvt.astype(BF16)
        for i in range(PER):
            out_ref[i, (at + h) * TOK : (at + h + 1) * TOK, :] = dv[i * TOK : (i + 1) * TOK]
        fresh2 = split(fresh)
        da = mm(dr, fresh2, NT)
        dp = mm(g, fresh2, NT)
        scaled = da * decay * kk
        dpd = dp * decay
        z = dpd * qk - beta * scaled
        dbeta = jnp.sum(dr * (v.astype(F32) - front * kh) - scaled, axis=1, keepdims=True)
        b_sum = b_sum - jnp.where(columns < rows, beta * da * decay, 0.0)
        bq_sum = bq_sum + dpd
        outer = mm(fresh2, back2, NT)
        gs = mm(g, state2, NT)
        e = (last * rk) * jnp.sum(kf * outer, axis=1, keepdims=True)
        dsum = jnp.sum(front * ((rq * qf) * gs - dvt * kh) + z, axis=1, keepdims=True) - e
        dsum_row = jnp.sum(jnp.where(rows == columns, dsum, 0.0) - z, axis=0, keepdims=True)
        tail = jnp.sum(e, axis=0, keepdims=True) + front[L - 1 : L, :] * jnp.sum(
            jnp.sum(state * back, axis=0, keepdims=True), axis=1, keepdims=True
        )
        dgate = jnp.sum(jnp.where(columns >= rows, dsum_row, 0.0), axis=1, keepdims=True) + tail
        small = jnp.where(columns == h, -dgate * sig, small)
        small = jnp.where(columns == heads + h, dbeta * beta * (1.0 - beta), small)
        dq = dq + front * gs
        dk = dk + last * outer - front * mm(dvt, state2, NT)
    kn = split(rk * kf)
    dq = dq + mm(bq_sum, kn)
    dk = dk + mm(b_sum + b_sum.T, kn) + mm(bq_sum, rq * qf, TN)
    dq = rq * (dq - qf * (r * r * jnp.sum(qf * dq, axis=1, keepdims=True)))
    dk = rk * (dk - kf * (rk * rk * jnp.sum(kf * dk, axis=1, keepdims=True)))
    small = small.T[: ROWS // 2]
    high = small.astype(BF16).astype(F32)
    pair = jnp.concatenate([high, small - high], axis=0)
    for i in range(PER):
        here = slice(i * TOK, (i + 1) * TOK)
        if wide:
            wide_refs[0][i, 0:TOK, :] = dq[here]
            wide_refs[0][i, TOK : 2 * TOK, :] = dk[here]
        else:
            out_ref[i, 0:TOK, :] = dq[here].astype(BF16)
            out_ref[i, TOK : 2 * TOK, :] = dk[here].astype(BF16)
        moved = pair if i == 0 else pltpu.roll(pair, L - i * TOK, 1)
        out_ref[i, (at + heads) * TOK :, :] = moved.astype(BF16)


def unpack_kernel(peers, heads, wide, *refs):
    if wide:
        x_ref, wide_ref, *outs = refs
    else:
        x_ref, *outs = refs
        wide_ref = None
    dq_ref, dk_ref, dv_ref, decay_ref, beta_ref = outs
    at = 0 if wide else 2
    spots = lax.broadcasted_iota(jnp.int32, (ROWS, L), 0)
    decays, betas = jnp.zeros((ROWS, L), F32), jnp.zeros((ROWS, L), F32)
    for j in range(peers):
        for h in range(heads):
            lanes = slice((j * heads + h) * DV, (j * heads + h + 1) * DV)
            dv_ref[:, lanes] = x_ref[j, (at + h) * TOK : (at + h + 1) * TOK, :]
        pair = x_ref[j, (at + heads) * TOK :, :].astype(F32)
        small = pair[: ROWS // 2] + pair[ROWS // 2 :]
        for h in range(heads):
            decays = jnp.where(spots == j * heads + h, small[h : h + 1], decays)
            betas = jnp.where(spots == j * heads + h, small[heads + h : heads + h + 1], betas)
    for i in range(HK):
        lanes = slice(i * DK, (i + 1) * DK)
        if wide:
            some = [wide_ref[i * GROUP + m] for m in range(GROUP)]
            total = some[0]
            for other in some[1:]:
                total = total + other
            total = total.astype(BF16)
            dq_ref[:, lanes] = total[:TOK]
            dk_ref[:, lanes] = total[TOK:]
        else:
            dq_ref[:, lanes] = x_ref[i, 0:TOK, :]
            dk_ref[:, lanes] = x_ref[i, TOK : 2 * TOK, :]
    decay_ref[...] = decays[:, :TOK]
    beta_ref[...] = betas[:, :TOK]


def over_edges(even, odd):
    size = lax.axis_size("ctx")
    results = []
    for first, value in ((0, even), (1, odd)):
        pairs = []
        for i in range(first, size - 1, 2):
            pairs += [(i, i + 1), (i + 1, i)]
        results.append(lax.ppermute(value, "ctx", pairs) if pairs else jnp.zeros_like(value))
    return results


def work(passes):
    return pl.CostEstimate(
        flops=2 * L * DK * DV * passes, bytes_accessed=1 << 20, transcendentals=0
    )


PARAMS = pltpu.CompilerParams(vmem_limit_bytes=16 << 20)


def body(queries, key_vectors, values, out_grad, decay_logit, beta_logit, doc_lengths):
    assert queries.shape[0] == TOK
    peers = lax.axis_size("head") * lax.axis_size("rep")
    heads = VALUE_HEADS // peers
    wide = heads % GROUP != 0
    blocks = TOK * peers // L
    units = blocks * heads
    assert heads == (1 if wide else GROUP) and units <= ROWS // 2

    def exchange(array):
        return lax.all_to_all(array, ("head", "rep"), split_axis=0, concat_axis=0, tiled=True)

    def call(kernel, shapes, inputs, passes, name, params=PARAMS, **rest):
        return pl.pallas_call(
            kernel,
            out_shape=shapes,
            compiler_params=params,
            cost_estimate=work(passes),
            name=name,
            **rest,
        )(*inputs)

    square = jax.ShapeDtypeStruct((units, DK, DV), F32)
    single = jax.ShapeDtypeStruct((blocks, DK, DV), F32)
    edge = jax.ShapeDtypeStruct((heads, DK, DV), F32)

    depth = (2 + 2 * heads) * TOK + ROWS
    sources = (queries, key_vectors, values, out_grad, decay_logit.T, beta_logit.T)
    sources = tuple(pltpu.with_memory_space_constraint(array, pltpu.HBM) for array in sources)
    packed = call(
        functools.partial(pack_kernel, peers, heads),
        jax.ShapeDtypeStruct((peers, depth, DK), BF16),
        sources,
        1,
        "pack",
        in_specs=[pl.BlockSpec(memory_space=pltpu.HBM)] * 6,
        scratch_shapes=[pltpu.VMEM(array.shape, BF16) for array in sources]
        + [pltpu.SemaphoreType.DMA((6,))],
    )
    x = exchange(packed)
    (t, w, u, y, m, decay, kk, qk, cols, state_loc, back_loc, end, begin, total, even, odd) = call(
        functools.partial(blocks_kernel, heads, blocks),
        [square] * 6 + [single] * 3 + [square] * 2 + [edge] * 5,
        (pltpu.with_memory_space_constraint(doc_lengths.reshape(1, -1), pltpu.HBM), x),
        60 * units,
        "blocks",
        in_specs=[pl.BlockSpec(memory_space=pltpu.HBM), pl.BlockSpec(memory_space=pltpu.VMEM)],
        scratch_shapes=[pltpu.VMEM((1, doc_lengths.shape[0]), jnp.int32), pltpu.SemaphoreType.DMA],
    )
    pre, post, fmap, rmap = call(
        functools.partial(maps_kernel, heads, blocks),
        [square] * 4,
        (x, t, w, m, cols),
        12 * units,
        "maps",
    )
    fresh, dr = call(
        functools.partial(local_kernel, heads, blocks),
        [square] * 2,
        (x, t, w, cols, u, y, state_loc, back_loc),
        8 * units,
        "local_rows",
    )

    shards = lax.axis_size("ctx")
    turns = min(shards - 1, (shards + 1) // 2)
    if turns == 0:
        even, odd = jnp.zeros_like(even), jnp.zeros_like(odd)
    for step in range(turns):
        if step:
            even, odd = call(
                functools.partial(turn_kernel, heads),
                [edge] * 2,
                (total, end, begin, even, odd),
                6 * heads,
                "turn",
            )
        even, odd = over_edges(even, odd)

    def step_of(array, count):
        rest = array.shape[1:]
        return pl.BlockSpec((count,) + rest, lambda n: (n,) + (0,) * len(rest))

    shapes = [jax.ShapeDtypeStruct((peers, (heads + (0 if wide else 2)) * TOK + ROWS, DV), BF16)]
    if wide:
        shapes.append(jax.ShapeDtypeStruct((peers, 2 * TOK, DK), F32))
    grads = call(
        functools.partial(gradients_kernel, heads),
        shapes,
        (x, decay, kk, qk, cols, fresh, dr, state_loc, back_loc, pre, post, fmap, rmap, even, odd),
        50 * units,
        "gradients",
        grid=(blocks,),
        in_specs=[step_of(x, PER), step_of(decay, heads)]
        + [step_of(kk, 1)] * 3
        + [step_of(fresh, heads)] * 8
        + [pl.BlockSpec((heads, DK, DV), lambda n: (0, 0, 0))] * 2,
        out_specs=[step_of(shape, PER) for shape in shapes],
    )
    grads = [exchange(array) for array in grads]
    *wide_grads, grad_decay, grad_beta = call(
        functools.partial(unpack_kernel, peers, heads, wide),
        [
            jax.ShapeDtypeStruct((TOK, HK * DK), BF16),
            jax.ShapeDtypeStruct((TOK, HK * DK), BF16),
            jax.ShapeDtypeStruct((TOK, VALUE_HEADS * DV), BF16),
            jax.ShapeDtypeStruct((VALUE_HEADS, TOK), F32),
            jax.ShapeDtypeStruct((VALUE_HEADS, TOK), F32),
        ],
        grads,
        1,
        "unpack",
    )
    return (*wide_grads, grad_decay.T, grad_beta.T)


def solution(mesh):
    spec = P(("groups", "ctx", "head", "rep"), None)
    return jax.shard_map(
        body,
        mesh=mesh,
        in_specs=(spec,) * 6 + (P("groups"),),
        out_specs=(spec,) * 5,
        check_vma=False,
    )
```

```python
import functools

import jax
import jax.numpy as jnp
from jax import lax
from jax.experimental import pallas as pl
from jax.experimental.pallas import tpu as pltpu
from jax.sharding import PartitionSpec as P

VALUE_HEADS = 16
HK = 8
DK = 128
DV = 128
GROUP = VALUE_HEADS // HK
L = 128
ROWS = 16
TOK = 64
PER = L // TOK
EPS = 1e-06
F32 = jnp.float32
BF16 = jnp.bfloat16

NN = ((1,), (0,))
NT = ((1,), (1,))
TN = ((0,), (0,))


def split(x):
    if isinstance(x, tuple):
        return x
    if x.dtype == BF16:
        return (x,)
    high = x.astype(BF16)
    return (high, (x - high.astype(F32)).astype(BF16))


def mm(a, b, dims=NN):
    a, b = split(a), split(b)
    free = 1 - dims[0][0]
    size = a[0].shape[free]

    def dot(left, right):
        return lax.dot_general(left, right, (dims, ((), ())), preferred_element_type=F32)

    total = dot(jnp.concatenate(a, axis=free), b[0]) if len(a) > 1 else dot(a[0], b[0])
    if len(a) > 1:
        total = total[:size] + total[size:]
    return total + dot(a[0], b[1]) if len(b) > 1 else total


def iotas():
    rows = lax.broadcasted_iota(jnp.int32, (L, L), 0)
    columns = lax.broadcasted_iota(jnp.int32, (L, L), 1)
    return rows, columns


def unit_lower_inverse(lowers):
    rows, columns = iotas()
    eye = (rows == columns).astype(F32)
    powers = [jnp.where(rows // 16 == columns // 16, -a, 0.0) for a in lowers]
    sums = [eye + x for x in powers]
    for _ in range(3):
        halves = [split(x) for x in powers]
        powers = [mm(x, x) for x in halves]
        sums = [s + mm(s, x) for s, x in zip(sums, powers)]
    size = 16
    while size < L:
        mask = (rows // (2 * size) == columns // (2 * size)) & (rows // size != columns // size)
        edges = [jnp.where(mask, a, 0.0) for a in lowers]
        halves = [split(s) for s in sums]
        inner = [mm(e, t) for e, t in zip(edges, halves)]
        sums = [s - mm(t, i) for s, t, i in zip(sums, halves, inner)]
        size *= 2
    return sums


def doc_offsets(doc_ref):
    lengths = doc_ref[...]
    count = lengths.shape[1]
    rows = lax.broadcasted_iota(jnp.int32, (count, count), 0)
    columns = lax.broadcasted_iota(jnp.int32, (count, count), 1)
    column = jnp.sum(
        jnp.where(columns < rows, lengths.astype(F32), 0.0), axis=1, keepdims=True
    )
    row = jnp.sum(jnp.where(columns == rows, column, 0.0), axis=0, keepdims=True)
    return column, row


def taken(ref, n, piece):
    here = slice(piece * TOK, (piece + 1) * TOK)
    return jnp.concatenate([ref[n * PER + i, here, :] for i in range(PER)], axis=0)


def column(cols, spot):
    return cols[:, spot : spot + 1]


def wide_column(cols, spot):
    return jnp.broadcast_to(column(cols, spot), (L, L))


def times_ones(rows_in, ones):
    parts, rest = [], rows_in
    for _ in range(3):
        part = rest.astype(BF16)
        parts.append(part.astype(F32))
        rest = rest - part.astype(F32)
    count = rows_in.shape[0]
    out = lax.dot_general(
        jnp.concatenate(parts, axis=0).astype(BF16),
        ones,
        (NN, ((), ())),
        preferred_element_type=F32,
    )
    return out[:count] + out[count : 2 * count] + out[2 * count :]


def pack_kernel(peers, heads, *refs):
    sources, out_ref, buffers, done = refs[:6], refs[6], refs[7:13], refs[13]
    copies = [
        pltpu.make_async_copy(source, buffer, done.at[i])
        for i, (source, buffer) in enumerate(zip(sources, buffers))
    ]
    for copy in copies:
        copy.start()
    q_ref, k_ref, v_ref, g_ref, decay_ref, beta_ref = buffers
    for i, (ref, piece) in enumerate(((q_ref, 0), (k_ref, 1))):
        copies[i].wait()
        for j in range(peers):
            key_head = j * heads // GROUP
            out_ref[j, piece * TOK : (piece + 1) * TOK, :] = ref[
                :, key_head * DK : (key_head + 1) * DK
            ]
    for i, (ref, piece) in enumerate(((v_ref, 2), (g_ref, 2 + heads))):
        copies[2 + i].wait()
        for j in range(peers):
            for h in range(heads):
                here = slice((piece + h) * TOK, (piece + h + 1) * TOK)
                lanes = slice((j * heads + h) * DV, (j * heads + h + 1) * DV)
                out_ref[j, here, :] = ref[:, lanes]
    copies[4].wait()
    copies[5].wait()
    logits = jnp.concatenate(
        [decay_ref[...].astype(F32), beta_ref[...].astype(F32)], axis=1
    ).astype(BF16)
    for j in range(peers):
        out_ref[j, (2 + 2 * heads) * TOK :, :] = logits


def to_neighbours(parity, even_ref, odd_ref, h, state, back):
    even = parity == 0
    even_ref[h] = jnp.where(even, state, back)
    odd_ref[h] = jnp.where(even, back, state)


def from_neighbours(parity, even_ref, odd_ref, h):
    even = parity == 0
    return jnp.where(even, odd_ref[h], even_ref[h]), jnp.where(even, even_ref[h], odd_ref[h])


def blocks_kernel(
    heads,
    blocks,
    doc_ref,
    x_ref,
    t_ref,
    w_ref,
    u_ref,
    y_ref,
    m_ref,
    decay_ref,
    kk_ref,
    qk_ref,
    rk_ref,
    rq_ref,
    state_ref,
    back_ref,
    end_ref,
    begin_ref,
    total_ref,
    even_ref,
    odd_ref,
    cols_ref,
    rows_ref,
    docs,
    arrived,
):
    rows, columns = iotas()
    eye = (rows == columns).astype(F32)
    shard = lax.axis_index("ctx")
    base = shard * (blocks * L)
    me = lax.axis_index("head") * lax.axis_size("rep") + lax.axis_index("rep")
    fetch = pltpu.make_async_copy(doc_ref, docs, arrived)
    fetch.start()
    lane = lax.broadcasted_iota(jnp.int32, (1, L), 1)
    units = [(n, h) for n in range(blocks) for h in range(heads)]
    half = ROWS // 2
    logit_row = lax.broadcasted_iota(jnp.int32, (ROWS, L), 0)
    unit_row = lax.broadcasted_iota(jnp.int32, (half, L), 0)

    def by_unit(row_of_block):
        out = jnp.zeros((half, L), F32)
        for n in range(blocks):
            out = jnp.where(unit_row // heads == n, row_of_block[n], out)
        return out

    keys, queries, grams, crosses, rk_rows, rq_rows = [], [], [], [], [], []
    for n in range(blocks):
        q, k = taken(x_ref, n, 0), taken(x_ref, n, 1)
        grams.append(mm(k, k, NT))
        crosses.append(mm(q, k, NT))
        for gram, out in ((grams[n], rk_rows), (mm(q, q, NT), rq_rows)):
            square = jnp.sum(jnp.where(rows == columns, gram, 0.0), axis=0, keepdims=True)
            out.append(lax.rsqrt(square + EPS))
        rq_rows[n] = rq_rows[n] * DK**-0.5
        keys.append(k)
        queries.append(q)
    decay_logits = jnp.zeros((half, L), F32)
    beta_logits = jnp.zeros((half, L), F32)
    for n in range(blocks):
        pieces = [x_ref[n * PER + i, (2 + 2 * heads) * TOK :, :].astype(F32) for i in range(PER)]
        for h in range(heads):
            mine = logit_row == me * heads + h
            first, second = (
                jnp.sum(jnp.where(mine, piece, 0.0), axis=0, keepdims=True) for piece in pieces
            )
            here = unit_row == n * heads + h
            decay_logits = jnp.where(
                here, jnp.where(lane < TOK, first, pltpu.roll(second, TOK, 1)), decay_logits
            )
            beta_logits = jnp.where(
                here, jnp.where(lane < TOK, pltpu.roll(first, TOK, 1), second), beta_logits
            )
    soft = jnp.maximum(decay_logits, 0.0) + jnp.log1p(jnp.exp(-jnp.abs(decay_logits)))
    beta_rows = 1.0 / (1.0 + jnp.exp(-beta_logits))
    sum_rows = times_ones(-soft, (rows <= columns).astype(BF16))
    rows_ref[...] = jnp.concatenate([1.0 / (1.0 + jnp.exp(-decay_logits)), beta_rows], axis=0)
    fetch.wait()
    off_col, off_row = doc_offsets(docs)
    doc_rows, befores = [], []
    for n in range(blocks):
        first = (base + n * L).astype(F32)
        doc_rows.append(
            jnp.sum((off_col <= first + lane.astype(F32)).astype(F32), axis=0, keepdims=True)
        )
        befores.append(jnp.sum((off_row <= first - 1.0).astype(F32), axis=1, keepdims=True))
    unit_docs = by_unit(doc_rows)
    front_rows = jnp.where(unit_docs == by_unit(befores), jnp.exp(sum_rows), 0.0)
    final = slice(L - 1, L)
    last_rows = jnp.where(
        unit_docs == unit_docs[:, final], jnp.exp(sum_rows[:, final] - sum_rows), 0.0
    )
    rk_units, rq_units = by_unit(rk_rows), by_unit(rq_rows)
    kinds = [
        sum_rows,
        beta_rows,
        front_rows,
        last_rows,
        last_rows * rk_units,
        rk_units,
        rq_units,
        unit_docs,
    ]
    cols = jnp.concatenate(kinds + [jnp.zeros((L - half * len(kinds), L), F32)], axis=0).T
    cols_ref[...] = cols
    write_rows = beta_rows * front_rows * rk_units
    read_rows = front_rows * rq_units
    lowers, decays = [], []
    for n in range(blocks):
        keep = (columns <= rows) & (column(cols, 7 * half + n * heads) == doc_rows[n])
        rk, rq = wide_column(cols, 5 * half + n * heads), wide_column(cols, 6 * half + n * heads)
        kk = jnp.where(columns < rows, grams[n] * rk * rk_rows[n], 0.0)
        rk_ref[n], rq_ref[n] = rk, rq
        kk_ref[n] = kk
        qk_ref[n] = crosses[n] * rq * rk_rows[n]
        for h in range(heads):
            u = n * heads + h
            spread = column(cols, u) - sum_rows[u : u + 1]
            decay = jnp.where(keep, jnp.exp(jnp.where(keep, spread, 0.0)), 0.0)
            decay_ref[u] = decay
            decays.append(decay)
            lowers.append(column(cols, half + u) * (decay * kk))
    inverses = unit_lower_inverse(lowers)
    moves, adds, backs = {}, {}, {}
    for n in range(blocks):
        k = keys[n]
        turned = queries[n].astype(F32).T
        for h in range(heads):
            u = n * heads + h
            here = slice(u, u + 1)
            v, g = taken(x_ref, n, 2 + h), taken(x_ref, n, 2 + heads + h)
            t = inverses[u] * beta_rows[here]
            w = mm(inverses[u] * write_rows[here], k)
            value = mm(t, v)
            spread = mm(k, column(cols, 4 * half + u) * jnp.concatenate([w, value], axis=1), TN)
            move = front_rows[here, final] * eye - spread[:, :DK]
            y = mm(decays[u] * qk_ref[n], g, TN)
            back = mm(turned * read_rows[here], g) - mm(w, y, TN)
            t_ref[u] = t
            w_ref[u] = w
            u_ref[u] = value
            y_ref[u] = y
            m_ref[u] = move
            moves[n, h], adds[n, h], backs[n, h] = split(move), spread[:, DK:], back
    ends, totals, begins = [], [], []
    zero = jnp.zeros((DK, DV), F32)
    for h in range(heads):
        state_ref[h] = zero
        back_ref[(blocks - 1) * heads + h] = zero
        ends.append(adds[0, h])
        begins.append(backs[blocks - 1, h])
        totals.append(m_ref[h])
    for step in range(1, blocks):
        ahead, behind = step, blocks - 1 - step
        for h in range(heads):
            state_ref[ahead * heads + h] = ends[h]
            both = mm(moves[ahead, h], jnp.concatenate([ends[h], totals[h]], axis=1))
            ends[h], totals[h] = both[:, :DV] + adds[ahead, h], both[:, DV:]
            back_ref[behind * heads + h] = begins[h]
            begins[h] = mm(moves[behind, h], begins[h], TN) + backs[behind, h]
    for h in range(heads):
        end_ref[h] = ends[h]
        begin_ref[h] = begins[h]
        total_ref[h] = totals[h]
        to_neighbours(shard % 2, even_ref, odd_ref, h, ends[h], begins[h])


def maps_kernel(
    heads,
    blocks,
    x_ref,
    t_ref,
    w_ref,
    m_ref,
    cols_ref,
    pre_ref,
    post_ref,
    fmap_ref,
    rmap_ref,
    front_ref,
    last_ref,
):
    rows, columns = iotas()
    eye = (rows == columns).astype(F32)
    half = ROWS // 2
    cols = cols_ref[...]
    pres, posts = [eye] * heads, [eye] * heads
    for step in range(blocks):
        ahead, behind = step, blocks - 1 - step
        k = taken(x_ref, behind, 1)
        for h in range(heads):
            u = ahead * heads + h
            front_ref[u] = wide_column(cols, 2 * half + u)
            last_ref[u] = wide_column(cols, 3 * half + u)
            pre_ref[u] = pres[h]
            if step == 0:
                fmap_ref[u] = w_ref[u]
                pres[h] = m_ref[u]
            else:
                halves = split(pres[h])
                fmap_ref[u] = mm(w_ref[u], halves)
                if step < blocks - 1:
                    pres[h] = mm(m_ref[u], halves)
            u = behind * heads + h
            post_ref[u] = posts[h]
            if step == 0:
                spread = k.astype(F32)
                posts[h] = m_ref[u].T
            else:
                halves = split(posts[h])
                spread = mm(k, halves)
                if step < blocks - 1:
                    posts[h] = mm(m_ref[u], halves, TN)
            rmap_ref[u] = mm(t_ref[u], column(cols, 4 * half + u) * spread, TN)


def local_kernel(
    heads,
    blocks,
    x_ref,
    t_ref,
    w_ref,
    cols_ref,
    u_ref,
    y_ref,
    state_ref,
    back_ref,
    fresh_ref,
    dv_ref,
):
    half = ROWS // 2
    cols = cols_ref[...]
    for n in range(blocks):
        k = taken(x_ref, n, 1)
        for h in range(heads):
            u = n * heads + h
            fresh_ref[u] = u_ref[u] - mm(w_ref[u], state_ref[u]) if n else u_ref[u]
            dfresh = y_ref[u]
            if n < blocks - 1:
                dfresh = dfresh + column(cols, 4 * half + u) * mm(k, back_ref[u])
            dv_ref[u] = mm(t_ref[u], dfresh, TN)


def turn_kernel(heads, total_ref, end_ref, begin_ref, even_in, odd_in, even_out, odd_out):
    parity = lax.axis_index("ctx") % 2
    for h in range(heads):
        total = split(total_ref[h])
        state, back = from_neighbours(parity, even_in, odd_in, h)
        state = mm(total, state) + end_ref[h]
        back = mm(total, back, TN) + begin_ref[h]
        to_neighbours(parity, even_out, odd_out, h, state, back)


def against(left, exact, right):
    left, right = split(left), split(right)

    def dot(parts, other):
        return lax.dot_general(
            jnp.concatenate(parts, axis=0), other, (NT, ((), ())), preferred_element_type=F32
        )

    high = dot([left[0], exact, left[1]], right[0])
    low = dot([left[0], exact], right[1])
    return high[:L] + high[2 * L :] + low[:L], high[L : 2 * L] + low[L:]


def gradients_kernel(
    heads,
    blocks,
    x_ref,
    decay_ref,
    kk_ref,
    qk_ref,
    rk_ref,
    rq_ref,
    rows_ref,
    fresh_ref,
    dv_ref,
    state_ref,
    back_ref,
    pre_ref,
    post_ref,
    fmap_ref,
    rmap_ref,
    front_ref,
    last_ref,
    even_ref,
    odd_ref,
    out_ref,
    *wide_refs,
):
    rows, columns = iotas()
    half = ROWS // 2
    small_row = lax.broadcasted_iota(jnp.int32, (half, L), 0)
    parity = lax.axis_index("ctx") % 2
    from_here = (rows >= columns).astype(BF16)
    wide = len(wide_refs) > 0
    at = 0 if wide else 2
    outside = [from_neighbours(parity, even_ref, odd_ref, h) for h in range(heads)]
    outside = [(split(enter), split(leave)) for enter, leave in outside]
    for n in range(blocks):
        kk, qk, rk, rq = kk_ref[n], qk_ref[n], rk_ref[n], rq_ref[n]
        q, k = taken(x_ref, n, 0), taken(x_ref, n, 1)
        kn, qn = rk * k.astype(F32), rq * q.astype(F32)
        dq = dk = bq_sum = b_sum = 0.0
        sums = jnp.zeros((L, L), F32)
        crossed = jnp.zeros((half, L), F32)
        tails = jnp.zeros((half, 1), F32)
        for h in range(heads):
            u = n * heads + h
            decay, front = decay_ref[u], front_ref[u]
            v = taken(x_ref, n, 2 + h).astype(F32)
            g = taken(x_ref, n, 2 + heads + h)
            enter2, leave2 = outside[h]
            state = state_ref[u] + mm(pre_ref[u], enter2)
            back = back_ref[u] + mm(post_ref[u], leave2)
            fresh2 = split(fresh_ref[u] - mm(fmap_ref[u], enter2))
            dv = dv_ref[u] + mm(rmap_ref[u], leave2)
            dv2, state2 = split(dv), split(state)
            for i in range(PER):
                out_ref[n * PER + i, (at + h) * TOK : (at + h + 1) * TOK, :] = dv2[0][
                    i * TOK : (i + 1) * TOK
                ]
            read = front * (rk * mm(k, state2))
            da, dp = against(dv2, g, fresh2)
            ds, gs = against(dv2, g, state2)
            b = jnp.where(columns < rows, da * decay, 0.0)
            bq = dp * decay
            scaled = b * kk
            z = bq * qk - scaled
            gs = front * gs
            outer = last_ref[u] * mm(fresh2, back, NT)
            kept = kn * outer
            by_sum = jnp.sum(qn * gs - dv * read - kept + z, axis=1, keepdims=True)
            by_beta = jnp.sum(dv * (v - read) - scaled, axis=1, keepdims=True)
            sums = jnp.where(columns == h, by_sum, sums)
            sums = jnp.where(columns == heads + h, by_beta, sums)
            crossed = jnp.where(small_row == h, jnp.sum(z, axis=0, keepdims=True), crossed)
            tail = jnp.sum(kept + front[L - 1 : L] * (state * back), axis=0, keepdims=True)
            tail = jnp.sum(tail, axis=1, keepdims=True)
            tails = jnp.where(small_row[:, :1] == h, tail, tails)
            b_sum = b_sum - b
            bq_sum = bq_sum + bq
            dq = dq + gs
            dk = dk + outer - front * ds
        turned = sums.T[:half]
        dsum = times_ones(turned - crossed, from_here) + tails
        small = turned
        for h in range(heads):
            u = n * heads + h
            sig, beta = rows_ref[u : u + 1], rows_ref[half + u : half + u + 1]
            small = jnp.where(small_row == h, -dsum * sig, small)
            small = jnp.where(small_row == heads + h, turned * (1.0 - beta), small)
        both = mm(jnp.concatenate([bq_sum, b_sum + b_sum.T], axis=0), kn)
        dq = dq + both[:L]
        dk = dk + both[L:] + mm(bq_sum, qn, TN)
        dq = rq * (dq - qn * (DK * jnp.sum(qn * dq, axis=1, keepdims=True)))
        dk = rk * (dk - kn * jnp.sum(kn * dk, axis=1, keepdims=True))
        high = small.astype(BF16).astype(F32)
        pair = jnp.concatenate([high, small - high], axis=0)
        for i in range(PER):
            here = slice(i * TOK, (i + 1) * TOK)
            if wide:
                wide_refs[0][n * PER + i, 0:TOK, :] = dq[here]
                wide_refs[0][n * PER + i, TOK : 2 * TOK, :] = dk[here]
            else:
                out_ref[n * PER + i, 0:TOK, :] = dq[here].astype(BF16)
                out_ref[n * PER + i, TOK : 2 * TOK, :] = dk[here].astype(BF16)
            moved = pair if i == 0 else pltpu.roll(pair, L - i * TOK, 1)
            out_ref[n * PER + i, (at + heads) * TOK :, :] = moved.astype(BF16)


def unpack_kernel(peers, heads, wide, *refs):
    if wide:
        x_ref, wide_ref, *outs = refs
    else:
        x_ref, *outs = refs
        wide_ref = None
    dq_ref, dk_ref, dv_ref, decay_ref, beta_ref = outs
    at = 0 if wide else 2
    spots = lax.broadcasted_iota(jnp.int32, (ROWS, L), 0)
    decays, betas = jnp.zeros((ROWS, L), F32), jnp.zeros((ROWS, L), F32)
    for j in range(peers):
        for h in range(heads):
            lanes = slice((j * heads + h) * DV, (j * heads + h + 1) * DV)
            dv_ref[:, lanes] = x_ref[j, (at + h) * TOK : (at + h + 1) * TOK, :]
        pair = x_ref[j, (at + heads) * TOK :, :].astype(F32)
        small = pair[: ROWS // 2] + pair[ROWS // 2 :]
        for h in range(heads):
            decays = jnp.where(spots == j * heads + h, small[h : h + 1], decays)
            betas = jnp.where(spots == j * heads + h, small[heads + h : heads + h + 1], betas)
    for i in range(HK):
        lanes = slice(i * DK, (i + 1) * DK)
        if wide:
            some = [wide_ref[i * GROUP + m] for m in range(GROUP)]
            total = some[0]
            for other in some[1:]:
                total = total + other
            total = total.astype(BF16)
            dq_ref[:, lanes] = total[:TOK]
            dk_ref[:, lanes] = total[TOK:]
        else:
            dq_ref[:, lanes] = x_ref[i, 0:TOK, :]
            dk_ref[:, lanes] = x_ref[i, TOK : 2 * TOK, :]
    decay_ref[...] = decays[:, :TOK]
    beta_ref[...] = betas[:, :TOK]


def over_edges(even, odd):
    size = lax.axis_size("ctx")
    results = []
    for first, value in ((0, even), (1, odd)):
        pairs = []
        for i in range(first, size - 1, 2):
            pairs += [(i, i + 1), (i + 1, i)]
        results.append(lax.ppermute(value, "ctx", pairs) if pairs else jnp.zeros_like(value))
    return results


def work(passes):
    return pl.CostEstimate(
        flops=2 * L * DK * DV * passes, bytes_accessed=1 << 20, transcendentals=0
    )


PARAMS = pltpu.CompilerParams(vmem_limit_bytes=16 << 20)


def body(queries, key_vectors, values, out_grad, decay_logit, beta_logit, doc_lengths):
    assert queries.shape[0] == TOK
    peers = lax.axis_size("head") * lax.axis_size("rep")
    heads = VALUE_HEADS // peers
    wide = heads % GROUP != 0
    blocks = TOK * peers // L
    units = blocks * heads
    assert heads == (1 if wide else GROUP) and units <= ROWS // 2

    def exchange(array):
        return lax.all_to_all(array, ("head", "rep"), split_axis=0, concat_axis=0, tiled=True)

    def call(kernel, shapes, inputs, passes, name, params=PARAMS, **rest):
        return pl.pallas_call(
            kernel,
            out_shape=shapes,
            compiler_params=params,
            cost_estimate=work(passes),
            name=name,
            **rest,
        )(*inputs)

    square = jax.ShapeDtypeStruct((units, DK, DV), F32)
    single = jax.ShapeDtypeStruct((blocks, DK, DV), F32)
    edge = jax.ShapeDtypeStruct((heads, DK, DV), F32)

    depth = (2 + 2 * heads) * TOK + ROWS
    sources = (queries, key_vectors, values, out_grad, decay_logit.T, beta_logit.T)
    sources = tuple(pltpu.with_memory_space_constraint(array, pltpu.HBM) for array in sources)
    packed = call(
        functools.partial(pack_kernel, peers, heads),
        jax.ShapeDtypeStruct((peers, depth, DK), BF16),
        sources,
        1,
        "pack",
        in_specs=[pl.BlockSpec(memory_space=pltpu.HBM)] * 6,
        scratch_shapes=[pltpu.VMEM(array.shape, BF16) for array in sources]
        + [pltpu.SemaphoreType.DMA((6,))],
    )
    x = exchange(packed)
    local = call(
        functools.partial(blocks_kernel, heads, blocks),
        [square] * 6
        + [single] * 4
        + [square] * 2
        + [edge] * 5
        + [jax.ShapeDtypeStruct((L, L), F32), jax.ShapeDtypeStruct((ROWS, L), F32)],
        (pltpu.with_memory_space_constraint(doc_lengths.reshape(1, -1), pltpu.HBM), x),
        60 * units,
        "blocks",
        in_specs=[pl.BlockSpec(memory_space=pltpu.HBM), pl.BlockSpec(memory_space=pltpu.VMEM)],
        scratch_shapes=[pltpu.VMEM((1, doc_lengths.shape[0]), jnp.int32), pltpu.SemaphoreType.DMA],
    )
    t, w, u, y, m, decay, kk, qk, rk, rq, state_loc, back_loc = local[:12]
    end, begin, total, even, odd, cols, rows = local[12:]
    pre, post, fmap, rmap, front, last = call(
        functools.partial(maps_kernel, heads, blocks),
        [square] * 6,
        (x, t, w, m, cols),
        12 * units,
        "maps",
    )
    fresh, dv = call(
        functools.partial(local_kernel, heads, blocks),
        [square] * 2,
        (x, t, w, cols, u, y, state_loc, back_loc),
        8 * units,
        "local_rows",
    )

    shards = lax.axis_size("ctx")
    turns = min(shards - 1, (shards + 1) // 2)
    if turns == 0:
        even, odd = jnp.zeros_like(even), jnp.zeros_like(odd)
    for step in range(turns):
        if step:
            even, odd = call(
                functools.partial(turn_kernel, heads),
                [edge] * 2,
                (total, end, begin, even, odd),
                6 * heads,
                "turn",
            )
        even, odd = over_edges(even, odd)

    shapes = [jax.ShapeDtypeStruct((peers, (heads + (0 if wide else 2)) * TOK + ROWS, DV), BF16)]
    if wide:
        shapes.append(jax.ShapeDtypeStruct((peers, 2 * TOK, DK), F32))
    grads = call(
        functools.partial(gradients_kernel, heads, blocks),
        shapes,
        (
            *(x, decay, kk, qk, rk, rq, rows, fresh, dv, state_loc, back_loc),
            *(pre, post, fmap, rmap, front, last, even, odd),
        ),
        50 * units,
        "gradients",
    )
    grads = [exchange(array) for array in grads]
    *wide_grads, grad_decay, grad_beta = call(
        functools.partial(unpack_kernel, peers, heads, wide),
        [
            jax.ShapeDtypeStruct((TOK, HK * DK), BF16),
            jax.ShapeDtypeStruct((TOK, HK * DK), BF16),
            jax.ShapeDtypeStruct((TOK, VALUE_HEADS * DV), BF16),
            jax.ShapeDtypeStruct((VALUE_HEADS, TOK), F32),
            jax.ShapeDtypeStruct((VALUE_HEADS, TOK), F32),
        ],
        grads,
        1,
        "unpack",
    )
    return (*wide_grads, grad_decay.T, grad_beta.T)


def solution(mesh):
    spec = P(("groups", "ctx", "head", "rep"), None)
    return jax.shard_map(
        body,
        mesh=mesh,
        in_specs=(spec,) * 6 + (P("groups"),),
        out_specs=(spec,) * 5,
        check_vma=False,
    )
```

```python
import functools

import jax
import jax.numpy as jnp
from jax import lax
from jax.experimental import pallas as pl
from jax.experimental.pallas import tpu as pltpu
from jax.sharding import PartitionSpec as P

VALUE_HEADS = 16
HK = 8
DK = 128
DV = 128
GROUP = VALUE_HEADS // HK
L = 128
ROWS = 16
TOK = 64
PER = L // TOK
EPS = 1e-06
F32 = jnp.float32
BF16 = jnp.bfloat16

NN = ((1,), (0,))
NT = ((1,), (1,))
TN = ((0,), (0,))


def split(x):
    if isinstance(x, tuple):
        return x
    if x.dtype == BF16:
        return (x,)
    high = x.astype(BF16)
    return (high, (x - high.astype(F32)).astype(BF16))


def mm(a, b, dims=NN):
    a, b = split(a), split(b)
    free = 1 - dims[0][0]
    size = a[0].shape[free]

    def dot(left, right):
        return lax.dot_general(left, right, (dims, ((), ())), preferred_element_type=F32)

    total = dot(jnp.concatenate(a, axis=free), b[0]) if len(a) > 1 else dot(a[0], b[0])
    if len(a) > 1:
        total = total[:size] + total[size:]
    return total + dot(a[0], b[1]) if len(b) > 1 else total


def iotas():
    rows = lax.broadcasted_iota(jnp.int32, (L, L), 0)
    columns = lax.broadcasted_iota(jnp.int32, (L, L), 1)
    return rows, columns


def odd_blocks(x, size):
    return jnp.concatenate([x[i + size : i + 2 * size] for i in range(0, L, 2 * size)], axis=0)


def into_odd_blocks(x, even, size):
    pieces = []
    for i in range(0, L, 2 * size):
        pieces += [even[i : i + size], x[i // 2 : i // 2 + size]]
    return jnp.concatenate(pieces, axis=0)


def unit_lower_inverse(lowers):
    rows, columns = iotas()
    eye = (rows == columns).astype(F32)
    zero = jnp.zeros((L, L), F32)
    firsts = [jnp.where(rows // 16 == columns // 16, -a, 0.0) for a in lowers]
    sums = [eye + x for x in firsts]
    powers = [mm(x, x) for x in firsts]
    for _ in range(2):
        both = [mm(jnp.concatenate([x, s], axis=0), x) for x, s in zip(powers, sums)]
        powers = [x[:L] for x in both]
        sums = [s + x[L:] for s, x in zip(sums, both)]
    sums = [s + mm(s, x) for s, x in zip(sums, powers)]
    size = 16
    while size < L:
        mask = (rows // (2 * size) == columns // (2 * size)) & (rows // size != columns // size)
        edges = [odd_blocks(jnp.where(mask, a, 0.0), size) for a in lowers]
        inner = [mm(e, s) for e, s in zip(edges, sums)]
        odds = [odd_blocks(s, size) for s in sums]
        odds = [o - mm(o, into_odd_blocks(i, zero, size)) for o, i in zip(odds, inner)]
        sums = [into_odd_blocks(o, s, size) for o, s in zip(odds, sums)]
        size *= 2
    return sums


def doc_offsets(doc_ref):
    lengths = doc_ref[...]
    count = lengths.shape[1]
    rows = lax.broadcasted_iota(jnp.int32, (count, count), 0)
    columns = lax.broadcasted_iota(jnp.int32, (count, count), 1)
    return jnp.sum(jnp.where(columns < rows, lengths.astype(F32), 0.0), axis=1, keepdims=True)


def taken(ref, n, piece):
    here = slice(piece * TOK, (piece + 1) * TOK)
    return jnp.concatenate([ref[n * PER + i, here, :] for i in range(PER)], axis=0)


def column(cols, spot):
    return cols[:, spot : spot + 1]


def wide_column(cols, spot):
    return jnp.broadcast_to(column(cols, spot), (L, L))


def times_ones(rows_in, ones):
    parts, rest = [], rows_in
    for _ in range(3):
        part = rest.astype(BF16)
        parts.append(part.astype(F32))
        rest = rest - part.astype(F32)
    count = rows_in.shape[0]
    out = lax.dot_general(
        jnp.concatenate(parts, axis=0).astype(BF16),
        ones,
        (NN, ((), ())),
        preferred_element_type=F32,
    )
    return out[:count] + out[count : 2 * count] + out[2 * count :]


def pack_kernel(peers, heads, *refs):
    count = 7
    sources, out_ref = refs[:count], refs[count]
    buffers, done = refs[count + 1 : 2 * count + 1], refs[2 * count + 1]
    copies = [
        pltpu.make_async_copy(source, buffer, done.at[i])
        for i, (source, buffer) in enumerate(zip(sources, buffers))
    ]
    for copy in copies:
        copy.start()
    decay_ref, beta_ref, doc_ref, q_ref, k_ref, v_ref, g_ref = buffers
    for copy in copies[:3]:
        copy.wait()
    logits = jnp.concatenate(
        [decay_ref[...].astype(F32), beta_ref[...].astype(F32)], axis=1
    )
    off_col = doc_offsets(doc_ref)
    place = lax.axis_index("ctx") * lax.axis_size("head") + lax.axis_index("head")
    first = (place * lax.axis_size("rep") + lax.axis_index("rep")) * TOK
    lane = lax.broadcasted_iota(jnp.int32, (1, L), 1)
    position = jnp.where(lane < TOK, first + lane, first - 1).astype(F32)
    docs = jnp.sum((off_col <= position).astype(F32), axis=0, keepdims=True)
    spot = lax.broadcasted_iota(jnp.int32, (ROWS, L), 0)
    for j in range(peers):
        tile = jnp.where(spot == heads, docs, 0.0)
        for h in range(heads):
            tile = jnp.where(spot == h, logits[j * heads + h : j * heads + h + 1], tile)
        out_ref[j, (2 + 2 * heads) * TOK :, :] = tile.astype(BF16)
    for i, (ref, piece) in enumerate(((q_ref, 0), (k_ref, 1))):
        copies[3 + i].wait()
        for j in range(peers):
            key_head = j * heads // GROUP
            out_ref[j, piece * TOK : (piece + 1) * TOK, :] = ref[
                :, key_head * DK : (key_head + 1) * DK
            ]
    for i, (ref, piece) in enumerate(((v_ref, 2), (g_ref, 2 + heads))):
        copies[5 + i].wait()
        for j in range(peers):
            for h in range(heads):
                here = slice((piece + h) * TOK, (piece + h + 1) * TOK)
                lanes = slice((j * heads + h) * DV, (j * heads + h + 1) * DV)
                out_ref[j, here, :] = ref[:, lanes]


def to_neighbours(parity, even_ref, odd_ref, h, state, back):
    even = parity == 0
    even_ref[h] = jnp.where(even, state, back)
    odd_ref[h] = jnp.where(even, back, state)


def from_neighbours(parity, even_ref, odd_ref, h):
    even = parity == 0
    return jnp.where(even, odd_ref[h], even_ref[h]), jnp.where(even, even_ref[h], odd_ref[h])


def blocks_kernel(
    heads,
    blocks,
    x_ref,
    t_ref,
    w_ref,
    u_ref,
    y_ref,
    m_ref,
    decay_ref,
    kk_ref,
    qk_ref,
    rk_ref,
    rq_ref,
    state_ref,
    back_ref,
    end_ref,
    begin_ref,
    even_ref,
    odd_ref,
    cols_ref,
    rows_ref,
):
    rows, columns = iotas()
    eye = (rows == columns).astype(F32)
    shard = lax.axis_index("ctx")
    lane = lax.broadcasted_iota(jnp.int32, (1, L), 1)
    units = [(n, h) for n in range(blocks) for h in range(heads)]
    half = ROWS // 2
    unit_row = lax.broadcasted_iota(jnp.int32, (half, L), 0)

    def by_unit(row_of_block):
        out = jnp.zeros((half, L), F32)
        for n in range(blocks):
            out = jnp.where(unit_row // heads == n, row_of_block[n], out)
        return out

    keys, queries, grams, crosses, rk_rows, rq_rows = [], [], [], [], [], []
    for n in range(blocks):
        q, k = taken(x_ref, n, 0), taken(x_ref, n, 1)
        grams.append(mm(k, k, NT))
        crosses.append(mm(q, k, NT))
        for gram, out in ((grams[n], rk_rows), (mm(q, q, NT), rq_rows)):
            square = jnp.sum(jnp.where(rows == columns, gram, 0.0), axis=0, keepdims=True)
            out.append(lax.rsqrt(square + EPS))
        rq_rows[n] = rq_rows[n] * DK**-0.5
        keys.append(k)
        queries.append(q)
    decay_logits = jnp.zeros((half, L), F32)
    beta_logits = jnp.zeros((half, L), F32)
    doc_rows, befores = [], []
    for n in range(blocks):
        first, second = (
            x_ref[n * PER + i, (2 + 2 * heads) * TOK :, :].astype(F32) for i in range(PER)
        )
        left = jnp.where(lane < TOK, first, pltpu.roll(second, TOK, 1))
        right = jnp.where(lane < TOK, pltpu.roll(first, TOK, 1), second)
        for h in range(heads):
            here = unit_row == n * heads + h
            decay_logits = jnp.where(here, left[h : h + 1], decay_logits)
            beta_logits = jnp.where(here, right[h : h + 1], beta_logits)
        doc_rows.append(left[heads : heads + 1])
        befores.append(first[heads : heads + 1, TOK : TOK + 1])
    soft = jnp.maximum(decay_logits, 0.0) + jnp.log1p(jnp.exp(-jnp.abs(decay_logits)))
    beta_rows = 1.0 / (1.0 + jnp.exp(-beta_logits))
    sum_rows = times_ones(-soft, (rows <= columns).astype(BF16))
    rows_ref[...] = jnp.concatenate([1.0 / (1.0 + jnp.exp(-decay_logits)), beta_rows], axis=0)
    unit_docs = by_unit(doc_rows)
    front_rows = jnp.where(unit_docs == by_unit(befores), jnp.exp(sum_rows), 0.0)
    final = slice(L - 1, L)
    last_rows = jnp.where(
        unit_docs == unit_docs[:, final], jnp.exp(sum_rows[:, final] - sum_rows), 0.0
    )
    rk_units, rq_units = by_unit(rk_rows), by_unit(rq_rows)
    kinds = [
        sum_rows,
        beta_rows,
        front_rows,
        last_rows,
        last_rows * rk_units,
        rk_units,
        rq_units,
        unit_docs,
    ]
    cols = jnp.concatenate(kinds + [jnp.zeros((L - half * len(kinds), L), F32)], axis=0).T
    cols_ref[...] = cols
    write_rows = beta_rows * front_rows * rk_units
    read_rows = front_rows * rq_units
    lowers, decays = [], []
    for n in range(blocks):
        keep = (columns <= rows) & (column(cols, 7 * half + n * heads) == doc_rows[n])
        rk, rq = wide_column(cols, 5 * half + n * heads), wide_column(cols, 6 * half + n * heads)
        kk = jnp.where(columns < rows, grams[n] * rk * rk_rows[n], 0.0)
        rk_ref[n], rq_ref[n] = rk, rq
        kk_ref[n] = kk
        qk_ref[n] = crosses[n] * rq * rk_rows[n]
        for h in range(heads):
            u = n * heads + h
            spread = column(cols, u) - sum_rows[u : u + 1]
            decay = jnp.where(keep, jnp.exp(jnp.where(keep, spread, 0.0)), 0.0)
            decay_ref[u] = decay
            decays.append(decay)
            lowers.append(column(cols, half + u) * (decay * kk))
    inverses = unit_lower_inverse(lowers)
    moves, adds, backs = {}, {}, {}
    for n in range(blocks):
        k = keys[n]
        turned = queries[n].astype(F32).T
        for h in range(heads):
            u = n * heads + h
            here = slice(u, u + 1)
            v, g = taken(x_ref, n, 2 + h), taken(x_ref, n, 2 + heads + h)
            t = inverses[u] * beta_rows[here]
            w = mm(inverses[u] * write_rows[here], k)
            value = mm(t, v)
            spread = mm(k, column(cols, 4 * half + u) * jnp.concatenate([w, value], axis=1), TN)
            move = front_rows[here, final] * eye - spread[:, :DK]
            y = mm(decays[u] * qk_ref[n], g, TN)
            back = mm(turned * read_rows[here], g) - mm(w, y, TN)
            t_ref[u] = t
            w_ref[u] = w
            u_ref[u] = value
            y_ref[u] = y
            m_ref[u] = move
            moves[n, h], adds[n, h], backs[n, h] = split(move), spread[:, DK:], back
    ends, begins = [], []
    zero = jnp.zeros((DK, DV), F32)
    for h in range(heads):
        state_ref[h] = zero
        back_ref[(blocks - 1) * heads + h] = zero
        ends.append(adds[0, h])
        begins.append(backs[blocks - 1, h])
    for step in range(1, blocks):
        ahead, behind = step, blocks - 1 - step
        for h in range(heads):
            state_ref[ahead * heads + h] = ends[h]
            ends[h] = mm(moves[ahead, h], ends[h]) + adds[ahead, h]
            back_ref[behind * heads + h] = begins[h]
            begins[h] = mm(moves[behind, h], begins[h], TN) + backs[behind, h]
    for h in range(heads):
        end_ref[h] = ends[h]
        begin_ref[h] = begins[h]
        to_neighbours(shard % 2, even_ref, odd_ref, h, ends[h], begins[h])


def maps_kernel(
    heads,
    blocks,
    x_ref,
    t_ref,
    w_ref,
    m_ref,
    cols_ref,
    pre_ref,
    post_ref,
    fmap_ref,
    rmap_ref,
    front_ref,
    last_ref,
    total_ref,
):
    rows, columns = iotas()
    eye = (rows == columns).astype(F32)
    half = ROWS // 2
    cols = cols_ref[...]
    pres, posts = [eye] * heads, [eye] * heads
    for step in range(blocks):
        ahead, behind = step, blocks - 1 - step
        k = taken(x_ref, behind, 1)
        for h in range(heads):
            u = ahead * heads + h
            front_ref[u] = wide_column(cols, 2 * half + u)
            last_ref[u] = wide_column(cols, 3 * half + u)
            pre_ref[u] = pres[h]
            if step == 0:
                fmap_ref[u] = w_ref[u]
                pres[h] = m_ref[u]
            else:
                halves = split(pres[h])
                both = mm(jnp.concatenate([w_ref[u], m_ref[u]], axis=0), halves)
                fmap_ref[u] = both[:L]
                pres[h] = both[L:]
            u = behind * heads + h
            post_ref[u] = posts[h]
            if step == 0:
                spread = k.astype(F32)
                posts[h] = m_ref[u].T
            else:
                halves = split(posts[h])
                spread = mm(k, halves)
                if step < blocks - 1:
                    posts[h] = mm(m_ref[u], halves, TN)
            rmap_ref[u] = mm(t_ref[u], column(cols, 4 * half + u) * spread, TN)
    for h in range(heads):
        total_ref[h] = pres[h]


def local_kernel(
    heads,
    blocks,
    x_ref,
    t_ref,
    w_ref,
    cols_ref,
    u_ref,
    y_ref,
    state_ref,
    back_ref,
    fresh_ref,
    dv_ref,
):
    half = ROWS // 2
    cols = cols_ref[...]
    for n in range(blocks):
        k = taken(x_ref, n, 1)
        for h in range(heads):
            u = n * heads + h
            fresh_ref[u] = u_ref[u] - mm(w_ref[u], state_ref[u]) if n else u_ref[u]
            dfresh = y_ref[u]
            if n < blocks - 1:
                dfresh = dfresh + column(cols, 4 * half + u) * mm(k, back_ref[u])
            dv_ref[u] = mm(t_ref[u], dfresh, TN)


def turn_kernel(heads, total_ref, end_ref, begin_ref, even_in, odd_in, even_out, odd_out):
    parity = lax.axis_index("ctx") % 2
    for h in range(heads):
        total = split(total_ref[h])
        state, back = from_neighbours(parity, even_in, odd_in, h)
        state = mm(total, state) + end_ref[h]
        back = mm(total, back, TN) + begin_ref[h]
        to_neighbours(parity, even_out, odd_out, h, state, back)


def against(left, exact, right):
    left, right = split(left), split(right)

    def dot(parts, other):
        return lax.dot_general(
            jnp.concatenate(parts, axis=0), other, (NT, ((), ())), preferred_element_type=F32
        )

    high = dot([left[0], exact, left[1]], right[0])
    low = dot([left[0], exact], right[1])
    return high[:L] + high[2 * L :] + low[:L], high[L : 2 * L] + low[L:]


def gradients_kernel(
    heads,
    blocks,
    x_ref,
    decay_ref,
    kk_ref,
    qk_ref,
    rk_ref,
    rq_ref,
    rows_ref,
    fresh_ref,
    dv_ref,
    state_ref,
    back_ref,
    pre_ref,
    post_ref,
    fmap_ref,
    rmap_ref,
    front_ref,
    last_ref,
    even_ref,
    odd_ref,
    out_ref,
    *wide_refs,
):
    rows, columns = iotas()
    half = ROWS // 2
    small_row = lax.broadcasted_iota(jnp.int32, (half, L), 0)
    parity = lax.axis_index("ctx") % 2
    from_here = (rows >= columns).astype(BF16)
    wide = len(wide_refs) > 0
    at = 0 if wide else 2
    outside = [from_neighbours(parity, even_ref, odd_ref, h) for h in range(heads)]
    outside = [(split(enter), split(leave)) for enter, leave in outside]
    for n in range(blocks):
        kk, qk, rk, rq = kk_ref[n], qk_ref[n], rk_ref[n], rq_ref[n]
        q, k = taken(x_ref, n, 0), taken(x_ref, n, 1)
        kn, qn = rk * k.astype(F32), rq * q.astype(F32)
        dq = dk = bq_sum = b_sum = 0.0
        sums = jnp.zeros((L, L), F32)
        crossed = jnp.zeros((half, L), F32)
        tails = jnp.zeros((half, 1), F32)
        for h in range(heads):
            u = n * heads + h
            decay, front = decay_ref[u], front_ref[u]
            v = taken(x_ref, n, 2 + h).astype(F32)
            g = taken(x_ref, n, 2 + heads + h)
            enter2, leave2 = outside[h]
            state = state_ref[u] + mm(pre_ref[u], enter2)
            back = back_ref[u] + mm(post_ref[u], leave2)
            fresh2 = split(fresh_ref[u] - mm(fmap_ref[u], enter2))
            dv = dv_ref[u] + mm(rmap_ref[u], leave2)
            dv2, state2 = split(dv), split(state)
            for i in range(PER):
                out_ref[n * PER + i, (at + h) * TOK : (at + h + 1) * TOK, :] = dv2[0][
                    i * TOK : (i + 1) * TOK
                ]
            read = front * (rk * mm(k, state2))
            da, dp = against(dv2, g, fresh2)
            ds, gs = against(dv2, g, state2)
            b = jnp.where(columns < rows, da * decay, 0.0)
            bq = dp * decay
            scaled = b * kk
            z = bq * qk - scaled
            gs = front * gs
            outer = last_ref[u] * mm(fresh2, back, NT)
            kept = kn * outer
            by_sum = jnp.sum(qn * gs - dv * read - kept + z, axis=1, keepdims=True)
            by_beta = jnp.sum(dv * (v - read) - scaled, axis=1, keepdims=True)
            sums = jnp.where(columns == h, by_sum, sums)
            sums = jnp.where(columns == heads + h, by_beta, sums)
            crossed = jnp.where(small_row == h, jnp.sum(z, axis=0, keepdims=True), crossed)
            tail = jnp.sum(kept + front[L - 1 : L] * (state * back), axis=0, keepdims=True)
            tail = jnp.sum(tail, axis=1, keepdims=True)
            tails = jnp.where(small_row[:, :1] == h, tail, tails)
            b_sum = b_sum - b
            bq_sum = bq_sum + bq
            dq = dq + gs
            dk = dk + outer - front * ds
        turned = sums.T[:half]
        dsum = times_ones(turned - crossed, from_here) + tails
        small = turned
        for h in range(heads):
            u = n * heads + h
            sig, beta = rows_ref[u : u + 1], rows_ref[half + u : half + u + 1]
            small = jnp.where(small_row == h, -dsum * sig, small)
            small = jnp.where(small_row == heads + h, turned * (1.0 - beta), small)
        both = mm(jnp.concatenate([bq_sum, b_sum + b_sum.T], axis=0), kn)
        dq = dq + both[:L]
        dk = dk + both[L:] + mm(bq_sum, qn, TN)
        dq = rq * (dq - qn * (DK * jnp.sum(qn * dq, axis=1, keepdims=True)))
        dk = rk * (dk - kn * jnp.sum(kn * dk, axis=1, keepdims=True))
        high = small.astype(BF16).astype(F32)
        pair = jnp.concatenate([high, small - high], axis=0)
        for i in range(PER):
            here = slice(i * TOK, (i + 1) * TOK)
            if wide:
                wide_refs[0][n * PER + i, 0:TOK, :] = dq[here]
                wide_refs[0][n * PER + i, TOK : 2 * TOK, :] = dk[here]
            else:
                out_ref[n * PER + i, 0:TOK, :] = dq[here].astype(BF16)
                out_ref[n * PER + i, TOK : 2 * TOK, :] = dk[here].astype(BF16)
            moved = pair if i == 0 else pltpu.roll(pair, L - i * TOK, 1)
            out_ref[n * PER + i, (at + heads) * TOK :, :] = moved.astype(BF16)


def unpack_kernel(peers, heads, wide, *refs):
    if wide:
        x_ref, wide_ref, *outs = refs
    else:
        x_ref, *outs = refs
        wide_ref = None
    dq_ref, dk_ref, dv_ref, decay_ref, beta_ref = outs
    at = 0 if wide else 2
    spots = lax.broadcasted_iota(jnp.int32, (ROWS, L), 0)
    decays, betas = jnp.zeros((ROWS, L), F32), jnp.zeros((ROWS, L), F32)
    for j in range(peers):
        for h in range(heads):
            lanes = slice((j * heads + h) * DV, (j * heads + h + 1) * DV)
            dv_ref[:, lanes] = x_ref[j, (at + h) * TOK : (at + h + 1) * TOK, :]
        pair = x_ref[j, (at + heads) * TOK :, :].astype(F32)
        small = pair[: ROWS // 2] + pair[ROWS // 2 :]
        for h in range(heads):
            decays = jnp.where(spots == j * heads + h, small[h : h + 1], decays)
            betas = jnp.where(spots == j * heads + h, small[heads + h : heads + h + 1], betas)
    for i in range(HK):
        lanes = slice(i * DK, (i + 1) * DK)
        if wide:
            some = [wide_ref[i * GROUP + m] for m in range(GROUP)]
            total = some[0]
            for other in some[1:]:
                total = total + other
            total = total.astype(BF16)
            dq_ref[:, lanes] = total[:TOK]
            dk_ref[:, lanes] = total[TOK:]
        else:
            dq_ref[:, lanes] = x_ref[i, 0:TOK, :]
            dk_ref[:, lanes] = x_ref[i, TOK : 2 * TOK, :]
    decay_ref[...] = decays[:, :TOK]
    beta_ref[...] = betas[:, :TOK]


def over_edges(even, odd):
    size = lax.axis_size("ctx")
    results = []
    for first, value in ((0, even), (1, odd)):
        pairs = []
        for i in range(first, size - 1, 2):
            pairs += [(i, i + 1), (i + 1, i)]
        results.append(lax.ppermute(value, "ctx", pairs) if pairs else jnp.zeros_like(value))
    return results


def work(passes):
    return pl.CostEstimate(
        flops=2 * L * DK * DV * passes, bytes_accessed=1 << 20, transcendentals=0
    )


PARAMS = pltpu.CompilerParams(vmem_limit_bytes=16 << 20)


def body(queries, key_vectors, values, out_grad, decay_logit, beta_logit, doc_lengths):
    assert queries.shape[0] == TOK
    peers = lax.axis_size("head") * lax.axis_size("rep")
    heads = VALUE_HEADS // peers
    wide = heads % GROUP != 0
    blocks = TOK * peers // L
    units = blocks * heads
    assert heads == (1 if wide else GROUP) and units <= ROWS // 2

    def exchange(array):
        return lax.all_to_all(array, ("head", "rep"), split_axis=0, concat_axis=0, tiled=True)

    def call(kernel, shapes, inputs, passes, name, params=PARAMS, **rest):
        return pl.pallas_call(
            kernel,
            out_shape=shapes,
            compiler_params=params,
            cost_estimate=work(passes),
            name=name,
            **rest,
        )(*inputs)

    square = jax.ShapeDtypeStruct((units, DK, DV), F32)
    single = jax.ShapeDtypeStruct((blocks, DK, DV), F32)
    edge = jax.ShapeDtypeStruct((heads, DK, DV), F32)

    depth = (2 + 2 * heads) * TOK + ROWS
    assert doc_lengths.shape[0] <= 256
    docs = doc_lengths.reshape(1, -1)
    sources = (decay_logit.T, beta_logit.T, docs, queries, key_vectors, values, out_grad)
    sources = tuple(pltpu.with_memory_space_constraint(array, pltpu.HBM) for array in sources)
    packed = call(
        functools.partial(pack_kernel, peers, heads),
        jax.ShapeDtypeStruct((peers, depth, DK), BF16),
        sources,
        1,
        "pack",
        in_specs=[pl.BlockSpec(memory_space=pltpu.HBM)] * len(sources),
        scratch_shapes=[pltpu.VMEM(array.shape, array.dtype) for array in sources]
        + [pltpu.SemaphoreType.DMA((len(sources),))],
    )
    x = exchange(packed)
    local = call(
        functools.partial(blocks_kernel, heads, blocks),
        [square] * 6
        + [single] * 4
        + [square] * 2
        + [edge] * 4
        + [jax.ShapeDtypeStruct((L, L), F32), jax.ShapeDtypeStruct((ROWS, L), F32)],
        (x,),
        60 * units,
        "blocks",
    )
    t, w, u, y, m, decay, kk, qk, rk, rq, state_loc, back_loc = local[:12]
    end, begin, even, odd, cols, rows = local[12:]
    pre, post, fmap, rmap, front, last, total = call(
        functools.partial(maps_kernel, heads, blocks),
        [square] * 6 + [edge],
        (x, t, w, m, cols),
        12 * units,
        "maps",
    )
    fresh, dv = call(
        functools.partial(local_kernel, heads, blocks),
        [square] * 2,
        (x, t, w, cols, u, y, state_loc, back_loc),
        8 * units,
        "local_rows",
    )

    shards = lax.axis_size("ctx")
    turns = min(shards - 1, (shards + 1) // 2)
    if turns == 0:
        even, odd = jnp.zeros_like(even), jnp.zeros_like(odd)
    for step in range(turns):
        if step:
            even, odd = call(
                functools.partial(turn_kernel, heads),
                [edge] * 2,
                (total, end, begin, even, odd),
                6 * heads,
                "turn",
            )
        even, odd = over_edges(even, odd)

    shapes = [jax.ShapeDtypeStruct((peers, (heads + (0 if wide else 2)) * TOK + ROWS, DV), BF16)]
    if wide:
        shapes.append(jax.ShapeDtypeStruct((peers, 2 * TOK, DK), F32))
    grads = call(
        functools.partial(gradients_kernel, heads, blocks),
        shapes,
        (
            *(x, decay, kk, qk, rk, rq, rows, fresh, dv, state_loc, back_loc),
            *(pre, post, fmap, rmap, front, last, even, odd),
        ),
        50 * units,
        "gradients",
    )
    grads = [exchange(array) for array in grads]
    *wide_grads, grad_decay, grad_beta = call(
        functools.partial(unpack_kernel, peers, heads, wide),
        [
            jax.ShapeDtypeStruct((TOK, HK * DK), BF16),
            jax.ShapeDtypeStruct((TOK, HK * DK), BF16),
            jax.ShapeDtypeStruct((TOK, VALUE_HEADS * DV), BF16),
            jax.ShapeDtypeStruct((VALUE_HEADS, TOK), F32),
            jax.ShapeDtypeStruct((VALUE_HEADS, TOK), F32),
        ],
        grads,
        1,
        "unpack",
    )
    return (*wide_grads, grad_decay.T, grad_beta.T)


def solution(mesh):
    spec = P(("groups", "ctx", "head", "rep"), None)
    return jax.shard_map(
        body,
        mesh=mesh,
        in_specs=(spec,) * 6 + (P("groups"),),
        out_specs=(spec,) * 5,
        check_vma=False,
    )
```

```python
import functools

import jax
import jax.numpy as jnp
from jax import lax
from jax.experimental import pallas as pl
from jax.experimental.pallas import tpu as pltpu
from jax.sharding import PartitionSpec as P

VALUE_HEADS = 16
HK = 8
DK = 128
DV = 128
GROUP = VALUE_HEADS // HK
L = 128
ROWS = 16
TOK = 64
PER = L // TOK
EPS = 1e-06
F32 = jnp.float32
BF16 = jnp.bfloat16

NN = ((1,), (0,))
NT = ((1,), (1,))
TN = ((0,), (0,))


def split(x):
    if isinstance(x, tuple):
        return x
    if x.dtype == BF16:
        return (x,)
    high = x.astype(BF16)
    return (high, (x - high.astype(F32)).astype(BF16))


def mm(a, b, dims=NN):
    a, b = split(a), split(b)
    left_along, right_along = dims[0][0], dims[1][0]
    across = 1 - right_along
    size = b[0].shape[across]
    left = jnp.concatenate(a, axis=left_along) if len(a) > 1 else a[0]
    right = jnp.concatenate(b, axis=across) if len(b) > 1 else b[0]
    if len(a) > 1:
        below = [b[0], jnp.zeros_like(b[0])] if len(b) > 1 else [b[0]]
        below = jnp.concatenate(below, axis=across) if len(below) > 1 else below[0]
        right = jnp.concatenate([right, below], axis=right_along)
    out = lax.dot_general(left, right, (dims, ((), ())), preferred_element_type=F32)
    return out[:, :size] + out[:, size:] if len(b) > 1 else out


def iotas():
    rows = lax.broadcasted_iota(jnp.int32, (L, L), 0)
    columns = lax.broadcasted_iota(jnp.int32, (L, L), 1)
    return rows, columns


def unit_lower_inverse(lowers):
    rows, columns = iotas()
    eye = (rows == columns).astype(F32)
    near = rows // 16 == columns // 16
    firsts = [jnp.where(near, -a, 0.0) for a in lowers]
    sums = [eye + x for x in firsts]
    powers = [mm(x, x) for x in firsts]
    for _ in range(2):
        both = [mm(jnp.concatenate([x, s], axis=0), x) for x, s in zip(powers, sums)]
        powers = [x[:L] for x in both]
        sums = [s + x[L:] for s, x in zip(sums, both)]
    sums = [s + mm(s, x) for s, x in zip(sums, powers)]
    firsts = [mm(s, jnp.where(near, 0.0, -a)) for s, a in zip(sums, lowers)]
    powers = [mm(x, x) for x in firsts]
    both = [mm(jnp.concatenate([x, y], axis=0), x) for x, y in zip(powers, firsts)]
    fourths = [x[:L] for x in both]
    leads = [eye + y + x + b[L:] for y, x, b in zip(firsts, powers, both)]
    sums = [s + mm(x, s) for s, x in zip(sums, fourths)]
    return [mm(x, s) for x, s in zip(leads, sums)]


def doc_offsets(doc_ref):
    lengths = doc_ref[...]
    count = lengths.shape[1]
    rows = lax.broadcasted_iota(jnp.int32, (count, count), 0)
    columns = lax.broadcasted_iota(jnp.int32, (count, count), 1)
    return jnp.sum(jnp.where(columns < rows, lengths.astype(F32), 0.0), axis=1, keepdims=True)


def taken(ref, n, piece):
    here = slice(piece * TOK, (piece + 1) * TOK)
    return jnp.concatenate([ref[n * PER + i, here, :] for i in range(PER)], axis=0)


def column(cols, spot):
    return cols[:, spot : spot + 1]


def wide_column(cols, spot):
    return jnp.broadcast_to(column(cols, spot), (L, L))


def times_ones(rows_in, ones):
    parts, rest = [], rows_in
    for _ in range(3):
        part = rest.astype(BF16)
        parts.append(part.astype(F32))
        rest = rest - part.astype(F32)
    count = rows_in.shape[0]
    out = lax.dot_general(
        jnp.concatenate(parts, axis=0).astype(BF16),
        ones,
        (NN, ((), ())),
        preferred_element_type=F32,
    )
    return out[:count] + out[count : 2 * count] + out[2 * count :]


def pack_kernel(peers, heads, *refs):
    count = 7
    sources, out_ref = refs[:count], refs[count]
    buffers, done = refs[count + 1 : 2 * count + 1], refs[2 * count + 1]
    copies = [
        pltpu.make_async_copy(source, buffer, done.at[i])
        for i, (source, buffer) in enumerate(zip(sources, buffers))
    ]
    for copy in copies:
        copy.start()
    decay_ref, beta_ref, doc_ref, q_ref, k_ref, v_ref, g_ref = buffers
    for copy in copies[:3]:
        copy.wait()
    logits = jnp.concatenate(
        [decay_ref[...].astype(F32), beta_ref[...].astype(F32)], axis=1
    )
    off_col = doc_offsets(doc_ref)
    place = lax.axis_index("ctx") * lax.axis_size("head") + lax.axis_index("head")
    first = (place * lax.axis_size("rep") + lax.axis_index("rep")) * TOK
    lane = lax.broadcasted_iota(jnp.int32, (1, L), 1)
    position = jnp.where(lane < TOK, first + lane, first - 1).astype(F32)
    docs = jnp.sum((off_col <= position).astype(F32), axis=0, keepdims=True)
    spot = lax.broadcasted_iota(jnp.int32, (ROWS, L), 0)
    for j in range(peers):
        tile = jnp.where(spot == heads, docs, 0.0)
        for h in range(heads):
            tile = jnp.where(spot == h, logits[j * heads + h : j * heads + h + 1], tile)
        out_ref[j, (2 + 2 * heads) * TOK :, :] = tile.astype(BF16)
    for i, (ref, piece) in enumerate(((q_ref, 0), (k_ref, 1))):
        copies[3 + i].wait()
        for j in range(peers):
            key_head = j * heads // GROUP
            out_ref[j, piece * TOK : (piece + 1) * TOK, :] = ref[
                :, key_head * DK : (key_head + 1) * DK
            ]
    for i, (ref, piece) in enumerate(((v_ref, 2), (g_ref, 2 + heads))):
        copies[5 + i].wait()
        for j in range(peers):
            for h in range(heads):
                here = slice((piece + h) * TOK, (piece + h + 1) * TOK)
                lanes = slice((j * heads + h) * DV, (j * heads + h + 1) * DV)
                out_ref[j, here, :] = ref[:, lanes]


def to_neighbours(parity, even_ref, odd_ref, h, state, back):
    even = parity == 0
    even_ref[h] = jnp.where(even, state, back)
    odd_ref[h] = jnp.where(even, back, state)


def from_neighbours(parity, even_ref, odd_ref, h):
    even = parity == 0
    return jnp.where(even, odd_ref[h], even_ref[h]), jnp.where(even, even_ref[h], odd_ref[h])


def blocks_kernel(
    heads,
    blocks,
    x_ref,
    t_ref,
    w_ref,
    u_ref,
    y_ref,
    m_ref,
    decay_ref,
    kk_ref,
    qk_ref,
    rk_ref,
    rq_ref,
    state_ref,
    back_ref,
    end_ref,
    begin_ref,
    even_ref,
    odd_ref,
    cols_ref,
    rows_ref,
):
    rows, columns = iotas()
    eye = (rows == columns).astype(F32)
    shard = lax.axis_index("ctx")
    lane = lax.broadcasted_iota(jnp.int32, (1, L), 1)
    units = [(n, h) for n in range(blocks) for h in range(heads)]
    half = ROWS // 2
    unit_row = lax.broadcasted_iota(jnp.int32, (half, L), 0)

    def by_unit(row_of_block):
        out = jnp.zeros((half, L), F32)
        for n in range(blocks):
            out = jnp.where(unit_row // heads == n, row_of_block[n], out)
        return out

    keys, queries, grams, crosses, rk_rows, rq_rows = [], [], [], [], [], []
    for n in range(blocks):
        q, k = taken(x_ref, n, 0), taken(x_ref, n, 1)
        grams.append(mm(k, k, NT))
        crosses.append(mm(q, k, NT))
        for gram, out in ((grams[n], rk_rows), (mm(q, q, NT), rq_rows)):
            square = jnp.sum(jnp.where(rows == columns, gram, 0.0), axis=0, keepdims=True)
            out.append(lax.rsqrt(square + EPS))
        rq_rows[n] = rq_rows[n] * DK**-0.5
        keys.append(k)
        queries.append(q)
    decay_logits = jnp.zeros((half, L), F32)
    beta_logits = jnp.zeros((half, L), F32)
    doc_rows, befores = [], []
    for n in range(blocks):
        first, second = (
            x_ref[n * PER + i, (2 + 2 * heads) * TOK :, :].astype(F32) for i in range(PER)
        )
        left = jnp.where(lane < TOK, first, pltpu.roll(second, TOK, 1))
        right = jnp.where(lane < TOK, pltpu.roll(first, TOK, 1), second)
        for h in range(heads):
            here = unit_row == n * heads + h
            decay_logits = jnp.where(here, left[h : h + 1], decay_logits)
            beta_logits = jnp.where(here, right[h : h + 1], beta_logits)
        doc_rows.append(left[heads : heads + 1])
        befores.append(first[heads : heads + 1, TOK : TOK + 1])
    soft = jnp.maximum(decay_logits, 0.0) + jnp.log1p(jnp.exp(-jnp.abs(decay_logits)))
    beta_rows = 1.0 / (1.0 + jnp.exp(-beta_logits))
    sum_rows = times_ones(-soft, (rows <= columns).astype(BF16))
    rows_ref[...] = jnp.concatenate([1.0 / (1.0 + jnp.exp(-decay_logits)), beta_rows], axis=0)
    unit_docs = by_unit(doc_rows)
    front_rows = jnp.where(unit_docs == by_unit(befores), jnp.exp(sum_rows), 0.0)
    final = slice(L - 1, L)
    last_rows = jnp.where(
        unit_docs == unit_docs[:, final], jnp.exp(sum_rows[:, final] - sum_rows), 0.0
    )
    rk_units, rq_units = by_unit(rk_rows), by_unit(rq_rows)
    kinds = [
        sum_rows,
        beta_rows,
        front_rows,
        last_rows,
        last_rows * rk_units,
        rk_units,
        rq_units,
        unit_docs,
    ]
    cols = jnp.concatenate(kinds + [jnp.zeros((L - half * len(kinds), L), F32)], axis=0).T
    cols_ref[...] = cols
    write_rows = beta_rows * front_rows * rk_units
    read_rows = front_rows * rq_units
    lowers, decays = [], []
    for n in range(blocks):
        keep = (columns <= rows) & (column(cols, 7 * half + n * heads) == doc_rows[n])
        rk, rq = wide_column(cols, 5 * half + n * heads), wide_column(cols, 6 * half + n * heads)
        kk = jnp.where(columns < rows, grams[n] * rk * rk_rows[n], 0.0)
        rk_ref[n], rq_ref[n] = rk, rq
        kk_ref[n] = kk
        qk_ref[n] = crosses[n] * rq * rk_rows[n]
        for h in range(heads):
            u = n * heads + h
            spread = column(cols, u) - sum_rows[u : u + 1]
            decay = jnp.where(keep, jnp.exp(jnp.where(keep, spread, 0.0)), 0.0)
            decay_ref[u] = decay
            decays.append(decay)
            lowers.append(column(cols, half + u) * (decay * kk))
    inverses = unit_lower_inverse(lowers)
    moves, adds, backs = {}, {}, {}
    for n in range(blocks):
        k = keys[n]
        turned = queries[n].astype(F32).T
        for h in range(heads):
            u = n * heads + h
            here = slice(u, u + 1)
            v, g = taken(x_ref, n, 2 + h), taken(x_ref, n, 2 + heads + h)
            t = inverses[u] * beta_rows[here]
            w = mm(inverses[u] * write_rows[here], k)
            value = mm(t, v)
            spread = mm(k, column(cols, 4 * half + u) * jnp.concatenate([w, value], axis=1), TN)
            move = front_rows[here, final] * eye - spread[:, :DK]
            y = mm(decays[u] * qk_ref[n], g, TN)
            back = mm(turned * read_rows[here], g) - mm(w, y, TN)
            t_ref[u] = t
            w_ref[u] = w
            u_ref[u] = value
            y_ref[u] = y
            m_ref[u] = move
            moves[n, h], adds[n, h], backs[n, h] = split(move), spread[:, DK:], back
    ends, begins = [], []
    zero = jnp.zeros((DK, DV), F32)
    for h in range(heads):
        state_ref[h] = zero
        back_ref[(blocks - 1) * heads + h] = zero
        ends.append(adds[0, h])
        begins.append(backs[blocks - 1, h])
    for step in range(1, blocks):
        ahead, behind = step, blocks - 1 - step
        for h in range(heads):
            state_ref[ahead * heads + h] = ends[h]
            ends[h] = mm(moves[ahead, h], ends[h]) + adds[ahead, h]
            back_ref[behind * heads + h] = begins[h]
            begins[h] = mm(moves[behind, h], begins[h], TN) + backs[behind, h]
    for h in range(heads):
        end_ref[h] = ends[h]
        begin_ref[h] = begins[h]
        to_neighbours(shard % 2, even_ref, odd_ref, h, ends[h], begins[h])


def maps_kernel(
    heads,
    blocks,
    x_ref,
    t_ref,
    w_ref,
    m_ref,
    cols_ref,
    pre_ref,
    post_ref,
    fmap_ref,
    rmap_ref,
    front_ref,
    last_ref,
    total_ref,
):
    rows, columns = iotas()
    eye = (rows == columns).astype(F32)
    half = ROWS // 2
    cols = cols_ref[...]
    pres, posts = [eye] * heads, [eye] * heads
    for step in range(blocks):
        ahead, behind = step, blocks - 1 - step
        k = taken(x_ref, behind, 1)
        for h in range(heads):
            u = ahead * heads + h
            front_ref[u] = wide_column(cols, 2 * half + u)
            last_ref[u] = wide_column(cols, 3 * half + u)
            pre_ref[u] = pres[h]
            if step == 0:
                fmap_ref[u] = w_ref[u]
                pres[h] = m_ref[u]
            else:
                halves = split(pres[h])
                both = mm(jnp.concatenate([w_ref[u], m_ref[u]], axis=0), halves)
                fmap_ref[u] = both[:L]
                pres[h] = both[L:]
            u = behind * heads + h
            post_ref[u] = posts[h]
            if step == 0:
                spread = k.astype(F32)
                posts[h] = m_ref[u].T
            else:
                halves = split(posts[h])
                spread = mm(k, halves)
                if step < blocks - 1:
                    posts[h] = mm(m_ref[u], halves, TN)
            rmap_ref[u] = mm(t_ref[u], column(cols, 4 * half + u) * spread, TN)
    for h in range(heads):
        total_ref[h] = pres[h]


def local_kernel(
    heads,
    blocks,
    x_ref,
    t_ref,
    w_ref,
    cols_ref,
    u_ref,
    y_ref,
    state_ref,
    back_ref,
    fresh_ref,
    dv_ref,
):
    half = ROWS // 2
    cols = cols_ref[...]
    for n in range(blocks):
        k = taken(x_ref, n, 1)
        for h in range(heads):
            u = n * heads + h
            fresh_ref[u] = u_ref[u] - mm(w_ref[u], state_ref[u]) if n else u_ref[u]
            dfresh = y_ref[u]
            if n < blocks - 1:
                dfresh = dfresh + column(cols, 4 * half + u) * mm(k, back_ref[u])
            dv_ref[u] = mm(t_ref[u], dfresh, TN)


def turn_kernel(heads, total_ref, end_ref, begin_ref, even_in, odd_in, even_out, odd_out):
    parity = lax.axis_index("ctx") % 2
    for h in range(heads):
        total = split(total_ref[h])
        state, back = from_neighbours(parity, even_in, odd_in, h)
        state = mm(total, state) + end_ref[h]
        back = mm(total, back, TN) + begin_ref[h]
        to_neighbours(parity, even_out, odd_out, h, state, back)


def against(left, exact, right):
    left = split(left)
    exact = (exact, jnp.zeros_like(exact))
    both = tuple(jnp.concatenate(parts, axis=0) for parts in zip(left, exact))
    out = mm(both, right, NT)
    return out[:L], out[L:]


def gradients_kernel(
    heads,
    blocks,
    x_ref,
    decay_ref,
    kk_ref,
    qk_ref,
    rk_ref,
    rq_ref,
    rows_ref,
    fresh_ref,
    dv_ref,
    state_ref,
    back_ref,
    pre_ref,
    post_ref,
    fmap_ref,
    rmap_ref,
    front_ref,
    last_ref,
    even_ref,
    odd_ref,
    out_ref,
    *wide_refs,
):
    rows, columns = iotas()
    half = ROWS // 2
    small_row = lax.broadcasted_iota(jnp.int32, (half, L), 0)
    parity = lax.axis_index("ctx") % 2
    from_here = (rows >= columns).astype(BF16)
    wide = len(wide_refs) > 0
    at = 0 if wide else 2
    outside = [from_neighbours(parity, even_ref, odd_ref, h) for h in range(heads)]
    outside2 = [(split(enter), split(leave)) for enter, leave in outside]
    for n in range(blocks):
        kk, qk, rk, rq = kk_ref[n], qk_ref[n], rk_ref[n], rq_ref[n]
        q, k = taken(x_ref, n, 0), taken(x_ref, n, 1)
        kn, qn = rk * k.astype(F32), rq * q.astype(F32)
        dq = dk = bq_sum = b_sum = 0.0
        sums = jnp.zeros((L, L), F32)
        crossed = jnp.zeros((half, L), F32)
        tails = jnp.zeros((half, 1), F32)
        for h in range(heads):
            u = n * heads + h
            decay, front = decay_ref[u], front_ref[u]
            v = taken(x_ref, n, 2 + h).astype(F32)
            g = taken(x_ref, n, 2 + heads + h)
            enter2, leave2 = outside2[h]
            if n == 0:
                state, seen = outside[h][0], mm(fmap_ref[u], enter2)
            else:
                both = mm(jnp.concatenate([pre_ref[u], fmap_ref[u]], axis=0), enter2)
                state, seen = state_ref[u] + both[:L], both[L:]
            if n == blocks - 1:
                back, dv = outside[h][1], mm(rmap_ref[u], leave2)
            else:
                both = mm(jnp.concatenate([post_ref[u], rmap_ref[u]], axis=0), leave2)
                back, dv = back_ref[u] + both[:L], both[L:]
            fresh2 = split(fresh_ref[u] - seen)
            dv = dv_ref[u] + dv
            dv2, state2 = split(dv), split(state)
            for i in range(PER):
                out_ref[n * PER + i, (at + h) * TOK : (at + h + 1) * TOK, :] = dv2[0][
                    i * TOK : (i + 1) * TOK
                ]
            read = front * (rk * mm(k, state2))
            da, dp = against(dv2, g, fresh2)
            ds, gs = against(dv2, g, state2)
            b = jnp.where(columns < rows, da * decay, 0.0)
            bq = dp * decay
            scaled = b * kk
            z = bq * qk - scaled
            gs = front * gs
            outer = last_ref[u] * mm(fresh2, back, NT)
            kept = kn * outer
            by_sum = jnp.sum(qn * gs - dv * read - kept + z, axis=1, keepdims=True)
            by_beta = jnp.sum(dv * (v - read) - scaled, axis=1, keepdims=True)
            sums = jnp.where(columns == h, by_sum, sums)
            sums = jnp.where(columns == heads + h, by_beta, sums)
            crossed = jnp.where(small_row == h, jnp.sum(z, axis=0, keepdims=True), crossed)
            tail = jnp.sum(kept + front[L - 1 : L] * (state * back), axis=0, keepdims=True)
            tail = jnp.sum(tail, axis=1, keepdims=True)
            tails = jnp.where(small_row[:, :1] == h, tail, tails)
            b_sum = b_sum - b
            bq_sum = bq_sum + bq
            dq = dq + gs
            dk = dk + outer - front * ds
        turned = sums.T[:half]
        dsum = times_ones(turned - crossed, from_here) + tails
        small = turned
        for h in range(heads):
            u = n * heads + h
            sig, beta = rows_ref[u : u + 1], rows_ref[half + u : half + u + 1]
            small = jnp.where(small_row == h, -dsum * sig, small)
            small = jnp.where(small_row == heads + h, turned * (1.0 - beta), small)
        both = mm(jnp.concatenate([bq_sum, b_sum + b_sum.T], axis=0), kn)
        dq = dq + both[:L]
        dk = dk + both[L:] + mm(bq_sum, qn, TN)
        dq = rq * (dq - qn * (DK * jnp.sum(qn * dq, axis=1, keepdims=True)))
        dk = rk * (dk - kn * jnp.sum(kn * dk, axis=1, keepdims=True))
        high = small.astype(BF16).astype(F32)
        pair = jnp.concatenate([high, small - high], axis=0)
        for i in range(PER):
            here = slice(i * TOK, (i + 1) * TOK)
            if wide:
                wide_refs[0][n * PER + i, 0:TOK, :] = dq[here]
                wide_refs[0][n * PER + i, TOK : 2 * TOK, :] = dk[here]
            else:
                out_ref[n * PER + i, 0:TOK, :] = dq[here].astype(BF16)
                out_ref[n * PER + i, TOK : 2 * TOK, :] = dk[here].astype(BF16)
            moved = pair if i == 0 else pltpu.roll(pair, L - i * TOK, 1)
            out_ref[n * PER + i, (at + heads) * TOK :, :] = moved.astype(BF16)


def unpack_kernel(peers, heads, wide, *refs):
    if wide:
        x_ref, wide_ref, *outs = refs
    else:
        x_ref, *outs = refs
        wide_ref = None
    dq_ref, dk_ref, dv_ref, decay_ref, beta_ref = outs
    at = 0 if wide else 2
    spots = lax.broadcasted_iota(jnp.int32, (ROWS, L), 0)
    decays, betas = jnp.zeros((ROWS, L), F32), jnp.zeros((ROWS, L), F32)
    for j in range(peers):
        for h in range(heads):
            lanes = slice((j * heads + h) * DV, (j * heads + h + 1) * DV)
            dv_ref[:, lanes] = x_ref[j, (at + h) * TOK : (at + h + 1) * TOK, :]
        pair = x_ref[j, (at + heads) * TOK :, :].astype(F32)
        small = pair[: ROWS // 2] + pair[ROWS // 2 :]
        for h in range(heads):
            decays = jnp.where(spots == j * heads + h, small[h : h + 1], decays)
            betas = jnp.where(spots == j * heads + h, small[heads + h : heads + h + 1], betas)
    for i in range(HK):
        lanes = slice(i * DK, (i + 1) * DK)
        if wide:
            some = [wide_ref[i * GROUP + m] for m in range(GROUP)]
            total = some[0]
            for other in some[1:]:
                total = total + other
            total = total.astype(BF16)
            dq_ref[:, lanes] = total[:TOK]
            dk_ref[:, lanes] = total[TOK:]
        else:
            dq_ref[:, lanes] = x_ref[i, 0:TOK, :]
            dk_ref[:, lanes] = x_ref[i, TOK : 2 * TOK, :]
    decay_ref[...] = decays[:, :TOK]
    beta_ref[...] = betas[:, :TOK]


def over_edges(even, odd):
    size = lax.axis_size("ctx")
    results = []
    for first, value in ((0, even), (1, odd)):
        pairs = []
        for i in range(first, size - 1, 2):
            pairs += [(i, i + 1), (i + 1, i)]
        results.append(lax.ppermute(value, "ctx", pairs) if pairs else jnp.zeros_like(value))
    return results


def work(passes):
    return pl.CostEstimate(
        flops=2 * L * DK * DV * passes, bytes_accessed=1 << 20, transcendentals=0
    )


PARAMS = pltpu.CompilerParams(vmem_limit_bytes=16 << 20)


def body(queries, key_vectors, values, out_grad, decay_logit, beta_logit, doc_lengths):
    assert queries.shape[0] == TOK
    peers = lax.axis_size("head") * lax.axis_size("rep")
    heads = VALUE_HEADS // peers
    wide = heads % GROUP != 0
    blocks = TOK * peers // L
    units = blocks * heads
    assert heads == (1 if wide else GROUP) and units <= ROWS // 2

    def exchange(array):
        return lax.all_to_all(array, ("head", "rep"), split_axis=0, concat_axis=0, tiled=True)

    def call(kernel, shapes, inputs, passes, name, params=PARAMS, **rest):
        return pl.pallas_call(
            kernel,
            out_shape=shapes,
            compiler_params=params,
            cost_estimate=work(passes),
            name=name,
            **rest,
        )(*inputs)

    square = jax.ShapeDtypeStruct((units, DK, DV), F32)
    single = jax.ShapeDtypeStruct((blocks, DK, DV), F32)
    edge = jax.ShapeDtypeStruct((heads, DK, DV), F32)

    depth = (2 + 2 * heads) * TOK + ROWS
    assert doc_lengths.shape[0] <= 256
    docs = doc_lengths.reshape(1, -1)
    sources = (decay_logit.T, beta_logit.T, docs, queries, key_vectors, values, out_grad)
    sources = tuple(pltpu.with_memory_space_constraint(array, pltpu.HBM) for array in sources)
    packed = call(
        functools.partial(pack_kernel, peers, heads),
        jax.ShapeDtypeStruct((peers, depth, DK), BF16),
        sources,
        1,
        "pack",
        in_specs=[pl.BlockSpec(memory_space=pltpu.HBM)] * len(sources),
        scratch_shapes=[pltpu.VMEM(array.shape, array.dtype) for array in sources]
        + [pltpu.SemaphoreType.DMA((len(sources),))],
    )
    x = exchange(packed)
    local = call(
        functools.partial(blocks_kernel, heads, blocks),
        [square] * 6
        + [single] * 4
        + [square] * 2
        + [edge] * 4
        + [jax.ShapeDtypeStruct((L, L), F32), jax.ShapeDtypeStruct((ROWS, L), F32)],
        (x,),
        60 * units,
        "blocks",
    )
    t, w, u, y, m, decay, kk, qk, rk, rq, state_loc, back_loc = local[:12]
    end, begin, even, odd, cols, rows = local[12:]
    pre, post, fmap, rmap, front, last, total = call(
        functools.partial(maps_kernel, heads, blocks),
        [square] * 6 + [edge],
        (x, t, w, m, cols),
        12 * units,
        "maps",
    )
    fresh, dv = call(
        functools.partial(local_kernel, heads, blocks),
        [square] * 2,
        (x, t, w, cols, u, y, state_loc, back_loc),
        8 * units,
        "local_rows",
    )

    shards = lax.axis_size("ctx")
    turns = min(shards - 1, (shards + 1) // 2)
    if turns == 0:
        even, odd = jnp.zeros_like(even), jnp.zeros_like(odd)
    for step in range(turns):
        if step:
            even, odd = call(
                functools.partial(turn_kernel, heads),
                [edge] * 2,
                (total, end, begin, even, odd),
                6 * heads,
                "turn",
            )
        even, odd = over_edges(even, odd)

    shapes = [jax.ShapeDtypeStruct((peers, (heads + (0 if wide else 2)) * TOK + ROWS, DV), BF16)]
    if wide:
        shapes.append(jax.ShapeDtypeStruct((peers, 2 * TOK, DK), F32))
    grads = call(
        functools.partial(gradients_kernel, heads, blocks),
        shapes,
        (
            *(x, decay, kk, qk, rk, rq, rows, fresh, dv, state_loc, back_loc),
            *(pre, post, fmap, rmap, front, last, even, odd),
        ),
        50 * units,
        "gradients",
    )
    grads = [exchange(array) for array in grads]
    *wide_grads, grad_decay, grad_beta = call(
        functools.partial(unpack_kernel, peers, heads, wide),
        [
            jax.ShapeDtypeStruct((TOK, HK * DK), BF16),
            jax.ShapeDtypeStruct((TOK, HK * DK), BF16),
            jax.ShapeDtypeStruct((TOK, VALUE_HEADS * DV), BF16),
            jax.ShapeDtypeStruct((VALUE_HEADS, TOK), F32),
            jax.ShapeDtypeStruct((VALUE_HEADS, TOK), F32),
        ],
        grads,
        1,
        "unpack",
    )
    return (*wide_grads, grad_decay.T, grad_beta.T)


def solution(mesh):
    spec = P(("groups", "ctx", "head", "rep"), None)
    return jax.shard_map(
        body,
        mesh=mesh,
        in_specs=(spec,) * 6 + (P("groups"),),
        out_specs=(spec,) * 5,
        check_vma=False,
    )
```

```python
import functools

import jax
import jax.numpy as jnp
from jax import lax
from jax.experimental import pallas as pl
from jax.experimental.pallas import tpu as pltpu
from jax.sharding import PartitionSpec as P

VALUE_HEADS = 16
HK = 8
DK = 128
DV = 128
GROUP = VALUE_HEADS // HK
L = 128
ROWS = 16
TOK = 64
PER = L // TOK
EPS = 1e-06
F32 = jnp.float32
BF16 = jnp.bfloat16

NN = ((1,), (0,))
NT = ((1,), (1,))
TN = ((0,), (0,))


def split(x):
    if isinstance(x, tuple):
        return x
    if x.dtype == BF16:
        return (x,)
    high = x.astype(BF16)
    return (high, (x - high.astype(F32)).astype(BF16))


def mm(a, b, dims=NN):
    a, b = split(a), split(b)
    left_along, right_along = dims[0][0], dims[1][0]
    across = 1 - right_along
    size = b[0].shape[across]
    left = jnp.concatenate(a, axis=left_along) if len(a) > 1 else a[0]
    right = jnp.concatenate(b, axis=across) if len(b) > 1 else b[0]
    if len(a) > 1:
        below = [b[0], jnp.zeros_like(b[0])] if len(b) > 1 else [b[0]]
        below = jnp.concatenate(below, axis=across) if len(below) > 1 else below[0]
        right = jnp.concatenate([right, below], axis=right_along)
    out = lax.dot_general(left, right, (dims, ((), ())), preferred_element_type=F32)
    return out[:, :size] + out[:, size:] if len(b) > 1 else out


def side_by_side(parts):
    parts = list(parts)
    while parts:
        parts = [part for part in parts if next(part, parts) is not parts]


def iotas():
    rows = lax.broadcasted_iota(jnp.int32, (L, L), 0)
    columns = lax.broadcasted_iota(jnp.int32, (L, L), 1)
    return rows, columns


def unit_lower_inverse(lowers):
    rows, columns = iotas()
    eye = (rows == columns).astype(F32)
    near = rows // 16 == columns // 16
    firsts = [jnp.where(near, -a, 0.0) for a in lowers]
    sums = [eye + x for x in firsts]
    powers = [mm(x, x) for x in firsts]
    for _ in range(2):
        both = [mm(jnp.concatenate([x, s], axis=0), x) for x, s in zip(powers, sums)]
        powers = [x[:L] for x in both]
        sums = [s + x[L:] for s, x in zip(sums, both)]
    sums = [s + mm(s, x) for s, x in zip(sums, powers)]
    firsts = [mm(s, jnp.where(near, 0.0, -a)) for s, a in zip(sums, lowers)]
    powers = [mm(x, x) for x in firsts]
    both = [mm(jnp.concatenate([x, y], axis=0), x) for x, y in zip(powers, firsts)]
    fourths = [x[:L] for x in both]
    leads = [eye + y + x + b[L:] for y, x, b in zip(firsts, powers, both)]
    sums = [s + mm(x, s) for s, x in zip(sums, fourths)]
    return [mm(x, s) for x, s in zip(leads, sums)]


def doc_offsets(doc_ref):
    lengths = doc_ref[...]
    count = lengths.shape[1]
    rows = lax.broadcasted_iota(jnp.int32, (count, count), 0)
    columns = lax.broadcasted_iota(jnp.int32, (count, count), 1)
    return jnp.sum(jnp.where(columns < rows, lengths.astype(F32), 0.0), axis=1, keepdims=True)


def taken(ref, n, piece):
    here = slice(piece * TOK, (piece + 1) * TOK)
    return jnp.concatenate([ref[n * PER + i, here, :] for i in range(PER)], axis=0)


def column(cols, spot):
    return cols[:, spot : spot + 1]


def wide_column(cols, spot):
    return jnp.broadcast_to(column(cols, spot), (L, L))


def times_ones(rows_in, ones):
    parts, rest = [], rows_in
    for _ in range(3):
        part = rest.astype(BF16)
        parts.append(part.astype(F32))
        rest = rest - part.astype(F32)
    count = rows_in.shape[0]
    out = lax.dot_general(
        jnp.concatenate(parts, axis=0).astype(BF16),
        ones,
        (NN, ((), ())),
        preferred_element_type=F32,
    )
    return out[:count] + out[count : 2 * count] + out[2 * count :]


def pack_kernel(peers, heads, *refs):
    count = 7
    sources, out_ref = refs[:count], refs[count]
    buffers, done = refs[count + 1 : 2 * count + 1], refs[2 * count + 1]
    copies = [
        pltpu.make_async_copy(source, buffer, done.at[i])
        for i, (source, buffer) in enumerate(zip(sources, buffers))
    ]
    for copy in copies:
        copy.start()
    decay_ref, beta_ref, doc_ref, q_ref, k_ref, v_ref, g_ref = buffers
    for copy in copies[:3]:
        copy.wait()
    logits = jnp.concatenate(
        [decay_ref[...].astype(F32), beta_ref[...].astype(F32)], axis=1
    )
    off_col = doc_offsets(doc_ref)
    place = lax.axis_index("ctx") * lax.axis_size("head") + lax.axis_index("head")
    first = (place * lax.axis_size("rep") + lax.axis_index("rep")) * TOK
    lane = lax.broadcasted_iota(jnp.int32, (1, L), 1)
    position = jnp.where(lane < TOK, first + lane, first - 1).astype(F32)
    docs = jnp.sum((off_col <= position).astype(F32), axis=0, keepdims=True)
    spot = lax.broadcasted_iota(jnp.int32, (ROWS, L), 0)
    for j in range(peers):
        tile = jnp.where(spot == heads, docs, 0.0)
        for h in range(heads):
            tile = jnp.where(spot == h, logits[j * heads + h : j * heads + h + 1], tile)
        out_ref[j, (2 + 2 * heads) * TOK :, :] = tile.astype(BF16)
    for i, (ref, piece) in enumerate(((q_ref, 0), (k_ref, 1))):
        copies[3 + i].wait()
        for j in range(peers):
            key_head = j * heads // GROUP
            out_ref[j, piece * TOK : (piece + 1) * TOK, :] = ref[
                :, key_head * DK : (key_head + 1) * DK
            ]
    for i, (ref, piece) in enumerate(((v_ref, 2), (g_ref, 2 + heads))):
        copies[5 + i].wait()
        for j in range(peers):
            for h in range(heads):
                here = slice((piece + h) * TOK, (piece + h + 1) * TOK)
                lanes = slice((j * heads + h) * DV, (j * heads + h + 1) * DV)
                out_ref[j, here, :] = ref[:, lanes]


def to_neighbours(parity, even_ref, odd_ref, h, state, back):
    even = parity == 0
    even_ref[h] = jnp.where(even, state, back)
    odd_ref[h] = jnp.where(even, back, state)


def from_neighbours(parity, even_ref, odd_ref, h):
    even = parity == 0
    return jnp.where(even, odd_ref[h], even_ref[h]), jnp.where(even, even_ref[h], odd_ref[h])


def blocks_kernel(
    heads,
    blocks,
    x_ref,
    t_ref,
    w_ref,
    u_ref,
    y_ref,
    m_ref,
    decay_ref,
    kk_ref,
    qk_ref,
    rk_ref,
    rq_ref,
    state_ref,
    back_ref,
    end_ref,
    begin_ref,
    even_ref,
    odd_ref,
    cols_ref,
    rows_ref,
):
    rows, columns = iotas()
    eye = (rows == columns).astype(F32)
    shard = lax.axis_index("ctx")
    lane = lax.broadcasted_iota(jnp.int32, (1, L), 1)
    units = [(n, h) for n in range(blocks) for h in range(heads)]
    half = ROWS // 2
    unit_row = lax.broadcasted_iota(jnp.int32, (half, L), 0)

    def by_unit(row_of_block):
        out = jnp.zeros((half, L), F32)
        for n in range(blocks):
            out = jnp.where(unit_row // heads == n, row_of_block[n], out)
        return out

    keys, queries, grams, crosses, rk_rows, rq_rows = [], [], [], [], [], []
    for n in range(blocks):
        q, k = taken(x_ref, n, 0), taken(x_ref, n, 1)
        grams.append(mm(k, k, NT))
        crosses.append(mm(q, k, NT))
        for gram, out in ((grams[n], rk_rows), (mm(q, q, NT), rq_rows)):
            square = jnp.sum(jnp.where(rows == columns, gram, 0.0), axis=0, keepdims=True)
            out.append(lax.rsqrt(square + EPS))
        rq_rows[n] = rq_rows[n] * DK**-0.5
        keys.append(k)
        queries.append(q)
    decay_logits = jnp.zeros((half, L), F32)
    beta_logits = jnp.zeros((half, L), F32)
    doc_rows, befores = [], []
    for n in range(blocks):
        first, second = (
            x_ref[n * PER + i, (2 + 2 * heads) * TOK :, :].astype(F32) for i in range(PER)
        )
        left = jnp.where(lane < TOK, first, pltpu.roll(second, TOK, 1))
        right = jnp.where(lane < TOK, pltpu.roll(first, TOK, 1), second)
        for h in range(heads):
            here = unit_row == n * heads + h
            decay_logits = jnp.where(here, left[h : h + 1], decay_logits)
            beta_logits = jnp.where(here, right[h : h + 1], beta_logits)
        doc_rows.append(left[heads : heads + 1])
        befores.append(first[heads : heads + 1, TOK : TOK + 1])
    soft = jnp.maximum(decay_logits, 0.0) + jnp.log1p(jnp.exp(-jnp.abs(decay_logits)))
    beta_rows = 1.0 / (1.0 + jnp.exp(-beta_logits))
    sum_rows = times_ones(-soft, (rows <= columns).astype(BF16))
    rows_ref[...] = jnp.concatenate([1.0 / (1.0 + jnp.exp(-decay_logits)), beta_rows], axis=0)
    unit_docs = by_unit(doc_rows)
    front_rows = jnp.where(unit_docs == by_unit(befores), jnp.exp(sum_rows), 0.0)
    final = slice(L - 1, L)
    last_rows = jnp.where(
        unit_docs == unit_docs[:, final], jnp.exp(sum_rows[:, final] - sum_rows), 0.0
    )
    rk_units, rq_units = by_unit(rk_rows), by_unit(rq_rows)
    kinds = [
        sum_rows,
        beta_rows,
        front_rows,
        last_rows,
        last_rows * rk_units,
        rk_units,
        rq_units,
        unit_docs,
    ]
    cols = jnp.concatenate(kinds + [jnp.zeros((L - half * len(kinds), L), F32)], axis=0).T
    cols_ref[...] = cols
    write_rows = beta_rows * front_rows * rk_units
    read_rows = front_rows * rq_units
    lowers, decays = [], []
    for n in range(blocks):
        keep = (columns <= rows) & (column(cols, 7 * half + n * heads) == doc_rows[n])
        rk, rq = wide_column(cols, 5 * half + n * heads), wide_column(cols, 6 * half + n * heads)
        kk = jnp.where(columns < rows, grams[n] * rk * rk_rows[n], 0.0)
        rk_ref[n], rq_ref[n] = rk, rq
        kk_ref[n] = kk
        qk_ref[n] = crosses[n] * rq * rk_rows[n]
        for h in range(heads):
            u = n * heads + h
            spread = column(cols, u) - sum_rows[u : u + 1]
            decay = jnp.where(keep, jnp.exp(jnp.where(keep, spread, 0.0)), 0.0)
            decay_ref[u] = decay
            decays.append(decay)
            lowers.append(column(cols, half + u) * (decay * kk))
    inverses = unit_lower_inverse(lowers)
    moves, adds, backs = {}, {}, {}
    turned = [q.astype(F32).T for q in queries]

    def unit(n, h):
        k = keys[n]
        u = n * heads + h
        here = slice(u, u + 1)
        v, g = taken(x_ref, n, 2 + h), taken(x_ref, n, 2 + heads + h)
        t = inverses[u] * beta_rows[here]
        w = mm(inverses[u] * write_rows[here], k)
        value = mm(t, v)
        yield
        spread = mm(k, column(cols, 4 * half + u) * jnp.concatenate([w, value], axis=1), TN)
        yield
        move = front_rows[here, final] * eye - spread[:, :DK]
        y = mm(decays[u] * qk_ref[n], g, TN)
        back = mm(turned[n] * read_rows[here], g) - mm(w, y, TN)
        yield
        t_ref[u] = t
        w_ref[u] = w
        u_ref[u] = value
        y_ref[u] = y
        m_ref[u] = move
        moves[n, h], adds[n, h], backs[n, h] = split(move), spread[:, DK:], back

    side_by_side(unit(n, h) for n, h in units)
    ends, begins = [], []
    zero = jnp.zeros((DK, DV), F32)
    for h in range(heads):
        state_ref[h] = zero
        back_ref[(blocks - 1) * heads + h] = zero
        ends.append(adds[0, h])
        begins.append(backs[blocks - 1, h])
    for step in range(1, blocks):
        ahead, behind = step, blocks - 1 - step
        for h in range(heads):
            state_ref[ahead * heads + h] = ends[h]
            ends[h] = mm(moves[ahead, h], ends[h]) + adds[ahead, h]
            back_ref[behind * heads + h] = begins[h]
            begins[h] = mm(moves[behind, h], begins[h], TN) + backs[behind, h]
    for h in range(heads):
        end_ref[h] = ends[h]
        begin_ref[h] = begins[h]
        to_neighbours(shard % 2, even_ref, odd_ref, h, ends[h], begins[h])


def maps_kernel(
    heads,
    blocks,
    x_ref,
    t_ref,
    w_ref,
    m_ref,
    cols_ref,
    pre_ref,
    post_ref,
    fmap_ref,
    rmap_ref,
    front_ref,
    last_ref,
    total_ref,
):
    rows, columns = iotas()
    eye = (rows == columns).astype(F32)
    half = ROWS // 2
    cols = cols_ref[...]
    pres, posts = [eye] * heads, [eye] * heads
    for step in range(blocks):
        ahead, behind = step, blocks - 1 - step
        k = taken(x_ref, behind, 1)
        for h in range(heads):
            u = ahead * heads + h
            front_ref[u] = wide_column(cols, 2 * half + u)
            last_ref[u] = wide_column(cols, 3 * half + u)
            pre_ref[u] = pres[h]
            if step == 0:
                fmap_ref[u] = w_ref[u]
                pres[h] = m_ref[u]
            else:
                halves = split(pres[h])
                both = mm(jnp.concatenate([w_ref[u], m_ref[u]], axis=0), halves)
                fmap_ref[u] = both[:L]
                pres[h] = both[L:]
            u = behind * heads + h
            post_ref[u] = posts[h]
            if step == 0:
                spread = k.astype(F32)
                posts[h] = m_ref[u].T
            else:
                halves = split(posts[h])
                spread = mm(k, halves)
                if step < blocks - 1:
                    posts[h] = mm(m_ref[u], halves, TN)
            rmap_ref[u] = mm(t_ref[u], column(cols, 4 * half + u) * spread, TN)
    for h in range(heads):
        total_ref[h] = pres[h]


def local_kernel(
    heads,
    blocks,
    x_ref,
    t_ref,
    w_ref,
    cols_ref,
    u_ref,
    y_ref,
    state_ref,
    back_ref,
    fresh_ref,
    dv_ref,
):
    half = ROWS // 2
    cols = cols_ref[...]
    for n in range(blocks):
        k = taken(x_ref, n, 1)
        for h in range(heads):
            u = n * heads + h
            fresh_ref[u] = u_ref[u] - mm(w_ref[u], state_ref[u]) if n else u_ref[u]
            dfresh = y_ref[u]
            if n < blocks - 1:
                dfresh = dfresh + column(cols, 4 * half + u) * mm(k, back_ref[u])
            dv_ref[u] = mm(t_ref[u], dfresh, TN)


def turn_kernel(heads, total_ref, end_ref, begin_ref, even_in, odd_in, even_out, odd_out):
    parity = lax.axis_index("ctx") % 2
    for h in range(heads):
        total = split(total_ref[h])
        state, back = from_neighbours(parity, even_in, odd_in, h)
        state = mm(total, state) + end_ref[h]
        back = mm(total, back, TN) + begin_ref[h]
        to_neighbours(parity, even_out, odd_out, h, state, back)


def against(left, exact, right):
    left = split(left)
    exact = (exact, jnp.zeros_like(exact))
    both = tuple(jnp.concatenate(parts, axis=0) for parts in zip(left, exact))
    out = mm(both, right, NT)
    return out[:L], out[L:]


def gradients_kernel(
    heads,
    blocks,
    x_ref,
    decay_ref,
    kk_ref,
    qk_ref,
    rk_ref,
    rq_ref,
    rows_ref,
    fresh_ref,
    dv_ref,
    state_ref,
    back_ref,
    pre_ref,
    post_ref,
    fmap_ref,
    rmap_ref,
    front_ref,
    last_ref,
    even_ref,
    odd_ref,
    out_ref,
    *wide_refs,
):
    rows, columns = iotas()
    half = ROWS // 2
    small_row = lax.broadcasted_iota(jnp.int32, (half, L), 0)
    parity = lax.axis_index("ctx") % 2
    from_here = (rows >= columns).astype(BF16)
    wide = len(wide_refs) > 0
    at = 0 if wide else 2
    outside = [from_neighbours(parity, even_ref, odd_ref, h) for h in range(heads)]
    outside2 = [(split(enter), split(leave)) for enter, leave in outside]

    def block(n):
        kk, qk, rk, rq = kk_ref[n], qk_ref[n], rk_ref[n], rq_ref[n]
        q, k = taken(x_ref, n, 0), taken(x_ref, n, 1)
        kn, qn = rk * k.astype(F32), rq * q.astype(F32)
        dq = dk = bq_sum = b_sum = 0.0
        sums = jnp.zeros((L, L), F32)
        crossed = jnp.zeros((half, L), F32)
        tails = jnp.zeros((half, 1), F32)
        for h in range(heads):
            u = n * heads + h
            decay, front = decay_ref[u], front_ref[u]
            v = taken(x_ref, n, 2 + h).astype(F32)
            g = taken(x_ref, n, 2 + heads + h)
            enter2, leave2 = outside2[h]
            if n == 0:
                state, seen = outside[h][0], mm(fmap_ref[u], enter2)
            else:
                both = mm(jnp.concatenate([pre_ref[u], fmap_ref[u]], axis=0), enter2)
                state, seen = state_ref[u] + both[:L], both[L:]
            if n == blocks - 1:
                back, dv = outside[h][1], mm(rmap_ref[u], leave2)
            else:
                both = mm(jnp.concatenate([post_ref[u], rmap_ref[u]], axis=0), leave2)
                back, dv = back_ref[u] + both[:L], both[L:]
            yield
            fresh2 = split(fresh_ref[u] - seen)
            dv = dv_ref[u] + dv
            dv2, state2 = split(dv), split(state)
            for i in range(PER):
                out_ref[n * PER + i, (at + h) * TOK : (at + h + 1) * TOK, :] = dv2[0][
                    i * TOK : (i + 1) * TOK
                ]
            yield
            read = front * (rk * mm(k, state2))
            da, dp = against(dv2, g, fresh2)
            ds, gs = against(dv2, g, state2)
            yield
            b = jnp.where(columns < rows, da * decay, 0.0)
            bq = dp * decay
            scaled = b * kk
            z = bq * qk - scaled
            gs = front * gs
            outer = last_ref[u] * mm(fresh2, back, NT)
            kept = kn * outer
            yield
            by_sum = jnp.sum(qn * gs - dv * read - kept + z, axis=1, keepdims=True)
            by_beta = jnp.sum(dv * (v - read) - scaled, axis=1, keepdims=True)
            sums = jnp.where(columns == h, by_sum, sums)
            sums = jnp.where(columns == heads + h, by_beta, sums)
            crossed = jnp.where(small_row == h, jnp.sum(z, axis=0, keepdims=True), crossed)
            tail = jnp.sum(kept + front[L - 1 : L] * (state * back), axis=0, keepdims=True)
            tail = jnp.sum(tail, axis=1, keepdims=True)
            tails = jnp.where(small_row[:, :1] == h, tail, tails)
            yield
            b_sum = b_sum - b
            bq_sum = bq_sum + bq
            dq = dq + gs
            dk = dk + outer - front * ds
        yield
        turned = sums.T[:half]
        dsum = times_ones(turned - crossed, from_here) + tails
        small = turned
        for h in range(heads):
            u = n * heads + h
            sig, beta = rows_ref[u : u + 1], rows_ref[half + u : half + u + 1]
            small = jnp.where(small_row == h, -dsum * sig, small)
            small = jnp.where(small_row == heads + h, turned * (1.0 - beta), small)
        both = mm(jnp.concatenate([bq_sum, b_sum + b_sum.T], axis=0), kn)
        yield
        dq = dq + both[:L]
        dk = dk + both[L:] + mm(bq_sum, qn, TN)
        dq = rq * (dq - qn * (DK * jnp.sum(qn * dq, axis=1, keepdims=True)))
        dk = rk * (dk - kn * jnp.sum(kn * dk, axis=1, keepdims=True))
        yield
        high = small.astype(BF16).astype(F32)
        pair = jnp.concatenate([high, small - high], axis=0)
        for i in range(PER):
            here = slice(i * TOK, (i + 1) * TOK)
            if wide:
                wide_refs[0][n * PER + i, 0:TOK, :] = dq[here]
                wide_refs[0][n * PER + i, TOK : 2 * TOK, :] = dk[here]
            else:
                out_ref[n * PER + i, 0:TOK, :] = dq[here].astype(BF16)
                out_ref[n * PER + i, TOK : 2 * TOK, :] = dk[here].astype(BF16)
            moved = pair if i == 0 else pltpu.roll(pair, L - i * TOK, 1)
            out_ref[n * PER + i, (at + heads) * TOK :, :] = moved.astype(BF16)

    side_by_side(block(n) for n in range(blocks))


def unpack_kernel(peers, heads, wide, *refs):
    if wide:
        x_ref, wide_ref, *outs = refs
    else:
        x_ref, *outs = refs
        wide_ref = None
    dq_ref, dk_ref, dv_ref, decay_ref, beta_ref = outs
    at = 0 if wide else 2
    spots = lax.broadcasted_iota(jnp.int32, (ROWS, L), 0)
    decays, betas = jnp.zeros((ROWS, L), F32), jnp.zeros((ROWS, L), F32)
    for j in range(peers):
        for h in range(heads):
            lanes = slice((j * heads + h) * DV, (j * heads + h + 1) * DV)
            dv_ref[:, lanes] = x_ref[j, (at + h) * TOK : (at + h + 1) * TOK, :]
        pair = x_ref[j, (at + heads) * TOK :, :].astype(F32)
        small = pair[: ROWS // 2] + pair[ROWS // 2 :]
        for h in range(heads):
            decays = jnp.where(spots == j * heads + h, small[h : h + 1], decays)
            betas = jnp.where(spots == j * heads + h, small[heads + h : heads + h + 1], betas)
    for i in range(HK):
        lanes = slice(i * DK, (i + 1) * DK)
        if wide:
            some = [wide_ref[i * GROUP + m] for m in range(GROUP)]
            total = some[0]
            for other in some[1:]:
                total = total + other
            total = total.astype(BF16)
            dq_ref[:, lanes] = total[:TOK]
            dk_ref[:, lanes] = total[TOK:]
        else:
            dq_ref[:, lanes] = x_ref[i, 0:TOK, :]
            dk_ref[:, lanes] = x_ref[i, TOK : 2 * TOK, :]
    decay_ref[...] = decays[:, :TOK]
    beta_ref[...] = betas[:, :TOK]


def over_edges(even, odd):
    size = lax.axis_size("ctx")
    results = []
    for first, value in ((0, even), (1, odd)):
        pairs = []
        for i in range(first, size - 1, 2):
            pairs += [(i, i + 1), (i + 1, i)]
        results.append(lax.ppermute(value, "ctx", pairs) if pairs else jnp.zeros_like(value))
    return results


def work(passes):
    return pl.CostEstimate(
        flops=2 * L * DK * DV * passes, bytes_accessed=1 << 20, transcendentals=0
    )


PARAMS = pltpu.CompilerParams(vmem_limit_bytes=16 << 20)


def body(queries, key_vectors, values, out_grad, decay_logit, beta_logit, doc_lengths):
    assert queries.shape[0] == TOK
    peers = lax.axis_size("head") * lax.axis_size("rep")
    heads = VALUE_HEADS // peers
    wide = heads % GROUP != 0
    blocks = TOK * peers // L
    units = blocks * heads
    assert heads == (1 if wide else GROUP) and units <= ROWS // 2

    def exchange(array):
        return lax.all_to_all(array, ("head", "rep"), split_axis=0, concat_axis=0, tiled=True)

    def call(kernel, shapes, inputs, passes, name, params=PARAMS, **rest):
        return pl.pallas_call(
            kernel,
            out_shape=shapes,
            compiler_params=params,
            cost_estimate=work(passes),
            name=name,
            **rest,
        )(*inputs)

    square = jax.ShapeDtypeStruct((units, DK, DV), F32)
    single = jax.ShapeDtypeStruct((blocks, DK, DV), F32)
    edge = jax.ShapeDtypeStruct((heads, DK, DV), F32)

    depth = (2 + 2 * heads) * TOK + ROWS
    assert doc_lengths.shape[0] <= 256
    docs = doc_lengths.reshape(1, -1)
    sources = (decay_logit.T, beta_logit.T, docs, queries, key_vectors, values, out_grad)
    sources = tuple(pltpu.with_memory_space_constraint(array, pltpu.HBM) for array in sources)
    packed = call(
        functools.partial(pack_kernel, peers, heads),
        jax.ShapeDtypeStruct((peers, depth, DK), BF16),
        sources,
        1,
        "pack",
        in_specs=[pl.BlockSpec(memory_space=pltpu.HBM)] * len(sources),
        scratch_shapes=[pltpu.VMEM(array.shape, array.dtype) for array in sources]
        + [pltpu.SemaphoreType.DMA((len(sources),))],
    )
    x = exchange(packed)
    local = call(
        functools.partial(blocks_kernel, heads, blocks),
        [square] * 6
        + [single] * 4
        + [square] * 2
        + [edge] * 4
        + [jax.ShapeDtypeStruct((L, L), F32), jax.ShapeDtypeStruct((ROWS, L), F32)],
        (x,),
        60 * units,
        "blocks",
    )
    t, w, u, y, m, decay, kk, qk, rk, rq, state_loc, back_loc = local[:12]
    end, begin, even, odd, cols, rows = local[12:]
    pre, post, fmap, rmap, front, last, total = call(
        functools.partial(maps_kernel, heads, blocks),
        [square] * 6 + [edge],
        (x, t, w, m, cols),
        12 * units,
        "maps",
    )
    fresh, dv = call(
        functools.partial(local_kernel, heads, blocks),
        [square] * 2,
        (x, t, w, cols, u, y, state_loc, back_loc),
        8 * units,
        "local_rows",
    )

    shards = lax.axis_size("ctx")
    turns = min(shards - 1, (shards + 1) // 2)
    if turns == 0:
        even, odd = jnp.zeros_like(even), jnp.zeros_like(odd)
    for step in range(turns):
        if step:
            even, odd = call(
                functools.partial(turn_kernel, heads),
                [edge] * 2,
                (total, end, begin, even, odd),
                6 * heads,
                "turn",
            )
        even, odd = over_edges(even, odd)

    shapes = [jax.ShapeDtypeStruct((peers, (heads + (0 if wide else 2)) * TOK + ROWS, DV), BF16)]
    if wide:
        shapes.append(jax.ShapeDtypeStruct((peers, 2 * TOK, DK), F32))
    grads = call(
        functools.partial(gradients_kernel, heads, blocks),
        shapes,
        (
            *(x, decay, kk, qk, rk, rq, rows, fresh, dv, state_loc, back_loc),
            *(pre, post, fmap, rmap, front, last, even, odd),
        ),
        50 * units,
        "gradients",
    )
    grads = [exchange(array) for array in grads]
    *wide_grads, grad_decay, grad_beta = call(
        functools.partial(unpack_kernel, peers, heads, wide),
        [
            jax.ShapeDtypeStruct((TOK, HK * DK), BF16),
            jax.ShapeDtypeStruct((TOK, HK * DK), BF16),
            jax.ShapeDtypeStruct((TOK, VALUE_HEADS * DV), BF16),
            jax.ShapeDtypeStruct((VALUE_HEADS, TOK), F32),
            jax.ShapeDtypeStruct((VALUE_HEADS, TOK), F32),
        ],
        grads,
        1,
        "unpack",
    )
    return (*wide_grads, grad_decay.T, grad_beta.T)


def solution(mesh):
    spec = P(("groups", "ctx", "head", "rep"), None)
    return jax.shard_map(
        body,
        mesh=mesh,
        in_specs=(spec,) * 6 + (P("groups"),),
        out_specs=(spec,) * 5,
        check_vma=False,
    )
```

```python
import functools

import jax
import jax.numpy as jnp
from jax import lax
from jax.experimental import pallas as pl
from jax.experimental.pallas import tpu as pltpu
from jax.sharding import PartitionSpec as P

VALUE_HEADS = 16
HK = 8
DK = 128
DV = 128
GROUP = VALUE_HEADS // HK
L = 128
ROWS = 16
TOK = 64
PER = L // TOK
EPS = 1e-06
F32 = jnp.float32
BF16 = jnp.bfloat16

NN = ((1,), (0,))
NT = ((1,), (1,))
TN = ((0,), (0,))


def split(x):
    if isinstance(x, tuple):
        return x
    if x.dtype == BF16:
        return (x,)
    high = x.astype(BF16)
    return (high, (x - high.astype(F32)).astype(BF16))


def mm(a, b, dims=NN):
    a, b = split(a), split(b)
    left_along, right_along = dims[0][0], dims[1][0]
    across = 1 - right_along
    size = b[0].shape[across]
    left = jnp.concatenate(a, axis=left_along) if len(a) > 1 else a[0]
    right = jnp.concatenate(b, axis=across) if len(b) > 1 else b[0]
    if len(a) > 1:
        below = [b[0], jnp.zeros_like(b[0])] if len(b) > 1 else [b[0]]
        below = jnp.concatenate(below, axis=across) if len(below) > 1 else below[0]
        right = jnp.concatenate([right, below], axis=right_along)
    out = lax.dot_general(left, right, (dims, ((), ())), preferred_element_type=F32)
    return out[:, :size] + out[:, size:] if len(b) > 1 else out


def side_by_side(parts):
    parts = list(parts)
    while parts:
        parts = [part for part in parts if next(part, parts) is not parts]


def iotas():
    rows = lax.broadcasted_iota(jnp.int32, (L, L), 0)
    columns = lax.broadcasted_iota(jnp.int32, (L, L), 1)
    return rows, columns


def unit_lower_inverse(lowers):
    rows, columns = iotas()
    eye = (rows == columns).astype(F32)
    near = rows // 16 == columns // 16
    firsts = [jnp.where(near, -a, 0.0) for a in lowers]
    sums = [eye + x for x in firsts]
    powers = [mm(x, x) for x in firsts]
    for _ in range(2):
        both = [mm(jnp.concatenate([x, s], axis=0), x) for x, s in zip(powers, sums)]
        powers = [x[:L] for x in both]
        sums = [s + x[L:] for s, x in zip(sums, both)]
    sums = [s + mm(s, x) for s, x in zip(sums, powers)]
    firsts = [mm(s, jnp.where(near, 0.0, -a)) for s, a in zip(sums, lowers)]
    powers = [mm(x, x) for x in firsts]
    both = [mm(jnp.concatenate([x, y], axis=0), x) for x, y in zip(powers, firsts)]
    fourths = [x[:L] for x in both]
    leads = [eye + y + x + b[L:] for y, x, b in zip(firsts, powers, both)]
    sums = [s + mm(x, s) for s, x in zip(sums, fourths)]
    return [mm(x, s) for x, s in zip(leads, sums)]


def doc_offsets(doc_ref):
    lengths = doc_ref[...]
    count = lengths.shape[1]
    rows = lax.broadcasted_iota(jnp.int32, (count, count), 0)
    columns = lax.broadcasted_iota(jnp.int32, (count, count), 1)
    return jnp.sum(jnp.where(columns < rows, lengths.astype(F32), 0.0), axis=1, keepdims=True)


def taken(ref, n, piece):
    here = slice(piece * TOK, (piece + 1) * TOK)
    return jnp.concatenate([ref[n * PER + i, here, :] for i in range(PER)], axis=0)


def column(cols, spot):
    return cols[:, spot : spot + 1]


def wide_column(cols, spot):
    return jnp.broadcast_to(column(cols, spot), (L, L))


def times_ones(rows_in, ones):
    parts, rest = [], rows_in
    for _ in range(3):
        part = rest.astype(BF16)
        parts.append(part.astype(F32))
        rest = rest - part.astype(F32)
    count = rows_in.shape[0]
    out = lax.dot_general(
        jnp.concatenate(parts, axis=0).astype(BF16),
        ones,
        (NN, ((), ())),
        preferred_element_type=F32,
    )
    return out[:count] + out[count : 2 * count] + out[2 * count :]


def pack_kernel(peers, heads, *refs):
    count = 7
    sources, out_ref = refs[:count], refs[count]
    buffers, done = refs[count + 1 : 2 * count + 1], refs[2 * count + 1]
    copies = [
        pltpu.make_async_copy(source, buffer, done.at[i])
        for i, (source, buffer) in enumerate(zip(sources, buffers))
    ]
    for copy in copies:
        copy.start()
    decay_ref, beta_ref, doc_ref, q_ref, k_ref, v_ref, g_ref = buffers
    for copy in copies[:3]:
        copy.wait()
    logits = jnp.concatenate(
        [decay_ref[...].astype(F32), beta_ref[...].astype(F32)], axis=1
    )
    off_col = doc_offsets(doc_ref)
    place = lax.axis_index("ctx") * lax.axis_size("head") + lax.axis_index("head")
    first = (place * lax.axis_size("rep") + lax.axis_index("rep")) * TOK
    lane = lax.broadcasted_iota(jnp.int32, (1, L), 1)
    position = jnp.where(lane < TOK, first + lane, first - 1).astype(F32)
    docs = jnp.sum((off_col <= position).astype(F32), axis=0, keepdims=True)
    spot = lax.broadcasted_iota(jnp.int32, (ROWS, L), 0)
    for j in range(peers):
        tile = jnp.where(spot == heads, docs, 0.0)
        for h in range(heads):
            tile = jnp.where(spot == h, logits[j * heads + h : j * heads + h + 1], tile)
        out_ref[j, (2 + 2 * heads) * TOK :, :] = tile.astype(BF16)
    for i, (ref, piece) in enumerate(((q_ref, 0), (k_ref, 1))):
        copies[3 + i].wait()
        for j in range(peers):
            key_head = j * heads // GROUP
            out_ref[j, piece * TOK : (piece + 1) * TOK, :] = ref[
                :, key_head * DK : (key_head + 1) * DK
            ]
    for i, (ref, piece) in enumerate(((v_ref, 2), (g_ref, 2 + heads))):
        copies[5 + i].wait()
        for j in range(peers):
            for h in range(heads):
                here = slice((piece + h) * TOK, (piece + h + 1) * TOK)
                lanes = slice((j * heads + h) * DV, (j * heads + h + 1) * DV)
                out_ref[j, here, :] = ref[:, lanes]


def to_neighbours(parity, even_ref, odd_ref, h, state, back):
    even = parity == 0
    even_ref[h] = jnp.where(even, state, back)
    odd_ref[h] = jnp.where(even, back, state)


def from_neighbours(parity, even_ref, odd_ref, h):
    even = parity == 0
    return jnp.where(even, odd_ref[h], even_ref[h]), jnp.where(even, even_ref[h], odd_ref[h])


def blocks_kernel(
    heads,
    blocks,
    x_ref,
    t_ref,
    w_ref,
    u_ref,
    y_ref,
    m_ref,
    decay_ref,
    kk_ref,
    qk_ref,
    rk_ref,
    rq_ref,
    state_ref,
    back_ref,
    end_ref,
    begin_ref,
    even_ref,
    odd_ref,
    cols_ref,
    rows_ref,
):
    rows, columns = iotas()
    eye = (rows == columns).astype(F32)
    shard = lax.axis_index("ctx")
    lane = lax.broadcasted_iota(jnp.int32, (1, L), 1)
    units = [(n, h) for n in range(blocks) for h in range(heads)]
    half = ROWS // 2
    unit_row = lax.broadcasted_iota(jnp.int32, (half, L), 0)

    def by_unit(row_of_block):
        out = jnp.zeros((half, L), F32)
        for n in range(blocks):
            out = jnp.where(unit_row // heads == n, row_of_block[n], out)
        return out

    keys, queries, rk_rows, rq_rows = [], [], [], []
    for n in range(blocks):
        queries.append(taken(x_ref, n, 0))
        keys.append(taken(x_ref, n, 1))
    grams = [mm(k, k, NT) for k in keys]
    squares = [mm(q, q, NT) for q in queries]
    crosses = [mm(q, k, NT) for q, k in zip(queries, keys)]
    for gram, out in [(x, rk_rows) for x in grams] + [(x, rq_rows) for x in squares]:
        square = jnp.sum(jnp.where(rows == columns, gram, 0.0), axis=0, keepdims=True)
        out.append(lax.rsqrt(square + EPS))
    rq_rows = [row * DK**-0.5 for row in rq_rows]
    decay_logits = jnp.zeros((half, L), F32)
    beta_logits = jnp.zeros((half, L), F32)
    doc_rows, befores = [], []
    for n in range(blocks):
        first, second = (
            x_ref[n * PER + i, (2 + 2 * heads) * TOK :, :].astype(F32) for i in range(PER)
        )
        left = jnp.where(lane < TOK, first, pltpu.roll(second, TOK, 1))
        right = jnp.where(lane < TOK, pltpu.roll(first, TOK, 1), second)
        for h in range(heads):
            here = unit_row == n * heads + h
            decay_logits = jnp.where(here, left[h : h + 1], decay_logits)
            beta_logits = jnp.where(here, right[h : h + 1], beta_logits)
        doc_rows.append(left[heads : heads + 1])
        befores.append(first[heads : heads + 1, TOK : TOK + 1])
    soft = jnp.maximum(decay_logits, 0.0) + jnp.log1p(jnp.exp(-jnp.abs(decay_logits)))
    beta_rows = 1.0 / (1.0 + jnp.exp(-beta_logits))
    sum_rows = times_ones(-soft, (rows <= columns).astype(BF16))
    rows_ref[...] = jnp.concatenate([1.0 / (1.0 + jnp.exp(-decay_logits)), beta_rows], axis=0)
    unit_docs = by_unit(doc_rows)
    front_rows = jnp.where(unit_docs == by_unit(befores), jnp.exp(sum_rows), 0.0)
    final = slice(L - 1, L)
    last_rows = jnp.where(
        unit_docs == unit_docs[:, final], jnp.exp(sum_rows[:, final] - sum_rows), 0.0
    )
    rk_units, rq_units = by_unit(rk_rows), by_unit(rq_rows)
    kinds = [
        sum_rows,
        beta_rows,
        front_rows,
        last_rows,
        last_rows * rk_units,
        rk_units,
        rq_units,
        unit_docs,
    ]
    cols = jnp.concatenate(kinds + [jnp.zeros((L - half * len(kinds), L), F32)], axis=0).T
    cols_ref[...] = cols
    write_rows = beta_rows * front_rows * rk_units
    read_rows = front_rows * rq_units
    decays, spreads, keeps, kks = [], [], [], []
    for n in range(blocks):
        keep = (columns <= rows) & (column(cols, 7 * half + n * heads) == doc_rows[n])
        rk, rq = wide_column(cols, 5 * half + n * heads), wide_column(cols, 6 * half + n * heads)
        kk = jnp.where(columns < rows, grams[n] * rk * rk_rows[n], 0.0)
        rk_ref[n], rq_ref[n] = rk, rq
        kk_ref[n] = kk
        keeps.append(keep)
        kks.append(kk)
        qk_ref[n] = crosses[n] * rq * rk_rows[n]
        for h in range(heads):
            u = n * heads + h
            spreads.append(column(cols, u) - sum_rows[u : u + 1])
    for n, h in units:
        u = n * heads + h
        decay = jnp.where(keeps[n], jnp.exp(jnp.where(keeps[n], spreads[u], 0.0)), 0.0)
        decay_ref[u] = decay
        decays.append(decay)
    lowers = [
        column(cols, half + n * heads + h) * (decays[n * heads + h] * kks[n]) for n, h in units
    ]
    inverses = unit_lower_inverse(lowers)
    moves, adds, backs = {}, {}, {}
    turned = [q.astype(F32).T for q in queries]

    def unit(n, h):
        k = keys[n]
        u = n * heads + h
        here = slice(u, u + 1)
        v, g = taken(x_ref, n, 2 + h), taken(x_ref, n, 2 + heads + h)
        t = inverses[u] * beta_rows[here]
        w = mm(inverses[u] * write_rows[here], k)
        value = mm(t, v)
        yield
        spread = mm(k, column(cols, 4 * half + u) * jnp.concatenate([w, value], axis=1), TN)
        yield
        move = front_rows[here, final] * eye - spread[:, :DK]
        y = mm(decays[u] * qk_ref[n], g, TN)
        back = mm(turned[n] * read_rows[here], g) - mm(w, y, TN)
        yield
        t_ref[u] = t
        w_ref[u] = w
        u_ref[u] = value
        y_ref[u] = y
        m_ref[u] = move
        moves[n, h], adds[n, h], backs[n, h] = split(move), spread[:, DK:], back

    side_by_side(unit(n, h) for n, h in units)
    ends, begins = [], []
    zero = jnp.zeros((DK, DV), F32)
    for h in range(heads):
        state_ref[h] = zero
        back_ref[(blocks - 1) * heads + h] = zero
        ends.append(adds[0, h])
        begins.append(backs[blocks - 1, h])
    for step in range(1, blocks):
        ahead, behind = step, blocks - 1 - step
        for h in range(heads):
            state_ref[ahead * heads + h] = ends[h]
            ends[h] = mm(moves[ahead, h], ends[h]) + adds[ahead, h]
            back_ref[behind * heads + h] = begins[h]
            begins[h] = mm(moves[behind, h], begins[h], TN) + backs[behind, h]
    for h in range(heads):
        end_ref[h] = ends[h]
        begin_ref[h] = begins[h]
        to_neighbours(shard % 2, even_ref, odd_ref, h, ends[h], begins[h])


def maps_kernel(
    heads,
    blocks,
    x_ref,
    t_ref,
    w_ref,
    m_ref,
    cols_ref,
    pre_ref,
    post_ref,
    fmap_ref,
    rmap_ref,
    front_ref,
    last_ref,
    total_ref,
):
    rows, columns = iotas()
    eye = (rows == columns).astype(F32)
    half = ROWS // 2
    cols = cols_ref[...]
    pres, posts = [eye] * heads, [eye] * heads
    for step in range(blocks):
        ahead, behind = step, blocks - 1 - step
        k = taken(x_ref, behind, 1)
        for h in range(heads):
            u = ahead * heads + h
            front_ref[u] = wide_column(cols, 2 * half + u)
            last_ref[u] = wide_column(cols, 3 * half + u)
            pre_ref[u] = pres[h]
            if step == 0:
                fmap_ref[u] = w_ref[u]
                pres[h] = m_ref[u]
            else:
                halves = split(pres[h])
                both = mm(jnp.concatenate([w_ref[u], m_ref[u]], axis=0), halves)
                fmap_ref[u] = both[:L]
                pres[h] = both[L:]
            u = behind * heads + h
            post_ref[u] = posts[h]
            if step == 0:
                spread = k.astype(F32)
                posts[h] = m_ref[u].T
            else:
                halves = split(posts[h])
                spread = mm(k, halves)
                if step < blocks - 1:
                    posts[h] = mm(m_ref[u], halves, TN)
            rmap_ref[u] = mm(t_ref[u], column(cols, 4 * half + u) * spread, TN)
    for h in range(heads):
        total_ref[h] = pres[h]


def local_kernel(
    heads,
    blocks,
    x_ref,
    t_ref,
    w_ref,
    cols_ref,
    u_ref,
    y_ref,
    state_ref,
    back_ref,
    fresh_ref,
    dv_ref,
):
    half = ROWS // 2
    cols = cols_ref[...]
    for n in range(blocks):
        k = taken(x_ref, n, 1)
        for h in range(heads):
            u = n * heads + h
            fresh_ref[u] = u_ref[u] - mm(w_ref[u], state_ref[u]) if n else u_ref[u]
            dfresh = y_ref[u]
            if n < blocks - 1:
                dfresh = dfresh + column(cols, 4 * half + u) * mm(k, back_ref[u])
            dv_ref[u] = mm(t_ref[u], dfresh, TN)


def turn_kernel(heads, total_ref, end_ref, begin_ref, even_in, odd_in, even_out, odd_out):
    parity = lax.axis_index("ctx") % 2
    for h in range(heads):
        total = split(total_ref[h])
        state, back = from_neighbours(parity, even_in, odd_in, h)
        state = mm(total, state) + end_ref[h]
        back = mm(total, back, TN) + begin_ref[h]
        to_neighbours(parity, even_out, odd_out, h, state, back)


def against(left, exact, right):
    left = split(left)
    exact = (exact, jnp.zeros_like(exact))
    both = tuple(jnp.concatenate(parts, axis=0) for parts in zip(left, exact))
    out = mm(both, right, NT)
    return out[:L], out[L:]


def gradients_kernel(
    heads,
    blocks,
    x_ref,
    decay_ref,
    kk_ref,
    qk_ref,
    rk_ref,
    rq_ref,
    rows_ref,
    fresh_ref,
    dv_ref,
    state_ref,
    back_ref,
    pre_ref,
    post_ref,
    fmap_ref,
    rmap_ref,
    front_ref,
    last_ref,
    even_ref,
    odd_ref,
    out_ref,
    *wide_refs,
):
    rows, columns = iotas()
    half = ROWS // 2
    small_row = lax.broadcasted_iota(jnp.int32, (half, L), 0)
    parity = lax.axis_index("ctx") % 2
    from_here = (rows >= columns).astype(BF16)
    wide = len(wide_refs) > 0
    at = 0 if wide else 2
    outside = [from_neighbours(parity, even_ref, odd_ref, h) for h in range(heads)]
    outside2 = [(split(enter), split(leave)) for enter, leave in outside]

    def block(n):
        kk, qk, rk, rq = kk_ref[n], qk_ref[n], rk_ref[n], rq_ref[n]
        q, k = taken(x_ref, n, 0), taken(x_ref, n, 1)
        kn, qn = rk * k.astype(F32), rq * q.astype(F32)
        dq = dk = bq_sum = b_sum = 0.0
        sums = jnp.zeros((L, L), F32)
        crossed = jnp.zeros((half, L), F32)
        tails = jnp.zeros((half, 1), F32)
        for h in range(heads):
            u = n * heads + h
            decay, front = decay_ref[u], front_ref[u]
            v = taken(x_ref, n, 2 + h).astype(F32)
            g = taken(x_ref, n, 2 + heads + h)
            enter2, leave2 = outside2[h]
            if n == 0:
                state, seen = outside[h][0], mm(fmap_ref[u], enter2)
            else:
                both = mm(jnp.concatenate([pre_ref[u], fmap_ref[u]], axis=0), enter2)
                state, seen = state_ref[u] + both[:L], both[L:]
            if n == blocks - 1:
                back, dv = outside[h][1], mm(rmap_ref[u], leave2)
            else:
                both = mm(jnp.concatenate([post_ref[u], rmap_ref[u]], axis=0), leave2)
                back, dv = back_ref[u] + both[:L], both[L:]
            yield
            fresh2 = split(fresh_ref[u] - seen)
            dv = dv_ref[u] + dv
            yield
            dv2, state2 = split(dv), split(state)
            for i in range(PER):
                out_ref[n * PER + i, (at + h) * TOK : (at + h + 1) * TOK, :] = dv2[0][
                    i * TOK : (i + 1) * TOK
                ]
            yield
            read = front * (rk * mm(k, state2))
            da, dp = against(dv2, g, fresh2)
            yield
            ds, gs = against(dv2, g, state2)
            yield
            b = jnp.where(columns < rows, da * decay, 0.0)
            bq = dp * decay
            scaled = b * kk
            z = bq * qk - scaled
            gs = front * gs
            yield
            outer = last_ref[u] * mm(fresh2, back, NT)
            kept = kn * outer
            yield
            by_sum = jnp.sum(qn * gs - dv * read - kept + z, axis=1, keepdims=True)
            by_beta = jnp.sum(dv * (v - read) - scaled, axis=1, keepdims=True)
            sums = jnp.where(columns == h, by_sum, sums)
            sums = jnp.where(columns == heads + h, by_beta, sums)
            crossed = jnp.where(small_row == h, jnp.sum(z, axis=0, keepdims=True), crossed)
            tail = jnp.sum(kept + front[L - 1 : L] * (state * back), axis=0, keepdims=True)
            tail = jnp.sum(tail, axis=1, keepdims=True)
            tails = jnp.where(small_row[:, :1] == h, tail, tails)
            yield
            b_sum = b_sum - b
            bq_sum = bq_sum + bq
            dq = dq + gs
            dk = dk + outer - front * ds
        yield
        turned = sums.T[:half]
        dsum = times_ones(turned - crossed, from_here) + tails
        small = turned
        for h in range(heads):
            u = n * heads + h
            sig, beta = rows_ref[u : u + 1], rows_ref[half + u : half + u + 1]
            small = jnp.where(small_row == h, -dsum * sig, small)
            small = jnp.where(small_row == heads + h, turned * (1.0 - beta), small)
        both = mm(jnp.concatenate([bq_sum, b_sum + b_sum.T], axis=0), kn)
        yield
        dq = dq + both[:L]
        dk = dk + both[L:] + mm(bq_sum, qn, TN)
        dq = rq * (dq - qn * (DK * jnp.sum(qn * dq, axis=1, keepdims=True)))
        dk = rk * (dk - kn * jnp.sum(kn * dk, axis=1, keepdims=True))
        yield
        high = small.astype(BF16).astype(F32)
        pair = jnp.concatenate([high, small - high], axis=0)
        for i in range(PER):
            here = slice(i * TOK, (i + 1) * TOK)
            if wide:
                wide_refs[0][n * PER + i, 0:TOK, :] = dq[here]
                wide_refs[0][n * PER + i, TOK : 2 * TOK, :] = dk[here]
            else:
                out_ref[n * PER + i, 0:TOK, :] = dq[here].astype(BF16)
                out_ref[n * PER + i, TOK : 2 * TOK, :] = dk[here].astype(BF16)
            moved = pair if i == 0 else pltpu.roll(pair, L - i * TOK, 1)
            out_ref[n * PER + i, (at + heads) * TOK :, :] = moved.astype(BF16)

    side_by_side(block(n) for n in range(blocks))


def unpack_kernel(peers, heads, wide, *refs):
    if wide:
        x_ref, wide_ref, *outs = refs
    else:
        x_ref, *outs = refs
        wide_ref = None
    dq_ref, dk_ref, dv_ref, decay_ref, beta_ref = outs
    at = 0 if wide else 2
    spots = lax.broadcasted_iota(jnp.int32, (ROWS, L), 0)
    decays, betas = jnp.zeros((ROWS, L), F32), jnp.zeros((ROWS, L), F32)
    for j in range(peers):
        for h in range(heads):
            lanes = slice((j * heads + h) * DV, (j * heads + h + 1) * DV)
            dv_ref[:, lanes] = x_ref[j, (at + h) * TOK : (at + h + 1) * TOK, :]
        pair = x_ref[j, (at + heads) * TOK :, :].astype(F32)
        small = pair[: ROWS // 2] + pair[ROWS // 2 :]
        for h in range(heads):
            decays = jnp.where(spots == j * heads + h, small[h : h + 1], decays)
            betas = jnp.where(spots == j * heads + h, small[heads + h : heads + h + 1], betas)
    for i in range(HK):
        lanes = slice(i * DK, (i + 1) * DK)
        if wide:
            some = [wide_ref[i * GROUP + m] for m in range(GROUP)]
            total = some[0]
            for other in some[1:]:
                total = total + other
            total = total.astype(BF16)
            dq_ref[:, lanes] = total[:TOK]
            dk_ref[:, lanes] = total[TOK:]
        else:
            dq_ref[:, lanes] = x_ref[i, 0:TOK, :]
            dk_ref[:, lanes] = x_ref[i, TOK : 2 * TOK, :]
    decay_ref[...] = decays[:, :TOK]
    beta_ref[...] = betas[:, :TOK]


def over_edges(even, odd):
    size = lax.axis_size("ctx")
    results = []
    for first, value in ((0, even), (1, odd)):
        pairs = []
        for i in range(first, size - 1, 2):
            pairs += [(i, i + 1), (i + 1, i)]
        results.append(lax.ppermute(value, "ctx", pairs) if pairs else jnp.zeros_like(value))
    return results


def work(passes):
    return pl.CostEstimate(
        flops=2 * L * DK * DV * passes, bytes_accessed=1 << 20, transcendentals=0
    )


PARAMS = pltpu.CompilerParams(vmem_limit_bytes=16 << 20)


def body(queries, key_vectors, values, out_grad, decay_logit, beta_logit, doc_lengths):
    assert queries.shape[0] == TOK
    peers = lax.axis_size("head") * lax.axis_size("rep")
    heads = VALUE_HEADS // peers
    wide = heads % GROUP != 0
    blocks = TOK * peers // L
    units = blocks * heads
    assert heads == (1 if wide else GROUP) and units <= ROWS // 2

    def exchange(array):
        return lax.all_to_all(array, ("head", "rep"), split_axis=0, concat_axis=0, tiled=True)

    def call(kernel, shapes, inputs, passes, name, params=PARAMS, **rest):
        return pl.pallas_call(
            kernel,
            out_shape=shapes,
            compiler_params=params,
            cost_estimate=work(passes),
            name=name,
            **rest,
        )(*inputs)

    square = jax.ShapeDtypeStruct((units, DK, DV), F32)
    single = jax.ShapeDtypeStruct((blocks, DK, DV), F32)
    edge = jax.ShapeDtypeStruct((heads, DK, DV), F32)

    depth = (2 + 2 * heads) * TOK + ROWS
    assert doc_lengths.shape[0] <= 256
    docs = doc_lengths.reshape(1, -1)
    sources = (decay_logit.T, beta_logit.T, docs, queries, key_vectors, values, out_grad)
    sources = tuple(pltpu.with_memory_space_constraint(array, pltpu.HBM) for array in sources)
    packed = call(
        functools.partial(pack_kernel, peers, heads),
        jax.ShapeDtypeStruct((peers, depth, DK), BF16),
        sources,
        1,
        "pack",
        in_specs=[pl.BlockSpec(memory_space=pltpu.HBM)] * len(sources),
        scratch_shapes=[pltpu.VMEM(array.shape, array.dtype) for array in sources]
        + [pltpu.SemaphoreType.DMA((len(sources),))],
    )
    x = exchange(packed)
    local = call(
        functools.partial(blocks_kernel, heads, blocks),
        [square] * 6
        + [single] * 4
        + [square] * 2
        + [edge] * 4
        + [jax.ShapeDtypeStruct((L, L), F32), jax.ShapeDtypeStruct((ROWS, L), F32)],
        (x,),
        60 * units,
        "blocks",
    )
    t, w, u, y, m, decay, kk, qk, rk, rq, state_loc, back_loc = local[:12]
    end, begin, even, odd, cols, rows = local[12:]
    pre, post, fmap, rmap, front, last, total = call(
        functools.partial(maps_kernel, heads, blocks),
        [square] * 6 + [edge],
        (x, t, w, m, cols),
        12 * units,
        "maps",
    )
    fresh, dv = call(
        functools.partial(local_kernel, heads, blocks),
        [square] * 2,
        (x, t, w, cols, u, y, state_loc, back_loc),
        8 * units,
        "local_rows",
    )

    shards = lax.axis_size("ctx")
    turns = min(shards - 1, (shards + 1) // 2)
    if turns == 0:
        even, odd = jnp.zeros_like(even), jnp.zeros_like(odd)
    for step in range(turns):
        if step:
            even, odd = call(
                functools.partial(turn_kernel, heads),
                [edge] * 2,
                (total, end, begin, even, odd),
                6 * heads,
                "turn",
            )
        even, odd = over_edges(even, odd)

    shapes = [jax.ShapeDtypeStruct((peers, (heads + (0 if wide else 2)) * TOK + ROWS, DV), BF16)]
    if wide:
        shapes.append(jax.ShapeDtypeStruct((peers, 2 * TOK, DK), F32))
    grads = call(
        functools.partial(gradients_kernel, heads, blocks),
        shapes,
        (
            *(x, decay, kk, qk, rk, rq, rows, fresh, dv, state_loc, back_loc),
            *(pre, post, fmap, rmap, front, last, even, odd),
        ),
        50 * units,
        "gradients",
    )
    grads = [exchange(array) for array in grads]
    *wide_grads, grad_decay, grad_beta = call(
        functools.partial(unpack_kernel, peers, heads, wide),
        [
            jax.ShapeDtypeStruct((TOK, HK * DK), BF16),
            jax.ShapeDtypeStruct((TOK, HK * DK), BF16),
            jax.ShapeDtypeStruct((TOK, VALUE_HEADS * DV), BF16),
            jax.ShapeDtypeStruct((VALUE_HEADS, TOK), F32),
            jax.ShapeDtypeStruct((VALUE_HEADS, TOK), F32),
        ],
        grads,
        1,
        "unpack",
    )
    return (*wide_grads, grad_decay.T, grad_beta.T)


def solution(mesh):
    spec = P(("groups", "ctx", "head", "rep"), None)
    return jax.shard_map(
        body,
        mesh=mesh,
        in_specs=(spec,) * 6 + (P("groups"),),
        out_specs=(spec,) * 5,
        check_vma=False,
    )
```

```python
import functools

import jax
import jax.numpy as jnp
from jax import lax
from jax.experimental import pallas as pl
from jax.experimental.pallas import tpu as pltpu
from jax.sharding import PartitionSpec as P

VALUE_HEADS = 16
HK = 8
DK = 128
DV = 128
GROUP = VALUE_HEADS // HK
L = 128
ROWS = 16
TOK = 64
PER = L // TOK
EPS = 1e-06
F32 = jnp.float32
BF16 = jnp.bfloat16

NN = ((1,), (0,))
NT = ((1,), (1,))
TN = ((0,), (0,))


def split(x):
    if isinstance(x, tuple):
        return x
    if x.dtype == BF16:
        return (x,)
    high = x.astype(BF16)
    return (high, (x - high.astype(F32)).astype(BF16))


def mm(a, b, dims=NN):
    a, b = split(a), split(b)
    left_along, right_along = dims[0][0], dims[1][0]
    across = 1 - right_along
    size = b[0].shape[across]
    left = jnp.concatenate(a, axis=left_along) if len(a) > 1 else a[0]
    right = jnp.concatenate(b, axis=across) if len(b) > 1 else b[0]
    if len(a) > 1:
        below = [b[0], jnp.zeros_like(b[0])] if len(b) > 1 else [b[0]]
        below = jnp.concatenate(below, axis=across) if len(below) > 1 else below[0]
        right = jnp.concatenate([right, below], axis=right_along)
    out = lax.dot_general(left, right, (dims, ((), ())), preferred_element_type=F32)
    return out[:, :size] + out[:, size:] if len(b) > 1 else out


def side_by_side(parts):
    parts = list(parts)
    while parts:
        parts = [part for part in parts if next(part, parts) is not parts]


def iotas():
    rows = lax.broadcasted_iota(jnp.int32, (L, L), 0)
    columns = lax.broadcasted_iota(jnp.int32, (L, L), 1)
    return rows, columns


def unit_lower_inverse(lowers):
    rows, columns = iotas()
    eye = (rows == columns).astype(F32)
    near = rows // 16 == columns // 16
    firsts = [jnp.where(near, -a, 0.0) for a in lowers]
    sums = [eye + x for x in firsts]
    powers = [mm(x, x) for x in firsts]
    for _ in range(2):
        both = [mm(jnp.concatenate([x, s], axis=0), x) for x, s in zip(powers, sums)]
        powers = [x[:L] for x in both]
        sums = [s + x[L:] for s, x in zip(sums, both)]
    sums = [s + mm(s, x) for s, x in zip(sums, powers)]
    firsts = [mm(s, jnp.where(near, 0.0, -a)) for s, a in zip(sums, lowers)]
    powers = [mm(x, x) for x in firsts]
    both = [mm(jnp.concatenate([x, y], axis=0), x) for x, y in zip(powers, firsts)]
    fourths = [x[:L] for x in both]
    leads = [eye + y + x + b[L:] for y, x, b in zip(firsts, powers, both)]
    sums = [s + mm(x, s) for s, x in zip(sums, fourths)]
    return [mm(x, s) for x, s in zip(leads, sums)]


def doc_offsets(doc_ref):
    lengths = doc_ref[...]
    count = lengths.shape[1]
    rows = lax.broadcasted_iota(jnp.int32, (count, count), 0)
    columns = lax.broadcasted_iota(jnp.int32, (count, count), 1)
    return jnp.sum(jnp.where(columns < rows, lengths.astype(F32), 0.0), axis=1, keepdims=True)


def taken(ref, n, piece):
    here = slice(piece * TOK, (piece + 1) * TOK)
    return jnp.concatenate([ref[n * PER + i, here, :] for i in range(PER)], axis=0)


def column(cols, spot):
    return cols[:, spot : spot + 1]


def wide_column(cols, spot):
    return jnp.broadcast_to(column(cols, spot), (L, L))


def times_ones(rows_in, ones):
    parts, rest = [], rows_in
    for _ in range(3):
        part = rest.astype(BF16)
        parts.append(part.astype(F32))
        rest = rest - part.astype(F32)
    count = rows_in.shape[0]
    out = lax.dot_general(
        jnp.concatenate(parts, axis=0).astype(BF16),
        ones,
        (NN, ((), ())),
        preferred_element_type=F32,
    )
    return out[:count] + out[count : 2 * count] + out[2 * count :]


def pack_kernel(peers, heads, *refs):
    count = 7
    sources, out_ref = refs[:count], refs[count]
    buffers, done = refs[count + 1 : 2 * count + 1], refs[2 * count + 1]
    copies = [
        pltpu.make_async_copy(source, buffer, done.at[i])
        for i, (source, buffer) in enumerate(zip(sources, buffers))
    ]
    for copy in copies:
        copy.start()
    decay_ref, beta_ref, doc_ref, q_ref, k_ref, v_ref, g_ref = buffers
    for copy in copies[:3]:
        copy.wait()
    logits = jnp.concatenate(
        [decay_ref[...].astype(F32), beta_ref[...].astype(F32)], axis=1
    )
    off_col = doc_offsets(doc_ref)
    place = lax.axis_index("ctx") * lax.axis_size("head") + lax.axis_index("head")
    first = (place * lax.axis_size("rep") + lax.axis_index("rep")) * TOK
    lane = lax.broadcasted_iota(jnp.int32, (1, L), 1)
    position = jnp.where(lane < TOK, first + lane, first - 1).astype(F32)
    docs = jnp.sum((off_col <= position).astype(F32), axis=0, keepdims=True)
    spot = lax.broadcasted_iota(jnp.int32, (ROWS, L), 0)
    for j in range(peers):
        tile = jnp.where(spot == heads, docs, 0.0)
        for h in range(heads):
            tile = jnp.where(spot == h, logits[j * heads + h : j * heads + h + 1], tile)
        out_ref[j, (2 + 2 * heads) * TOK :, :] = tile.astype(BF16)
    for i, (ref, piece) in enumerate(((q_ref, 0), (k_ref, 1))):
        copies[3 + i].wait()
        for j in range(peers):
            key_head = j * heads // GROUP
            out_ref[j, piece * TOK : (piece + 1) * TOK, :] = ref[
                :, key_head * DK : (key_head + 1) * DK
            ]
    for i, (ref, piece) in enumerate(((v_ref, 2), (g_ref, 2 + heads))):
        copies[5 + i].wait()
        for j in range(peers):
            for h in range(heads):
                here = slice((piece + h) * TOK, (piece + h + 1) * TOK)
                lanes = slice((j * heads + h) * DV, (j * heads + h + 1) * DV)
                out_ref[j, here, :] = ref[:, lanes]


def to_neighbours(parity, even_ref, odd_ref, h, state, back):
    even = parity == 0
    even_ref[h] = jnp.where(even, state, back)
    odd_ref[h] = jnp.where(even, back, state)


def from_neighbours(parity, even_ref, odd_ref, h):
    even = parity == 0
    return jnp.where(even, odd_ref[h], even_ref[h]), jnp.where(even, even_ref[h], odd_ref[h])


def blocks_kernel(
    heads,
    blocks,
    x_ref,
    t_ref,
    w_ref,
    u_ref,
    y_ref,
    m_ref,
    decay_ref,
    kk_ref,
    qk_ref,
    rk_ref,
    rq_ref,
    state_ref,
    back_ref,
    end_ref,
    begin_ref,
    even_ref,
    odd_ref,
    cols_ref,
    rows_ref,
):
    rows, columns = iotas()
    eye = (rows == columns).astype(F32)
    shard = lax.axis_index("ctx")
    lane = lax.broadcasted_iota(jnp.int32, (1, L), 1)
    units = [(n, h) for n in range(blocks) for h in range(heads)]
    half = ROWS // 2
    unit_row = lax.broadcasted_iota(jnp.int32, (half, L), 0)

    def by_unit(row_of_block):
        out = jnp.zeros((half, L), F32)
        for n in range(blocks):
            out = jnp.where(unit_row // heads == n, row_of_block[n], out)
        return out

    keys, queries, grams, crosses, rk_rows, rq_rows = [], [], [], [], [], []
    for n in range(blocks):
        q, k = taken(x_ref, n, 0), taken(x_ref, n, 1)
        grams.append(mm(k, k, NT))
        crosses.append(mm(q, k, NT))
        for gram, out in ((grams[n], rk_rows), (mm(q, q, NT), rq_rows)):
            square = jnp.sum(jnp.where(rows == columns, gram, 0.0), axis=0, keepdims=True)
            out.append(lax.rsqrt(square + EPS))
        rq_rows[n] = rq_rows[n] * DK**-0.5
        keys.append(k)
        queries.append(q)
    decay_logits = jnp.zeros((half, L), F32)
    beta_logits = jnp.zeros((half, L), F32)
    doc_rows, befores = [], []
    for n in range(blocks):
        first, second = (
            x_ref[n * PER + i, (2 + 2 * heads) * TOK :, :].astype(F32) for i in range(PER)
        )
        left = jnp.where(lane < TOK, first, pltpu.roll(second, TOK, 1))
        right = jnp.where(lane < TOK, pltpu.roll(first, TOK, 1), second)
        for h in range(heads):
            here = unit_row == n * heads + h
            decay_logits = jnp.where(here, left[h : h + 1], decay_logits)
            beta_logits = jnp.where(here, right[h : h + 1], beta_logits)
        doc_rows.append(left[heads : heads + 1])
        befores.append(first[heads : heads + 1, TOK : TOK + 1])
    soft = jnp.maximum(decay_logits, 0.0) + jnp.log1p(jnp.exp(-jnp.abs(decay_logits)))
    beta_rows = 1.0 / (1.0 + jnp.exp(-beta_logits))
    sum_rows = times_ones(-soft, (rows <= columns).astype(BF16))
    rows_ref[...] = jnp.concatenate([1.0 / (1.0 + jnp.exp(-decay_logits)), beta_rows], axis=0)
    unit_docs = by_unit(doc_rows)
    front_rows = jnp.where(unit_docs == by_unit(befores), jnp.exp(sum_rows), 0.0)
    final = slice(L - 1, L)
    last_rows = jnp.where(
        unit_docs == unit_docs[:, final], jnp.exp(sum_rows[:, final] - sum_rows), 0.0
    )
    rk_units, rq_units = by_unit(rk_rows), by_unit(rq_rows)
    kinds = [
        sum_rows,
        beta_rows,
        front_rows,
        last_rows,
        last_rows * rk_units,
        rk_units,
        rq_units,
        unit_docs,
    ]
    cols = jnp.concatenate(kinds + [jnp.zeros((L - half * len(kinds), L), F32)], axis=0).T
    cols_ref[...] = cols
    write_rows = beta_rows * front_rows * rk_units
    read_rows = front_rows * rq_units
    lowers, decays = [], []
    for n in range(blocks):
        keep = (columns <= rows) & (column(cols, 7 * half + n * heads) == doc_rows[n])
        rk, rq = wide_column(cols, 5 * half + n * heads), wide_column(cols, 6 * half + n * heads)
        kk = jnp.where(columns < rows, grams[n] * rk * rk_rows[n], 0.0)
        rk_ref[n], rq_ref[n] = rk, rq
        kk_ref[n] = kk
        qk_ref[n] = crosses[n] * rq * rk_rows[n]
        for h in range(heads):
            u = n * heads + h
            spread = column(cols, u) - sum_rows[u : u + 1]
            decay = jnp.where(keep, jnp.exp(jnp.where(keep, spread, 0.0)), 0.0)
            decay_ref[u] = decay
            decays.append(decay)
            lowers.append(column(cols, half + u) * (decay * kk))
    inverses = unit_lower_inverse(lowers)
    moves, adds, backs = {}, {}, {}
    turned = [q.astype(F32).T for q in queries]

    def unit(n, h):
        k = keys[n]
        u = n * heads + h
        here = slice(u, u + 1)
        v, g = taken(x_ref, n, 2 + h), taken(x_ref, n, 2 + heads + h)
        t = inverses[u] * beta_rows[here]
        w = mm(inverses[u] * write_rows[here], k)
        value = mm(t, v)
        yield
        spread = mm(k, column(cols, 4 * half + u) * jnp.concatenate([w, value], axis=1), TN)
        yield
        move = front_rows[here, final] * eye - spread[:, :DK]
        y = mm(decays[u] * qk_ref[n], g, TN)
        back = mm(turned[n] * read_rows[here], g) - mm(w, y, TN)
        yield
        t_ref[u] = t
        w_ref[u] = w
        u_ref[u] = value
        y_ref[u] = y
        m_ref[u] = move
        moves[n, h], adds[n, h], backs[n, h] = split(move), spread[:, DK:], back

    side_by_side(unit(n, h) for n, h in units)
    ends, begins = [], []
    zero = jnp.zeros((DK, DV), F32)
    for h in range(heads):
        state_ref[h] = zero
        back_ref[(blocks - 1) * heads + h] = zero
        ends.append(adds[0, h])
        begins.append(backs[blocks - 1, h])
    for step in range(1, blocks):
        ahead, behind = step, blocks - 1 - step
        for h in range(heads):
            state_ref[ahead * heads + h] = ends[h]
            ends[h] = mm(moves[ahead, h], ends[h]) + adds[ahead, h]
            back_ref[behind * heads + h] = begins[h]
            begins[h] = mm(moves[behind, h], begins[h], TN) + backs[behind, h]
    for h in range(heads):
        end_ref[h] = ends[h]
        begin_ref[h] = begins[h]
        to_neighbours(shard % 2, even_ref, odd_ref, h, ends[h], begins[h])


def maps_kernel(
    heads,
    blocks,
    x_ref,
    t_ref,
    w_ref,
    m_ref,
    cols_ref,
    pre_ref,
    post_ref,
    fmap_ref,
    rmap_ref,
    front_ref,
    last_ref,
    total_ref,
):
    rows, columns = iotas()
    eye = (rows == columns).astype(F32)
    half = ROWS // 2
    cols = cols_ref[...]
    pres, posts = [eye] * heads, [eye] * heads
    for step in range(blocks):
        ahead, behind = step, blocks - 1 - step
        k = taken(x_ref, behind, 1)
        for h in range(heads):
            u = ahead * heads + h
            front_ref[u] = wide_column(cols, 2 * half + u)
            last_ref[u] = wide_column(cols, 3 * half + u)
            pre_ref[u] = pres[h]
            if step == 0:
                fmap_ref[u] = w_ref[u]
                pres[h] = m_ref[u]
            else:
                halves = split(pres[h])
                both = mm(jnp.concatenate([w_ref[u], m_ref[u]], axis=0), halves)
                fmap_ref[u] = both[:L]
                pres[h] = both[L:]
            u = behind * heads + h
            post_ref[u] = posts[h]
            if step == 0:
                spread = k.astype(F32)
                posts[h] = m_ref[u].T
            else:
                halves = split(posts[h])
                spread = mm(k, halves)
                if step < blocks - 1:
                    posts[h] = mm(m_ref[u], halves, TN)
            rmap_ref[u] = mm(t_ref[u], column(cols, 4 * half + u) * spread, TN)
    for h in range(heads):
        total_ref[h] = pres[h]


def local_kernel(
    heads,
    blocks,
    x_ref,
    t_ref,
    w_ref,
    cols_ref,
    u_ref,
    y_ref,
    state_ref,
    back_ref,
    fresh_ref,
    dv_ref,
):
    half = ROWS // 2
    cols = cols_ref[...]
    for n in range(blocks):
        k = taken(x_ref, n, 1)
        for h in range(heads):
            u = n * heads + h
            fresh_ref[u] = u_ref[u] - mm(w_ref[u], state_ref[u]) if n else u_ref[u]
            dfresh = y_ref[u]
            if n < blocks - 1:
                dfresh = dfresh + column(cols, 4 * half + u) * mm(k, back_ref[u])
            dv_ref[u] = mm(t_ref[u], dfresh, TN)


def turn_kernel(heads, total_ref, end_ref, begin_ref, even_in, odd_in, even_out, odd_out):
    parity = lax.axis_index("ctx") % 2
    for h in range(heads):
        total = split(total_ref[h])
        state, back = from_neighbours(parity, even_in, odd_in, h)
        state = mm(total, state) + end_ref[h]
        back = mm(total, back, TN) + begin_ref[h]
        to_neighbours(parity, even_out, odd_out, h, state, back)


def against(left, exact, right):
    left = split(left)
    exact = (exact, jnp.zeros_like(exact))
    both = tuple(jnp.concatenate(parts, axis=0) for parts in zip(left, exact))
    out = mm(both, right, NT)
    return out[:L], out[L:]


def gradients_kernel(
    heads,
    blocks,
    x_ref,
    decay_ref,
    kk_ref,
    qk_ref,
    rk_ref,
    rq_ref,
    rows_ref,
    fresh_ref,
    dv_ref,
    state_ref,
    back_ref,
    pre_ref,
    post_ref,
    fmap_ref,
    rmap_ref,
    front_ref,
    last_ref,
    even_ref,
    odd_ref,
    out_ref,
    *wide_refs,
):
    rows, columns = iotas()
    half = ROWS // 2
    small_row = lax.broadcasted_iota(jnp.int32, (half, L), 0)
    parity = lax.axis_index("ctx") % 2
    from_here = (rows >= columns).astype(BF16)
    wide = len(wide_refs) > 0
    at = 0 if wide else 2
    outside = [from_neighbours(parity, even_ref, odd_ref, h) for h in range(heads)]
    outside2 = [(split(enter), split(leave)) for enter, leave in outside]

    def block(n):
        kk, qk, rk, rq = kk_ref[n], qk_ref[n], rk_ref[n], rq_ref[n]
        q, k = taken(x_ref, n, 0), taken(x_ref, n, 1)
        kn, qn = rk * k.astype(F32), rq * q.astype(F32)
        dq = dk = bq_sum = b_sum = 0.0
        sums = jnp.zeros((L, L), F32)
        crossed = jnp.zeros((half, L), F32)
        tails = jnp.zeros((half, 1), F32)
        for h in range(heads):
            u = n * heads + h
            decay, front = decay_ref[u], front_ref[u]
            v = taken(x_ref, n, 2 + h).astype(F32)
            g = taken(x_ref, n, 2 + heads + h)
            enter2, leave2 = outside2[h]
            if n == 0:
                state, seen = outside[h][0], mm(fmap_ref[u], enter2)
            else:
                both = mm(jnp.concatenate([pre_ref[u], fmap_ref[u]], axis=0), enter2)
                state, seen = state_ref[u] + both[:L], both[L:]
            if n == blocks - 1:
                back, dv = outside[h][1], mm(rmap_ref[u], leave2)
            else:
                both = mm(jnp.concatenate([post_ref[u], rmap_ref[u]], axis=0), leave2)
                back, dv = back_ref[u] + both[:L], both[L:]
            yield
            fresh2 = split(fresh_ref[u] - seen)
            dv = dv_ref[u] + dv
            dv2, state2 = split(dv), split(state)
            for i in range(PER):
                out_ref[n * PER + i, (at + h) * TOK : (at + h + 1) * TOK, :] = dv2[0][
                    i * TOK : (i + 1) * TOK
                ]
            yield
            read = front * (rk * mm(k, state2))
            da, dp = against(dv2, g, fresh2)
            ds, gs = against(dv2, g, state2)
            yield
            b = jnp.where(columns < rows, da * decay, 0.0)
            bq = dp * decay
            scaled = b * kk
            z = bq * qk - scaled
            gs = front * gs
            outer = last_ref[u] * mm(fresh2, back, NT)
            kept = kn * outer
            yield
            by_sum = jnp.sum(qn * gs - dv * read - kept + z, axis=1, keepdims=True)
            by_beta = jnp.sum(dv * (v - read) - scaled, axis=1, keepdims=True)
            sums = jnp.where(columns == h, by_sum, sums)
            sums = jnp.where(columns == heads + h, by_beta, sums)
            crossed = jnp.where(small_row == h, jnp.sum(z, axis=0, keepdims=True), crossed)
            tail = jnp.sum(kept + front[L - 1 : L] * (state * back), axis=0, keepdims=True)
            tail = jnp.sum(tail, axis=1, keepdims=True)
            tails = jnp.where(small_row[:, :1] == h, tail, tails)
            yield
            b_sum = b_sum - b
            bq_sum = bq_sum + bq
            dq = dq + gs
            dk = dk + outer - front * ds
        yield
        turned = sums.T[:half]
        dsum = times_ones(turned - crossed, from_here) + tails
        small = turned
        for h in range(heads):
            u = n * heads + h
            sig, beta = rows_ref[u : u + 1], rows_ref[half + u : half + u + 1]
            small = jnp.where(small_row == h, -dsum * sig, small)
            small = jnp.where(small_row == heads + h, turned * (1.0 - beta), small)
        both = mm(jnp.concatenate([bq_sum, b_sum + b_sum.T], axis=0), kn)
        yield
        dq = dq + both[:L]
        dk = dk + both[L:] + mm(bq_sum, qn, TN)
        dq = rq * (dq - qn * (DK * jnp.sum(qn * dq, axis=1, keepdims=True)))
        dk = rk * (dk - kn * jnp.sum(kn * dk, axis=1, keepdims=True))
        yield
        high = small.astype(BF16).astype(F32)
        pair = jnp.concatenate([high, small - high], axis=0)
        for i in range(PER):
            here = slice(i * TOK, (i + 1) * TOK)
            if wide:
                wide_refs[0][n * PER + i, 0:TOK, :] = dq[here]
                wide_refs[0][n * PER + i, TOK : 2 * TOK, :] = dk[here]
            else:
                out_ref[n * PER + i, 0:TOK, :] = dq[here].astype(BF16)
                out_ref[n * PER + i, TOK : 2 * TOK, :] = dk[here].astype(BF16)
            moved = pair if i == 0 else pltpu.roll(pair, L - i * TOK, 1)
            out_ref[n * PER + i, (at + heads) * TOK :, :] = moved.astype(BF16)

    side_by_side(block(n) for n in range(blocks))


def unpack_kernel(peers, heads, wide, *refs):
    if wide:
        x_ref, wide_ref, *outs = refs
    else:
        x_ref, *outs = refs
        wide_ref = None
    targets, (dq_ref, dk_ref, dv_ref, decay_ref, beta_ref), done = outs[:5], outs[5:10], outs[10]
    copies = [
        pltpu.make_async_copy(buffer, target, done.at[i])
        for i, (buffer, target) in enumerate(zip(outs[5:10], targets))
    ]
    at = 0 if wide else 2
    spots = lax.broadcasted_iota(jnp.int32, (ROWS, L), 0)
    decays, betas = jnp.zeros((ROWS, L), F32), jnp.zeros((ROWS, L), F32)
    for j in range(peers):
        for h in range(heads):
            lanes = slice((j * heads + h) * DV, (j * heads + h + 1) * DV)
            dv_ref[:, lanes] = x_ref[j, (at + h) * TOK : (at + h + 1) * TOK, :]
    copies[2].start()
    for j in range(peers):
        pair = x_ref[j, (at + heads) * TOK :, :].astype(F32)
        small = pair[: ROWS // 2] + pair[ROWS // 2 :]
        for h in range(heads):
            decays = jnp.where(spots == j * heads + h, small[h : h + 1], decays)
            betas = jnp.where(spots == j * heads + h, small[heads + h : heads + h + 1], betas)
    for i in range(HK):
        lanes = slice(i * DK, (i + 1) * DK)
        if wide:
            some = [wide_ref[i * GROUP + m] for m in range(GROUP)]
            total = some[0]
            for other in some[1:]:
                total = total + other
            total = total.astype(BF16)
            dq_ref[:, lanes] = total[:TOK]
            dk_ref[:, lanes] = total[TOK:]
        else:
            dq_ref[:, lanes] = x_ref[i, 0:TOK, :]
            dk_ref[:, lanes] = x_ref[i, TOK : 2 * TOK, :]
    copies[0].start()
    copies[1].start()
    decay_ref[...] = decays[:, :TOK]
    beta_ref[...] = betas[:, :TOK]
    copies[3].start()
    copies[4].start()
    for copy in copies:
        copy.wait()


def over_edges(even, odd):
    size = lax.axis_size("ctx")
    results = []
    for first, value in ((0, even), (1, odd)):
        pairs = []
        for i in range(first, size - 1, 2):
            pairs += [(i, i + 1), (i + 1, i)]
        results.append(lax.ppermute(value, "ctx", pairs) if pairs else jnp.zeros_like(value))
    return results


def work(passes):
    return pl.CostEstimate(
        flops=2 * L * DK * DV * passes, bytes_accessed=1 << 20, transcendentals=0
    )


PARAMS = pltpu.CompilerParams(vmem_limit_bytes=16 << 20)


def body(queries, key_vectors, values, out_grad, decay_logit, beta_logit, doc_lengths):
    assert queries.shape[0] == TOK
    peers = lax.axis_size("head") * lax.axis_size("rep")
    heads = VALUE_HEADS // peers
    wide = heads % GROUP != 0
    blocks = TOK * peers // L
    units = blocks * heads
    assert heads == (1 if wide else GROUP) and units <= ROWS // 2

    def exchange(array):
        return lax.all_to_all(array, ("head", "rep"), split_axis=0, concat_axis=0, tiled=True)

    def call(kernel, shapes, inputs, passes, name, params=PARAMS, **rest):
        return pl.pallas_call(
            kernel,
            out_shape=shapes,
            compiler_params=params,
            cost_estimate=work(passes),
            name=name,
            **rest,
        )(*inputs)

    square = jax.ShapeDtypeStruct((units, DK, DV), F32)
    single = jax.ShapeDtypeStruct((blocks, DK, DV), F32)
    edge = jax.ShapeDtypeStruct((heads, DK, DV), F32)

    depth = (2 + 2 * heads) * TOK + ROWS
    assert doc_lengths.shape[0] <= 256
    docs = doc_lengths.reshape(1, -1)
    sources = (decay_logit.T, beta_logit.T, docs, queries, key_vectors, values, out_grad)
    sources = tuple(pltpu.with_memory_space_constraint(array, pltpu.HBM) for array in sources)
    packed = call(
        functools.partial(pack_kernel, peers, heads),
        jax.ShapeDtypeStruct((peers, depth, DK), BF16),
        sources,
        1,
        "pack",
        in_specs=[pl.BlockSpec(memory_space=pltpu.HBM)] * len(sources),
        scratch_shapes=[pltpu.VMEM(array.shape, array.dtype) for array in sources]
        + [pltpu.SemaphoreType.DMA((len(sources),))],
    )
    x = exchange(packed)
    local = call(
        functools.partial(blocks_kernel, heads, blocks),
        [square] * 6
        + [single] * 4
        + [square] * 2
        + [edge] * 4
        + [jax.ShapeDtypeStruct((L, L), F32), jax.ShapeDtypeStruct((ROWS, L), F32)],
        (x,),
        60 * units,
        "blocks",
    )
    t, w, u, y, m, decay, kk, qk, rk, rq, state_loc, back_loc = local[:12]
    end, begin, even, odd, cols, rows = local[12:]
    pre, post, fmap, rmap, front, last, total = call(
        functools.partial(maps_kernel, heads, blocks),
        [square] * 6 + [edge],
        (x, t, w, m, cols),
        12 * units,
        "maps",
    )
    fresh, dv = call(
        functools.partial(local_kernel, heads, blocks),
        [square] * 2,
        (x, t, w, cols, u, y, state_loc, back_loc),
        8 * units,
        "local_rows",
    )

    shards = lax.axis_size("ctx")
    turns = min(shards - 1, (shards + 1) // 2)
    if turns == 0:
        even, odd = jnp.zeros_like(even), jnp.zeros_like(odd)
    for step in range(turns):
        if step:
            even, odd = call(
                functools.partial(turn_kernel, heads),
                [edge] * 2,
                (total, end, begin, even, odd),
                6 * heads,
                "turn",
            )
        even, odd = over_edges(even, odd)

    shapes = [jax.ShapeDtypeStruct((peers, (heads + (0 if wide else 2)) * TOK + ROWS, DV), BF16)]
    if wide:
        shapes.append(jax.ShapeDtypeStruct((peers, 2 * TOK, DK), F32))
    grads = call(
        functools.partial(gradients_kernel, heads, blocks),
        shapes,
        (
            *(x, decay, kk, qk, rk, rq, rows, fresh, dv, state_loc, back_loc),
            *(pre, post, fmap, rmap, front, last, even, odd),
        ),
        50 * units,
        "gradients",
    )
    grads = [exchange(array) for array in grads]
    shapes = [
            jax.ShapeDtypeStruct((TOK, HK * DK), BF16),
            jax.ShapeDtypeStruct((TOK, HK * DK), BF16),
            jax.ShapeDtypeStruct((TOK, VALUE_HEADS * DV), BF16),
            jax.ShapeDtypeStruct((VALUE_HEADS, TOK), F32),
            jax.ShapeDtypeStruct((VALUE_HEADS, TOK), F32),
        ]
    *wide_grads, grad_decay, grad_beta = call(
        functools.partial(unpack_kernel, peers, heads, wide),
        shapes,
        grads,
        1,
        "unpack",
        out_specs=[pl.BlockSpec(memory_space=pltpu.HBM)] * len(shapes),
        scratch_shapes=[pltpu.VMEM(shape.shape, shape.dtype) for shape in shapes]
        + [pltpu.SemaphoreType.DMA((len(shapes),))],
    )
    return (*wide_grads, grad_decay.T, grad_beta.T)


def solution(mesh):
    spec = P(("groups", "ctx", "head", "rep"), None)
    return jax.shard_map(
        body,
        mesh=mesh,
        in_specs=(spec,) * 6 + (P("groups"),),
        out_specs=(spec,) * 5,
        check_vma=False,
    )
```
